32 devices in a mesh: expert: 2 (over x), shard: 16 (over z, y, core).
Axes of the slice: x: 2, y: 2, z: 4, core: 2. Of those that a mesh axis runs over, the one named last changes fastest.
Arguments:
- tokens: bfloat16 [16, 512, 768], P('shard', 'expert'), may hold values from -32 to 32
- segment_ids: int32 [16, 512], P('shard'), may hold values from 0 to 3, never falling along the last dimension, each value on 1 to 256 neighbouring positions
- routes: int32 [16, 512, 2], P('shard', 'expert'), may hold values from 0 to 11, as said below
- earlier_logits: float32 [16, 512, 12], P('shard', 'expert'), may hold values from -3 to 3
- out_cotangent: bfloat16 [16, 512, 768], P('shard', 'expert'), may hold values from -6 to 6
- query_weight: bfloat16 [768, 768], P('shard'), may hold values from -0.3125 to 0.3125
- key_weight: bfloat16 [768, 768], P('shard'), may hold values from -0.3125 to 0.3125
- value_weight: bfloat16 [768, 768], P('shard'), may hold values from -0.21875 to 0.21875
- output_weight: bfloat16 [768, 768], P('shard'), may hold values from -0.875 to 0.875
- router_weight: bfloat16 [768, 12], P('shard'), may hold values from -0.109375 to 0.109375
- const_vectors: bfloat16 [768, 2], P('shard'), may hold values from -4 to 4
- attn_gain: bfloat16 [768], P('shard'), may hold values from 0.5 to 1.5
- moe_gain: bfloat16 [768], P('shard'), may hold values from 0.5 to 1.5
- gate_weight: bfloat16 [8, 768, 2048], P('expert', 'shard'), may hold values from -0.21875 to 0.21875
- up_weight: bfloat16 [8, 768, 2048], P('expert', 'shard'), may hold values from -0.21875 to 0.21875
- down_weight: bfloat16 [8, 2048, 768], P('expert', 'shard'), may hold values from -0.125 to 0.125
Outputs:
- layer_out: bfloat16 [16, 512, 768], P('shard', 'expert')
- tokens_grad: float32 [16, 512, 768], P('shard', 'expert')
- prior_logits_gradient: float32 [16, 512, 12], P('shard', 'expert')
- query_grad: float32 [768, 768], P('shard')
- key_grad: float32 [768, 768], P('shard')
- value_grad: float32 [768, 768], P('shard')
- output_grad: float32 [768, 768], P('shard')
- router_grad: float32 [768, 12], P('shard')
- const_grad: float32 [768, 2], P('shard')
- attn_gain_grad: float32 [768], P('shard')
- moe_gain_grad: float32 [768], P('shard')
- gate_grad: float32 [8, 768, 2048], P('expert', 'shard')
- up_grad: float32 [8, 768, 2048], P('expert', 'shard')
- down_grad: float32 [8, 2048, 768], P('expert', 'shard')
The draws below stay inside these ranges and needn't reach their ends.
Inputs may be any that keep to these rules, and one draw needn't show every extreme that they name: `routes`: each token names two different experts. In each aligned block of 256 positions of a sequence no expert is named more than 64 times, and some expert below 8 exactly 64 times. `segment_ids`: ids never fall along a sequence; each document has at most 256 positions, and one has exactly 256.
All inputs are finite; a program needn't handle non-finite values.
Results may differ from the reference program's by a relative error of at most 0.035.
Values may be sent and summed in bfloat16 or wider, within the bound.
No kernel may reach another device: no remote copies, remote signals or barrier semaphores. Data moves between devices by JAX's collectives and lax.ppermute only.
A program may use at most 128 MiB of HBM per device.

```python
import math
import jax
import jax.numpy as jnp
import numpy as np
from jax import lax

D = 768
HEADS = 12
HD = 64
FF = 2048
EXPERTS = 8
CHOICES = 12
POS_DEV = 256
CAP = 64
LEN = 512
SEQS = 16
DOCS = 4
DOC = 256


def draw_tokens(key, part):
    subkeys = jax.random.split(key, 3)
    noise_part = jnp.clip(jax.random.normal(subkeys[0], (SEQS, LEN, D), jnp.float32), -4.0, 4.0)
    row_scale = jnp.exp(jax.random.uniform(subkeys[1], (SEQS, LEN, 1), jnp.float32, math.log(0.3), math.log(3.0)))
    column_scale = jnp.exp(jax.random.uniform(subkeys[2], (D,), jnp.float32, math.log(0.5), math.log(2.0)))
    return (noise_part * row_scale * column_scale).astype(jnp.bfloat16)


def route_block(key):
    subkeys = jax.random.split(key, 4)
    choice_total = EXPERTS + 4
    hot_expert = jax.random.randint(subkeys[0], (), 0, EXPERTS)
    stride = jax.random.randint(subkeys[1], (), 1, choice_total)
    partner = (hot_expert - stride) % choice_total
    shuffle = jax.random.permutation(subkeys[2], choice_total)
    excluded = (shuffle == hot_expert) | (shuffle == partner)
    order_key = excluded.astype(jnp.int32) * choice_total + jnp.arange(choice_total, dtype=jnp.int32)
    others = shuffle[jnp.argsort(order_key, stable=True)]
    half_cap = CAP // 2
    places = jnp.arange(POS_DEV, dtype=jnp.int32)
    rest_index = jnp.clip((places - CAP) // half_cap, 0, choice_total - 3)
    first_route = jnp.where(places < half_cap, hot_expert, jnp.where(places < CAP, partner, others[rest_index]))
    first_route = first_route[jax.random.permutation(subkeys[3], POS_DEV)]
    second_route = (first_route + stride) % choice_total
    return jnp.stack([first_route, second_route], axis=-1).astype(jnp.int32)


def draw_routes(key, part):
    block_total = SEQS * (LEN // POS_DEV)
    block_keys = jax.random.split(jax.random.fold_in(key, 17), block_total)
    blocks = jax.vmap(route_block)(block_keys)
    return blocks.reshape(SEQS, LEN, 2)


def block_levels(key, extent, pieces, smallest, high):
    factor_of = 1.0
    for position, shards_of in pieces:
        draws = jax.random.uniform(jax.random.fold_in(jax.random.fold_in(key, 6), position), (shards_of,), jnp.float32, smallest / len(pieces), high / len(pieces))
        factor_of = factor_of * jnp.repeat(jnp.exp(draws), extent[position] // shards_of).reshape((-1,) + (1,) * (len(extent) - 1 - position))
    return factor_of


def profile(number_of, total, bound, lean):
    weights = [(1 << 20) // math.isqrt(rank ** lean) + 1 for rank in range(2, number_of + 1)]
    surplus, counts = total - bound - (number_of - 1), [1] * (number_of - 1)
    while surplus > 0:
        free = [i for i in range(number_of - 1) if counts[i] < bound]
        whole, left = sum([weights[i] for i in free]), surplus
        for i in free:
            more = min(bound - counts[i], max(1, left * weights[i] // whole), surplus)
            counts[i] = counts[i] + more
            surplus = surplus - more
    return np.array([bound] + counts)


def ragged(stream_key, amount, total, reach, lean):
    if amount == 2:
        one = jax.random.randint(stream_key, (), max(1, total - reach), min(reach, total - 1) + 1)
        return jnp.stack([one, total - one])
    lengths = jnp.asarray(profile(amount, total, reach, lean), jnp.int32)
    couples = (amount - 1) // 2
    source_of, receiver = lengths[1:1 + 2 * couples:2], lengths[2:2 + 2 * couples:2]
    margin = jnp.minimum(source_of - 1, reach - receiver)
    shifted = jax.random.randint(jax.random.fold_in(stream_key, 1), (couples,), 0, 1 << 20) % (margin + 1)
    lengths = lengths.at[1:1 + 2 * couples:2].set(source_of - shifted).at[2:2 + 2 * couples:2].set(receiver + shifted)
    return lengths[jax.random.permutation(jax.random.fold_in(stream_key, 2), amount)]


def scatter_about(rng, extent, deviation, reach, cuts=(), kind=jnp.bfloat16):
    level = block_levels(rng, extent, cuts, -0.22, 0.18) if cuts else 1.0
    drawn = jax.random.normal(rng, extent, jnp.float32) * deviation * level
    return jnp.minimum(jnp.maximum(drawn, -reach), reach).astype(kind)


def setup_inputs(seed: int = 0) -> dict:
    keys = jax.random.split(jax.random.key(seed), 17)
    tokens = draw_tokens(jax.random.fold_in(keys[16], 71), 0)
    segment_ids = jax.vmap(lambda own: jnp.searchsorted(jnp.cumsum(ragged(own, DOCS, LEN, DOC, 2)), jnp.arange(LEN), side="right"))(jax.random.split(keys[1], SEQS)).reshape((SEQS, LEN)).astype(jnp.int32)
    routes = draw_routes(jax.random.fold_in(keys[16], 71), 0)
    earlier_logits = scatter_about(keys[3], (SEQS, LEN, CHOICES), 0.5, 3.0, ((0, 16), (1, 2)), jnp.float32)
    out_cotangent = scatter_about(keys[4], (SEQS, LEN, D), 1.0, 6.0, ((0, 16), (1, 2)))
    query_weight = scatter_about(keys[5], (D, D), (D // 2) ** -0.5, 0.3125, ((0, 16),))
    key_weight = scatter_about(keys[6], (D, D), (D // 2) ** -0.5, 0.3125, ((0, 16),))
    value_weight = scatter_about(keys[7], (D, D), D ** -0.5, 0.21875, ((0, 16),))
    output_weight = scatter_about(keys[8], (D, D), (D // 16) ** -0.5, 0.875, ((0, 16),))
    router_weight = scatter_about(keys[9], (D, CHOICES), (4 * D) ** -0.5, 0.109375, ((0, 16),))
    const_vectors = scatter_about(keys[10], (D, 2), 1.0, 4.0, ((0, 16),))
    attn_gain = jnp.clip(1.0 + 0.1 * jax.random.normal(keys[11], (D,), jnp.float32), 0.5, 1.5).astype(jnp.bfloat16)
    moe_gain = jnp.clip(1.0 + 0.1 * jax.random.normal(keys[12], (D,), jnp.float32), 0.5, 1.5).astype(jnp.bfloat16)
    gate_weight = scatter_about(keys[13], (EXPERTS, D, FF), D ** -0.5, 0.21875, ((0, 2), (1, 16)))
    up_weight = scatter_about(keys[14], (EXPERTS, D, FF), D ** -0.5, 0.21875, ((0, 2), (1, 16)))
    down_weight = scatter_about(keys[15], (EXPERTS, FF, D), FF ** -0.5, 0.125, ((0, 2), (1, 16)))
    return dict(tokens=tokens, segment_ids=segment_ids, routes=routes, earlier_logits=earlier_logits, out_cotangent=out_cotangent, query_weight=query_weight, key_weight=key_weight, value_weight=value_weight, output_weight=output_weight, router_weight=router_weight, const_vectors=const_vectors, attn_gain=attn_gain, moe_gain=moe_gain, gate_weight=gate_weight, up_weight=up_weight, down_weight=down_weight)


@jax.custom_vjp
def low(v):
    return lax.optimization_barrier(v.astype(jnp.bfloat16)).astype(jnp.float32)

@jax.custom_vjp
def narrow_backward(v):
    return v

def low_keep(v):
    return (low(v), None)

def low_pass(kept, grad):
    return (grad,)

def back_keep(v):
    return (v, None)

def back_low(kept, grad):
    return (low(grad),)
low.defvjp(low_keep, low_pass)
narrow_backward.defvjp(back_keep, back_low)
norm_eps = 1e-06
masked_fill = -1e+30
top_scores = lax.Precision.HIGHEST

def rms_scale(values):
    return values * lax.rsqrt(lax.optimization_barrier(jnp.mean(values * values, axis=-1, keepdims=True)) + norm_eps)

def rotary(values, positions, direction):
    dims_in = values.shape
    heads_view = values.reshape(dims_in[:-1] + (HEADS, dims_in[-1] // HEADS))
    half_size = heads_view.shape[-1] // 2
    frequency = jnp.exp(jnp.arange(half_size, dtype=jnp.float32) * (-2.0 * math.log(10000.0) / (2 * half_size)))
    angles = positions.astype(jnp.float32)[:, None] * frequency[None, :]
    cosine = jnp.cos(angles)[:, None, :]
    sine_part = direction * jnp.sin(angles)[:, None, :]
    first_half = heads_view[..., :half_size]
    second_half = heads_view[..., half_size:]
    turned = jnp.concatenate([first_half * cosine - second_half * sine_part, second_half * cosine + first_half * sine_part], axis=-1)
    return turned.reshape(dims_in)

def attend_rows(query_rows, row_start, keys_seq, values_seq, segment_row):
    row_count = query_rows.shape[0]
    key_count = keys_seq.shape[0]
    query_heads = query_rows.reshape(row_count, HEADS, HD)
    key_heads = keys_seq.reshape(key_count, HEADS, HD)
    value_heads = values_seq.reshape(key_count, HEADS, HD)
    raw_scores = narrow_backward(jnp.einsum('qhd,khd->hqk', query_heads, key_heads, precision=top_scores))
    scores = raw_scores * HD ** (-0.5)
    query_pos = row_start.astype(jnp.int32) + jnp.arange(row_count, dtype=jnp.int32)
    key_pos = jnp.arange(key_count, dtype=jnp.int32)
    query_seg = lax.dynamic_slice_in_dim(segment_row, row_start.astype(jnp.int32), row_count)
    allowed = (key_pos[None, :] <= query_pos[:, None]) & (segment_row[None, :] == query_seg[:, None])
    masked = jnp.where(allowed[None], scores, masked_fill)
    row_max = lax.optimization_barrier(jnp.max(masked, axis=-1, keepdims=True))
    log_total = row_max + jnp.log(lax.optimization_barrier(jnp.sum(jnp.exp(masked - row_max), axis=-1, keepdims=True)))
    weights = low(jnp.exp(masked - log_total))
    mixed_heads = jnp.einsum('hqk,khd->qhd', weights, value_heads, precision=top_scores)
    return mixed_heads.reshape(row_count, HEADS * HD)

def attend_sequence(query_seq, keys_seq, values_seq, segment_row):
    block_rows = math.gcd(LEN, 512)
    query_blocks = query_seq.reshape(LEN // block_rows, block_rows, D)
    starts = jnp.arange(LEN // block_rows, dtype=jnp.int32) * block_rows
    checked = jax.checkpoint(attend_rows)
    outputs = lax.map(lambda packed: checked(packed[0], packed[1], keys_seq, values_seq, segment_row), (query_blocks, starts))
    return outputs.reshape(LEN, D)

def reference(tokens, segment_ids, routes, earlier_logits, out_cotangent, query_weight, key_weight, value_weight, output_weight, router_weight, const_vectors, attn_gain, moe_gain, gate_weight, up_weight, down_weight):
    flat_routes = routes.reshape(-1)
    most_rows = SEQS * (LEN // POS_DEV) * CAP
    index_list = []
    valid_list = []
    for expert_id in range(EXPERTS):
        matches = flat_routes == expert_id
        found_rows = jnp.nonzero(matches, size=most_rows, fill_value=0)[0].astype(jnp.int32)
        match_count = jnp.sum(matches.astype(jnp.int32))
        index_list.append(found_rows)
        valid_list.append((jnp.arange(most_rows, dtype=jnp.int32) < match_count).astype(jnp.float32))
    slot_index = jnp.stack(index_list)
    slot_valid = jnp.stack(valid_list)
    positions = jnp.arange(LEN, dtype=jnp.int32)

    def forward(tokens_wide, prior_layer, query_matrix, key_matrix, value_matrix, output_matrix, router_matrix, consts, gain_attn, gain_moe, gate_w, up_w, down_w):
        normalized_first = low(rms_scale(tokens_wide) * gain_attn)
        query_unrotated = narrow_backward(jnp.einsum('ibg,gv->ibv', normalized_first, query_matrix, precision=top_scores))
        key_unrotated = narrow_backward(jnp.einsum('ibg,gv->ibv', normalized_first, key_matrix, precision=top_scores))
        value_projected = narrow_backward(jnp.einsum('ibg,gv->ibv', normalized_first, value_matrix, precision=top_scores))
        query_rot = low(rotary(query_unrotated, positions, 1.0))
        key_rot = low(rotary(key_unrotated, positions, 1.0))
        value_low = low(value_projected)
        attention_output = lax.map(lambda packed: attend_sequence(packed[0], packed[1], packed[2], packed[3]), (query_rot, key_rot, value_low, segment_ids))
        attention_output = low(narrow_backward(attention_output))
        projected_rows = narrow_backward(jnp.einsum('ibg,gv->ibv', attention_output, output_matrix, precision=top_scores))
        middle = tokens_wide + projected_rows
        normed_two = rms_scale(middle) * gain_moe
        normalized_narrow = low(normed_two)
        router_logits = jnp.einsum('ibg,gv->ibv', normalized_narrow, router_matrix, precision=top_scores) + prior_layer
        chosen = jnp.take_along_axis(router_logits, routes, axis=-1)
        gate_probs = jax.nn.softmax(chosen, axis=-1)
        flat_rows = normalized_narrow.reshape(-1, D)

        def run_expert(packed):
            gate_m, up_m, down_m, index_row, valid_row = packed
            rows_in = narrow_backward(flat_rows[index_row // 2])
            gate_pre = narrow_backward(jnp.dot(rows_in, gate_m, precision=top_scores))
            up_pre = narrow_backward(jnp.dot(rows_in, up_m, precision=top_scores))
            hidden = low(jax.nn.silu(gate_pre) * up_pre)
            result = low(narrow_backward(jnp.dot(hidden, down_m, precision=top_scores)))
            return result * valid_row[:, None]
        expert_rows = lax.map(run_expert, (gate_w, up_w, down_w, slot_index, slot_valid))
        entry_out = jnp.zeros((flat_routes.shape[0], D), jnp.float32).at[slot_index.reshape(-1)].add(expert_rows.reshape(-1, D))
        copy_rows = jnp.repeat(normed_two.reshape(-1, D), 2, axis=0)
        entry_out = entry_out + jnp.where((flat_routes == EXPERTS + 1)[:, None], copy_rows, 0.0)
        first_const = (flat_routes == EXPERTS + 2).astype(jnp.float32)[:, None]
        second_const = (flat_routes == EXPERTS + 3).astype(jnp.float32)[:, None]
        entry_out = entry_out + first_const * consts[:, 0][None, :] + second_const * consts[:, 1][None, :]
        entry_out = entry_out.reshape(SEQS, LEN, 2, D)
        return middle + lax.optimization_barrier(jnp.sum(gate_probs[..., None] * entry_out, axis=2))
    layer_out, pullback = jax.vjp(forward, tokens.astype(jnp.float32), earlier_logits.astype(jnp.float32), query_weight.astype(jnp.float32), key_weight.astype(jnp.float32), value_weight.astype(jnp.float32), output_weight.astype(jnp.float32), router_weight.astype(jnp.float32), const_vectors.astype(jnp.float32), attn_gain.astype(jnp.float32), moe_gain.astype(jnp.float32), gate_weight.astype(jnp.float32), up_weight.astype(jnp.float32), down_weight.astype(jnp.float32))
    grads = pullback(out_cotangent.astype(jnp.float32))
    return (layer_out.astype(jnp.bfloat16), grads[0], grads[1], grads[2], grads[3], grads[4], grads[5], grads[6], grads[7], grads[8], grads[9], grads[10], grads[11], grads[12])
```

```python
import math

import jax
import jax.numpy as jnp
from jax import lax
from jax.experimental import pallas as pl
from jax.experimental.pallas import tpu as pltpu
from jax.sharding import PartitionSpec as P

HEADS = 12
EXPERTS = 8
CAP = 64


norm_eps = 1e-06
masked_fill = -1e30


def rotary(values, positions, direction):
    dims_in = values.shape
    heads_view = values.reshape(dims_in[:-1] + (HEADS, dims_in[-1] // HEADS))
    half_size = heads_view.shape[-1] // 2
    frequency = jnp.exp(
        jnp.arange(half_size, dtype=jnp.float32) * (-2.0 * math.log(10000.0) / (2 * half_size))
    )
    angles = positions.astype(jnp.float32)[:, None] * frequency[None, :]
    cosine = jnp.cos(angles)[:, None, :]
    sine_part = direction * jnp.sin(angles)[:, None, :]
    first_half = heads_view[..., :half_size]
    second_half = heads_view[..., half_size:]
    turned = jnp.concatenate(
        [
            first_half * cosine - second_half * sine_part,
            second_half * cosine + first_half * sine_part,
        ],
        axis=-1,
    )
    return turned.reshape(dims_in)


def rms_parts(values):
    inverse = lax.rsqrt(jnp.mean(values * values, axis=-1, keepdims=True) + norm_eps)
    return (values * inverse, inverse)


def rms_back(grad_scaled, values, inverse):
    inner_mean = jnp.mean(grad_scaled * values, axis=-1, keepdims=True)
    return inverse * grad_scaled - values * inverse * inverse * inverse * inner_mean


def block_scores(query_heads, keys_all, segment_row, query_pos, query_seg, key_start, width_block):
    key_block = lax.dynamic_slice_in_dim(keys_all, key_start, width_block, 0)
    key_heads = key_block.reshape(width_block, HEADS, key_block.shape[-1] // HEADS)
    raw_scores = jnp.einsum(
        "qhd,khd->hqk", query_heads, key_heads, preferred_element_type=jnp.float32
    )
    scaled = raw_scores * key_heads.shape[-1] ** (-0.5)
    key_pos = key_start + jnp.arange(width_block, dtype=jnp.int32)
    key_seg = lax.dynamic_slice_in_dim(segment_row, key_start, width_block, 0)
    allowed = (key_pos[None, :] <= query_pos[:, None]) & (key_seg[None, :] == query_seg[:, None])
    return (scaled, allowed[None], key_heads)


def attend_forward(query_rot, keys_all, values_all, segment_row, offset, block_count, width_block):
    row_count = query_rot.shape[0]
    query_heads = query_rot.reshape(row_count, HEADS, -1)
    query_pos = offset + jnp.arange(row_count, dtype=jnp.int32)
    query_seg = lax.dynamic_slice_in_dim(segment_row, offset, row_count, 0)

    def gather_stats(number, state_pair):
        running_max, running_sum = state_pair
        scaled, allowed, key_heads = block_scores(
            query_heads,
            keys_all,
            segment_row,
            query_pos,
            query_seg,
            number * width_block,
            width_block,
        )
        masked = jnp.where(allowed, scaled, masked_fill)
        new_max = jnp.maximum(running_max, jnp.max(masked, axis=-1))
        exp_terms = jnp.where(allowed, jnp.exp(masked - new_max[..., None]), 0.0)
        return (new_max, running_sum * jnp.exp(running_max - new_max) + jnp.sum(exp_terms, axis=-1))

    start_max = jnp.full((HEADS, row_count), masked_fill, jnp.float32)
    start_sum = jnp.zeros((HEADS, row_count), jnp.float32)
    final_max, final_sum = lax.fori_loop(0, block_count, gather_stats, (start_max, start_sum))
    log_total = final_max + jnp.log(final_sum)

    def gather_output(number, running_out):
        key_start = number * width_block
        scaled, allowed, key_heads = block_scores(
            query_heads, keys_all, segment_row, query_pos, query_seg, key_start, width_block
        )
        weights = jnp.where(allowed, jnp.exp(scaled - log_total[..., None]), 0.0).astype(
            jnp.bfloat16
        )
        value_heads = lax.dynamic_slice_in_dim(values_all, key_start, width_block, 0).reshape(
            width_block, HEADS, -1
        )
        return running_out + jnp.einsum(
            "hqk,khd->qhd", weights, value_heads, preferred_element_type=jnp.float32
        )

    start_out = jnp.zeros((row_count, HEADS, query_heads.shape[-1]), jnp.float32)
    attention_output = lax.fori_loop(0, block_count, gather_output, start_out)
    return (attention_output.reshape(row_count, -1), log_total)


def attend_backward(
    query_rot,
    keys_all,
    values_all,
    segment_row,
    log_total,
    delta_sum,
    grad_low,
    offset,
    block_count,
    width_block,
):
    row_count = query_rot.shape[0]
    key_total = keys_all.shape[0]
    model_width = keys_all.shape[1]
    query_heads = query_rot.reshape(row_count, HEADS, -1)
    grad_heads = grad_low.reshape(row_count, HEADS, -1)
    query_pos = offset + jnp.arange(row_count, dtype=jnp.int32)
    query_seg = lax.dynamic_slice_in_dim(segment_row, offset, row_count, 0)
    score_scale = query_heads.shape[-1] ** (-0.5)

    def block_parts(number):
        key_start = number * width_block
        scaled, allowed, key_heads = block_scores(
            query_heads, keys_all, segment_row, query_pos, query_seg, key_start, width_block
        )
        prob_block = jnp.where(allowed, jnp.exp(scaled - log_total[..., None]), 0.0)
        value_heads = lax.dynamic_slice_in_dim(values_all, key_start, width_block, 0).reshape(
            width_block, HEADS, -1
        )
        grad_probs = jnp.einsum(
            "qhd,khd->hqk", grad_heads, value_heads, preferred_element_type=jnp.float32
        )
        grad_raw = (prob_block * (grad_probs - delta_sum[..., None]) * score_scale).astype(
            jnp.bfloat16
        )
        return (key_start, key_heads, prob_block, grad_raw)

    start_query = jnp.zeros((row_count, HEADS, query_heads.shape[-1]), jnp.float32)

    def accumulate(number, state_all):
        grad_query, grad_keys, grad_values = state_all
        key_start, key_heads, prob_block, grad_raw = block_parts(number)
        grad_query = grad_query + jnp.einsum(
            "hqk,khd->qhd", grad_raw, key_heads, preferred_element_type=jnp.float32
        )
        key_part = jnp.einsum(
            "hqk,qhd->khd", grad_raw, query_heads, preferred_element_type=jnp.float32
        )
        value_part = jnp.einsum(
            "hqk,qhd->khd",
            prob_block.astype(jnp.bfloat16),
            grad_heads,
            preferred_element_type=jnp.float32,
        )
        grad_keys = lax.dynamic_update_slice_in_dim(
            grad_keys, key_part.reshape(width_block, -1), key_start, 0
        )
        grad_values = lax.dynamic_update_slice_in_dim(
            grad_values, value_part.reshape(width_block, -1), key_start, 0
        )
        return (grad_query, grad_keys, grad_values)

    start_state = (
        start_query,
        jnp.zeros((key_total, model_width), jnp.float32),
        jnp.zeros((key_total, model_width), jnp.float32),
    )
    grad_query, grad_keys, grad_values = lax.fori_loop(0, block_count, accumulate, start_state)
    return (grad_query.reshape(row_count, -1), grad_keys, grad_values)


def body(
    tokens,
    segment_ids,
    routes,
    earlier_logits,
    out_cotangent,
    query_weight,
    key_weight,
    value_weight,
    output_weight,
    router_weight,
    const_vectors,
    attn_gain,
    moe_gain,
    gate_weight,
    up_weight,
    down_weight,
):
    (
        query_weight_wide,
        key_weight_wide,
        value_weight_wide,
        output_weight_wide,
        router_weight_wide,
        const_full,
        gain_attn,
        gain_moe,
    ) = (
        lax.all_gather(query_weight, "shard", axis=0, tiled=True),
        lax.all_gather(key_weight, "shard", axis=0, tiled=True),
        lax.all_gather(value_weight, "shard", axis=0, tiled=True),
        lax.all_gather(output_weight, "shard", axis=0, tiled=True),
        lax.all_gather(router_weight, "shard", axis=0, tiled=True),
        lax.all_gather(const_vectors, "shard", axis=0, tiled=True),
        lax.all_gather(attn_gain, "shard", axis=0, tiled=True),
        lax.all_gather(moe_gain, "shard", axis=0, tiled=True),
    )
    gate_full, up_full, down_full = (
        lax.all_gather(gate_weight, "shard", axis=1, tiled=True),
        lax.all_gather(up_weight, "shard", axis=1, tiled=True),
        lax.all_gather(down_weight, "shard", axis=1, tiled=True),
    )
    seq_count, pos_count, model_width = tokens.shape
    expert_pos = lax.axis_index("expert")
    offset = expert_pos * pos_count
    width_block = math.gcd(pos_count, 128)
    block_count = (expert_pos + 1) * (pos_count // width_block)
    positions = offset + jnp.arange(pos_count, dtype=jnp.int32)
    tokens_wide = tokens.astype(jnp.float32)
    scaled_one, inverse_one = rms_parts(tokens_wide)
    attn_gain_wide = gain_attn.astype(jnp.float32)
    normalized_first = (scaled_one * attn_gain_wide).astype(jnp.bfloat16)
    query_unrotated = jnp.einsum(
        "ibg,gv->ibv", normalized_first, query_weight_wide, preferred_element_type=jnp.float32
    )
    key_unrotated = jnp.einsum(
        "ibg,gv->ibv", normalized_first, key_weight_wide, preferred_element_type=jnp.float32
    )
    value_projected = jnp.einsum(
        "ibg,gv->ibv", normalized_first, value_weight_wide, preferred_element_type=jnp.float32
    )
    query_rot = rotary(query_unrotated, positions, 1.0).astype(jnp.bfloat16)
    key_rot = rotary(key_unrotated, positions, 1.0).astype(jnp.bfloat16)
    value_low = value_projected.astype(jnp.bfloat16)
    keys_all, values_all = (
        lax.all_gather(key_rot, "expert", axis=1, tiled=True),
        lax.all_gather(value_low, "expert", axis=1, tiled=True),
    )

    def forward_one(packed):
        return attend_forward(
            packed[0], packed[1], packed[2], packed[3], offset, block_count, width_block
        )

    attention_output, log_total = lax.map(
        forward_one, (query_rot, keys_all, values_all, segment_ids)
    )
    attention_output_narrow = attention_output.astype(jnp.bfloat16)
    projected_rows = jnp.einsum(
        "ibg,gv->ibv",
        attention_output_narrow,
        output_weight_wide,
        preferred_element_type=jnp.float32,
    )
    middle = tokens_wide + projected_rows
    scaled_two, inverse_two = rms_parts(middle)
    moe_gain_wide = gain_moe.astype(jnp.float32)
    normed_two = scaled_two * moe_gain_wide
    normalized_narrow = normed_two.astype(jnp.bfloat16)
    router_logits = (
        jnp.einsum(
            "ibg,gv->ibv", normalized_narrow, router_weight_wide, preferred_element_type=jnp.float32
        )
        + earlier_logits
    )
    chosen = jnp.take_along_axis(router_logits, routes, axis=-1)
    gate_probs = jax.nn.softmax(chosen, axis=-1)
    slot_count = seq_count * CAP
    route_entries = routes.reshape(seq_count, pos_count * 2)
    one_hot = (route_entries[..., None] == jnp.arange(EXPERTS, dtype=jnp.int32)).astype(jnp.int32)
    entry_ranks = jnp.cumsum(one_hot, axis=1) - one_hot
    slot_rank = jnp.sum(entry_ranks * one_hot, axis=-1)
    is_real = route_entries < EXPERTS
    destination = jnp.where(
        is_real,
        route_entries * slot_count
        + jnp.arange(seq_count, dtype=jnp.int32)[:, None] * CAP
        + slot_rank,
        EXPERTS * slot_count,
    ).reshape(-1)
    entry_rows = jnp.repeat(normalized_narrow.reshape(-1, model_width), 2, axis=0)
    send_rows = (
        jnp.zeros((EXPERTS * slot_count + 1, model_width), jnp.bfloat16)
        .at[destination]
        .set(entry_rows)[:-1]
        .reshape(EXPERTS, 1, slot_count, model_width)
    )
    received = lax.all_to_all(send_rows, "expert", split_axis=0, concat_axis=1, tiled=True)
    gate_pre = jnp.einsum("ensi,eif->ensf", received, gate_full, preferred_element_type=jnp.float32)
    up_pre = jnp.einsum("ensi,eif->ensf", received, up_full, preferred_element_type=jnp.float32)
    hidden = (jax.nn.silu(gate_pre) * up_pre).astype(jnp.bfloat16)
    result = jnp.einsum(
        "ensf,efi->ensi", hidden, down_full, preferred_element_type=jnp.float32
    ).astype(jnp.bfloat16)
    returned = lax.all_to_all(result, "expert", split_axis=1, concat_axis=0, tiled=True)
    zero_row = jnp.zeros((1, model_width), jnp.bfloat16)
    expert_vals = jnp.concatenate([returned.reshape(-1, model_width), zero_row], axis=0)[
        destination
    ].astype(jnp.float32)
    flat_routes = routes.reshape(-1)
    copy_rows = jnp.repeat(normed_two.reshape(-1, model_width), 2, axis=0)
    const_wide = const_full.astype(jnp.float32)
    is_copy = (flat_routes == EXPERTS + 1)[:, None]
    first_const = (flat_routes == EXPERTS + 2).astype(jnp.float32)[:, None]
    second_const = (flat_routes == EXPERTS + 3).astype(jnp.float32)[:, None]
    entry_vals = (
        expert_vals
        + jnp.where(is_copy, copy_rows, 0.0)
        + first_const * const_wide[:, 0][None, :]
        + second_const * const_wide[:, 1][None, :]
    )
    entry_vals = entry_vals.reshape(seq_count, pos_count, 2, model_width)
    layer_out = middle + jnp.sum(gate_probs[..., None] * entry_vals, axis=2)
    grad_mixed = out_cotangent.astype(jnp.float32)
    grad_gates = jnp.sum(grad_mixed[:, :, None, :] * entry_vals, axis=-1)
    grad_chosen = gate_probs * (
        grad_gates - jnp.sum(gate_probs * grad_gates, axis=-1, keepdims=True)
    )
    choice_ids = jnp.arange(EXPERTS + 4, dtype=jnp.int32)
    prior_logits_gradient = jnp.sum(
        (routes[..., None] == choice_ids).astype(jnp.float32) * grad_chosen[..., None], axis=2
    )
    grad_entries = (gate_probs[..., None] * grad_mixed[:, :, None, :]).reshape(-1, model_width)
    send_grads = (
        jnp.zeros((EXPERTS * slot_count + 1, model_width), jnp.bfloat16)
        .at[destination]
        .set(grad_entries.astype(jnp.bfloat16))[:-1]
        .reshape(EXPERTS, 1, slot_count, model_width)
    )
    owner_grads = lax.all_to_all(send_grads, "expert", split_axis=0, concat_axis=1, tiled=True)
    sigmoid_gate = jax.nn.sigmoid(gate_pre)
    silu_gate = gate_pre * sigmoid_gate
    hidden_back = (silu_gate * up_pre).astype(jnp.bfloat16)
    grad_hidden = jnp.einsum(
        "ensd,efd->ensf", owner_grads, down_full, preferred_element_type=jnp.float32
    )
    grad_gate_pre = (
        grad_hidden * up_pre * sigmoid_gate * (1.0 + gate_pre * (1.0 - sigmoid_gate))
    ).astype(jnp.bfloat16)
    grad_up_pre = (grad_hidden * silu_gate).astype(jnp.bfloat16)
    down_part = jnp.einsum(
        "ensf,ensd->efd", hidden_back, owner_grads, preferred_element_type=jnp.float32
    )
    gate_part = jnp.einsum(
        "ensi,ensf->eif", received, grad_gate_pre, preferred_element_type=jnp.float32
    )
    up_part = jnp.einsum(
        "ensi,ensf->eif", received, grad_up_pre, preferred_element_type=jnp.float32
    )
    grad_rows = (
        jnp.einsum("ensf,eif->ensi", grad_gate_pre, gate_full, preferred_element_type=jnp.float32)
        + jnp.einsum("ensf,eif->ensi", grad_up_pre, up_full, preferred_element_type=jnp.float32)
    ).astype(jnp.bfloat16)
    rows_back = lax.all_to_all(grad_rows, "expert", split_axis=1, concat_axis=0, tiled=True)
    gate_grad, up_grad, down_grad = (
        lax.psum_scatter(
            gate_part.astype(jnp.bfloat16), "shard", scatter_dimension=1, tiled=True
        ).astype(jnp.float32),
        lax.psum_scatter(
            up_part.astype(jnp.bfloat16), "shard", scatter_dimension=1, tiled=True
        ).astype(jnp.float32),
        lax.psum_scatter(
            down_part.astype(jnp.bfloat16), "shard", scatter_dimension=1, tiled=True
        ).astype(jnp.float32),
    )
    grad_row_entries = jnp.concatenate([rows_back.reshape(-1, model_width), zero_row], axis=0)[
        destination
    ].astype(jnp.float32)
    grad_copy = jnp.where(is_copy, grad_entries, 0.0)
    router_widened = router_weight_wide.astype(jnp.float32)
    grad_normed_two = jnp.sum(
        (grad_row_entries + grad_copy).reshape(seq_count, pos_count, 2, model_width), axis=2
    ) + jnp.einsum(
        "hwk,ok->hwo", prior_logits_gradient, router_widened, precision=lax.Precision.HIGHEST
    )
    router_part = jnp.einsum(
        "vrx,vrb->xb",
        normalized_narrow.astype(jnp.float32),
        prior_logits_gradient,
        precision=lax.Precision.HIGHEST,
    )
    const_part = jnp.stack(
        [jnp.sum(first_const * grad_entries, axis=0), jnp.sum(second_const * grad_entries, axis=0)],
        axis=-1,
    )
    moe_gain_part = jnp.sum(grad_normed_two * scaled_two, axis=(0, 1))
    grad_middle = grad_mixed + rms_back(grad_normed_two * moe_gain_wide, middle, inverse_two)
    gradient_projected = grad_middle.astype(jnp.bfloat16)
    output_part = jnp.einsum(
        "vrx,vrb->xb",
        attention_output_narrow,
        gradient_projected,
        preferred_element_type=jnp.float32,
    )
    grad_attended = jnp.einsum(
        "hwk,ok->hwo", gradient_projected, output_weight_wide, preferred_element_type=jnp.float32
    ).astype(jnp.bfloat16)
    delta_rows = jnp.sum(
        (grad_attended.astype(jnp.float32) * attention_output).reshape(
            seq_count, pos_count, HEADS, -1
        ),
        axis=-1,
    )
    delta_sum = jnp.transpose(delta_rows, (0, 2, 1))

    def backward_one(packed):
        return attend_backward(
            packed[0],
            packed[1],
            packed[2],
            packed[3],
            packed[4],
            packed[5],
            packed[6],
            offset,
            block_count,
            width_block,
        )

    grad_query_rot, grad_keys_all, grad_values_all = lax.map(
        backward_one,
        (query_rot, keys_all, values_all, segment_ids, log_total, delta_sum, grad_attended),
    )
    grad_keys, grad_values = (
        lax.psum_scatter(
            grad_keys_all.astype(jnp.bfloat16), "expert", scatter_dimension=1, tiled=True
        ).astype(jnp.float32),
        lax.psum_scatter(
            grad_values_all.astype(jnp.bfloat16), "expert", scatter_dimension=1, tiled=True
        ).astype(jnp.float32),
    )
    gradient_query_unrotated = rotary(grad_query_rot, positions, -1.0).astype(jnp.bfloat16)
    gradient_key_unrotated = rotary(grad_keys, positions, -1.0).astype(jnp.bfloat16)
    gradient_value_narrow = grad_values.astype(jnp.bfloat16)
    query_part = jnp.einsum(
        "vrx,vrb->xb",
        normalized_first,
        gradient_query_unrotated,
        preferred_element_type=jnp.float32,
    )
    key_part = jnp.einsum(
        "vrx,vrb->xb", normalized_first, gradient_key_unrotated, preferred_element_type=jnp.float32
    )
    value_part = jnp.einsum(
        "vrx,vrb->xb", normalized_first, gradient_value_narrow, preferred_element_type=jnp.float32
    )
    grad_normed_one = jnp.einsum(
        "hwk,ok->hwo",
        gradient_query_unrotated,
        query_weight_wide,
        preferred_element_type=jnp.float32,
    )
    grad_normed_one = grad_normed_one + jnp.einsum(
        "hwk,ok->hwo", gradient_key_unrotated, key_weight_wide, preferred_element_type=jnp.float32
    )
    grad_normed_one = grad_normed_one + jnp.einsum(
        "hwk,ok->hwo", gradient_value_narrow, value_weight_wide, preferred_element_type=jnp.float32
    )
    attn_gain_part = jnp.sum(grad_normed_one * scaled_one, axis=(0, 1))
    tokens_grad = grad_middle + rms_back(grad_normed_one * attn_gain_wide, tokens_wide, inverse_one)
    layer_parts = (
        lax.psum_scatter(
            query_part.astype(jnp.bfloat16), "shard", scatter_dimension=0, tiled=True
        ).astype(jnp.float32),
        lax.psum_scatter(
            key_part.astype(jnp.bfloat16), "shard", scatter_dimension=0, tiled=True
        ).astype(jnp.float32),
        lax.psum_scatter(
            value_part.astype(jnp.bfloat16), "shard", scatter_dimension=0, tiled=True
        ).astype(jnp.float32),
        lax.psum_scatter(
            output_part.astype(jnp.bfloat16), "shard", scatter_dimension=0, tiled=True
        ).astype(jnp.float32),
        lax.psum_scatter(
            router_part.astype(jnp.bfloat16), "shard", scatter_dimension=0, tiled=True
        ).astype(jnp.float32),
        lax.psum_scatter(
            const_part.astype(jnp.bfloat16), "shard", scatter_dimension=0, tiled=True
        ).astype(jnp.float32),
        lax.psum_scatter(
            attn_gain_part.astype(jnp.bfloat16), "shard", scatter_dimension=0, tiled=True
        ).astype(jnp.float32),
        lax.psum_scatter(
            moe_gain_part.astype(jnp.bfloat16), "shard", scatter_dimension=0, tiled=True
        ).astype(jnp.float32),
    )
    layer_grads = (
        lax.psum(layer_parts[0].astype(jnp.bfloat16), "expert").astype(jnp.float32),
        lax.psum(layer_parts[1].astype(jnp.bfloat16), "expert").astype(jnp.float32),
        lax.psum(layer_parts[2].astype(jnp.bfloat16), "expert").astype(jnp.float32),
        lax.psum(layer_parts[3].astype(jnp.bfloat16), "expert").astype(jnp.float32),
        lax.psum(layer_parts[4].astype(jnp.bfloat16), "expert").astype(jnp.float32),
        lax.psum(layer_parts[5].astype(jnp.bfloat16), "expert").astype(jnp.float32),
        lax.psum(layer_parts[6].astype(jnp.bfloat16), "expert").astype(jnp.float32),
        lax.psum(layer_parts[7].astype(jnp.bfloat16), "expert").astype(jnp.float32),
    )
    return (
        layer_out.astype(jnp.bfloat16),
        tokens_grad,
        prior_logits_gradient,
        layer_grads[0],
        layer_grads[1],
        layer_grads[2],
        layer_grads[3],
        layer_grads[4],
        layer_grads[5],
        layer_grads[6],
        layer_grads[7],
        gate_grad,
        up_grad,
        down_grad,
    )


RING = 4
PAIR = 2
LOCAL = 4
META = 16


def z_pairs(step):
    lines = PAIR * PAIR
    return [
        (z * lines + rest, (z + step) % RING * lines + rest)
        for z in range(RING)
        for rest in range(lines)
    ]


def along_z(values, step):
    return lax.ppermute(values, "shard", z_pairs(step))


def across_y(values):
    return lax.ppermute(values, "shard", [(s, s ^ PAIR) for s in range(RING * PAIR * PAIR)])


def across_core(values):
    return lax.ppermute(values, "shard", [(s, s ^ 1) for s in range(RING * PAIR * PAIR)])


def across_x(values):
    return lax.ppermute(values, "expert", [(0, 1), (1, 0)])


def gather_rows(own):
    ring = [own]
    for _ in range(RING - 1):
        ring.append(along_z(ring[-1], 1))
    return ring + [across_x(block) for block in ring]


def reduce_rows(parts):
    total = None
    for step in reversed(range(RING)):
        here = parts[step].astype(jnp.float32) + across_x(parts[RING + step]).astype(jnp.float32)
        if total is not None:
            here = here + along_z(total, -1).astype(jnp.float32)
        total = here.astype(jnp.bfloat16)
    return here


def meta_rows(rows, width):
    filled = jnp.concatenate(rows, axis=-1).reshape(len(rows) // 2, -1)
    return jnp.pad(filled, ((0, META - filled.shape[0]), (0, width - filled.shape[1]))).astype(
        jnp.bfloat16
    )


def dot_rows(left, right):
    return lax.dot_general(left, right, (((1,), (0,)), ((), ())), preferred_element_type=jnp.float32)


def dot_wide(left, right):
    return lax.dot_general(left, right, (((1,), (1,)), ((), ())), preferred_element_type=jnp.float32)


def dot_tall(left, right):
    return lax.dot_general(left, right, (((0,), (0,)), ((), ())), preferred_element_type=jnp.float32)


def owner_index(place, step, side, core):
    return (
        lax.rem(place[1] - step + RING, RING) * (PAIR * PAIR)
        + (place[2] ^ side) * PAIR
        + (place[3] ^ core)
    )


def prepare_kernel(place, *refs):
    block_count = RING * PAIR
    grads = refs[:block_count]
    mixed = refs[block_count : block_count + 4]
    downs = refs[block_count + 4 : block_count + 8]
    pick_ref, slot_ref, back_ref, wide_ref, down_ref = refs[block_count + 8 :]
    number = pl.program_id(0)
    rows = pick_ref.shape[2]

    @pl.when(number == 0)
    def _():
        later = lax.broadcasted_iota(jnp.int32, (rows, rows), 1)
        earlier = lax.broadcasted_iota(jnp.int32, (rows, rows), 0)
        before = jnp.where(earlier < later, 1.0, 0.0).astype(jnp.bfloat16)
        wanted = (lax.broadcasted_iota(jnp.int32, (8, rows), 0) + place[0] * LOCAL).astype(
            jnp.float32
        )
        inside = lax.broadcasted_iota(jnp.int32, (8, rows), 0) < LOCAL
        ranks = lax.broadcasted_iota(jnp.int32, (CAP, rows), 0).astype(jnp.float32)
        for block in range(block_count):
            meta = grads[block][rows : rows + META, :].astype(jnp.float32)
            first = meta[1:2, :rows]
            second = meta[1:2, rows : 2 * rows]
            named = jnp.where(((first == wanted) | (second == wanted)) & inside, 1.0, 0.0)
            rank = dot_rows(named.astype(jnp.bfloat16), before)
            pieces = []
            for expert in range(LOCAL):
                hit = (rank[expert : expert + 1] == ranks) & (named[expert : expert + 1] > 0.5)
                pieces.append(jnp.where(hit, 1.0, 0.0))
            pick = jnp.concatenate(pieces, axis=0).astype(jnp.bfloat16)
            pick_ref[block] = pick
            slot_ref[block] = dot_rows(pick, grads[block][:rows, :]).astype(jnp.bfloat16)

    half = wide_ref.shape[2] // 2
    for core in range(PAIR):
        for side in range(PAIR):
            piece = mixed[core * PAIR + side]
            depth = piece.shape[3]
            for step in range(RING):
                start = pl.multiple_of(owner_index(place, step, side, core) * depth, 16)
                wide_ref[0, pl.ds(start, depth), :half] = piece[step, 0, 0]
                wide_ref[0, pl.ds(start, depth), half:] = piece[step, 1, 0]
            own = downs[core * PAIR + side]
            deep = own.shape[1]
            local = (place[2] ^ side) * PAIR + (place[3] ^ core)
            down_ref[0, pl.ds(pl.multiple_of(local * deep, 16), deep), :] = own[0]
    width = slot_ref.shape[2]
    mine = slot_ref[:, pl.ds(pl.multiple_of(number * CAP, CAP), CAP), :]
    back_ref[0] = dot_wide(mine.reshape(block_count * CAP, width), down_ref[0])


def expert_kernel(place, *refs):
    block_count = RING * PAIR
    tokens = refs[:block_count]
    pick_ref, wide_ref, down_ref, back_ref = refs[block_count : block_count + 4]
    rest = refs[block_count + 4 :]
    slot_ref, hidden_ref, mixed_ref = rest[:3]
    grad_refs = rest[3 : 3 + block_count]
    out_refs = rest[3 + block_count : 3 + 2 * block_count]
    out_slots, grad_slots, gate_grads = rest[3 + 2 * block_count :]
    number = pl.program_id(0)
    rows = pick_ref.shape[2]
    width = slot_ref.shape[2]
    half = wide_ref.shape[2] // 2

    @pl.when(number == 0)
    def _():
        gate_grads[...] = jnp.zeros_like(gate_grads)
        for block in range(block_count):
            slot_ref[block] = dot_rows(pick_ref[block], tokens[block][:rows, :]).astype(
                jnp.bfloat16
            )

    span = pl.ds(pl.multiple_of(number * CAP, CAP), CAP)
    mine = slot_ref[:, span, :].reshape(block_count * CAP, width)
    both = dot_rows(mine, wide_ref[0])
    gate = both[:, :half]
    up = both[:, half:]
    sigmoid = 1.0 / (1.0 + jnp.exp(-gate))
    silu = gate * sigmoid
    hidden = silu * up
    back = back_ref[0]
    expert_id = (number + place[0] * LOCAL).astype(jnp.float32)
    chances = []
    product = jnp.sum(hidden * back, axis=1, keepdims=True)
    for block in range(block_count):
        meta = tokens[block][rows : rows + META, :].astype(jnp.float32)
        first = jnp.where(meta[1:2, :rows] == expert_id, 1.0, 0.0)
        second = jnp.where(meta[1:2, rows : 2 * rows] == expert_id, 1.0, 0.0)
        pick = pick_ref[block, span, :].astype(jnp.float32)
        chance = first * meta[0:1, :rows] + second * meta[0:1, rows : 2 * rows]
        chances.append(jnp.sum(pick * chance, axis=1, keepdims=True))
        spread = jnp.sum(
            pick * product[block * CAP : (block + 1) * CAP], axis=0, keepdims=True
        )
        gate_grads[block, 0:1, :rows] += first * spread
        gate_grads[block, 0:1, rows : 2 * rows] += second * spread
    chance = jnp.concatenate(chances, axis=0)
    back = back * chance
    weighted = (hidden * chance).astype(jnp.bfloat16)
    grad_gate = back * up * sigmoid * (1.0 + gate * (1.0 - sigmoid))
    grad_up = back * silu
    mixed = jnp.concatenate([grad_gate, grad_up], axis=1).astype(jnp.bfloat16)
    hidden_ref[0] = weighted
    mixed_ref[0] = mixed
    out_part = dot_rows(weighted, down_ref[0]).astype(jnp.bfloat16)
    out_slots[:, span, :] = out_part.reshape(block_count, CAP, width)
    grad_part = dot_wide(mixed, wide_ref[0]).astype(jnp.bfloat16)
    grad_slots[:, span, :] = grad_part.reshape(block_count, CAP, width)

    @pl.when(number == LOCAL - 1)
    def _():
        for block in range(block_count):
            pick = pick_ref[block]
            grad_refs[block][:rows, :] = dot_tall(pick, grad_slots[block]).astype(jnp.bfloat16)
            grad_refs[block][rows : rows + META, :] = gate_grads[block].astype(jnp.bfloat16)
            out_refs[block][...] = dot_tall(pick, out_slots[block]).astype(jnp.bfloat16)


def weight_grad_kernel(place, *refs):
    slot_ref, back_ref, hidden_ref, mixed_ref = refs[:4]
    wide_refs = refs[4:8]
    down_refs = refs[8:12]
    wide_sum, down_sum = refs[12:]
    number = pl.program_id(0)
    block_count, _, width = slot_ref.shape
    span = pl.ds(pl.multiple_of(number * CAP, CAP), CAP)
    rows = slot_ref[:, span, :].reshape(block_count * CAP, width)
    wide_sum[...] = dot_tall(rows, mixed_ref[0])
    grads = back_ref[:, span, :].reshape(block_count * CAP, width)
    down_sum[...] = dot_tall(hidden_ref[0], grads)
    half = wide_sum.shape[1] // 2
    for core in range(PAIR):
        for side in range(PAIR):
            piece = wide_refs[core * PAIR + side]
            depth = piece.shape[3]
            for step in range(RING):
                start = pl.multiple_of(owner_index(place, step, side, core) * depth, 16)
                part = wide_sum[pl.ds(start, depth), :]
                piece[step, 0, 0] = part[:, :half].astype(jnp.bfloat16)
                piece[step, 1, 0] = part[:, half:].astype(jnp.bfloat16)
            own = down_refs[core * PAIR + side]
            deep = own.shape[1]
            local = (place[2] ^ side) * PAIR + (place[3] ^ core)
            part = down_sum[pl.ds(pl.multiple_of(local * deep, 16), deep), :]
            own[0] = part.astype(jnp.bfloat16)


def whole(shape):
    return pl.BlockSpec(shape, lambda number, place: (0,) * len(shape))


def by_expert(shape, axis=0):
    return pl.BlockSpec(
        shape,
        lambda number, place: tuple(number if d == axis else 0 for d in range(len(shape))),
    )


def prepare_experts(place, grads, mixed, downs):
    padded, width = grads[0].shape
    rows = padded - META
    blocks = len(grads)
    _, _, local, depth, span = mixed[0].shape
    deep = downs[0].shape[1]
    model = depth * RING * PAIR * PAIR
    slots = blocks * CAP
    shapes = [
        ((blocks, local * CAP, rows), jnp.bfloat16),
        ((blocks, local * CAP, width), jnp.bfloat16),
        ((local, slots, span), jnp.float32),
        ((local, model, 2 * span), jnp.bfloat16),
        ((local, deep * PAIR * PAIR, width), jnp.bfloat16),
    ]
    return pl.pallas_call(
        prepare_kernel,
        name="prepare_experts",
        out_shape=[jax.ShapeDtypeStruct(s, d) for s, d in shapes],
        grid_spec=pltpu.PrefetchScalarGridSpec(
            num_scalar_prefetch=1,
            grid=(local,),
            in_specs=[whole(g.shape) for g in grads]
            + [by_expert((RING, 2, 1, depth, span), 2)] * 4
            + [by_expert((1, deep, width))] * 4,
            out_specs=[
                whole(shapes[0][0]),
                whole(shapes[1][0]),
                by_expert((1, slots, span)),
                by_expert((1, model, 2 * span)),
                by_expert((1, deep * PAIR * PAIR, width)),
            ],
        ),
    )(place, *grads, *mixed, *downs)


def run_experts(place, tokens, pick, wide, down, back):
    padded, width = tokens[0].shape
    rows = padded - META
    blocks = len(tokens)
    local, model, span2 = wide.shape
    span = span2 // 2
    slots = blocks * CAP
    shapes = [
        ((blocks, local * CAP, width), jnp.bfloat16),
        ((local, slots, span), jnp.bfloat16),
        ((local, slots, span2), jnp.bfloat16),
    ]
    shapes = shapes + [((padded, width), jnp.bfloat16)] * blocks
    shapes = shapes + [((rows, width), jnp.bfloat16)] * blocks
    results = pl.pallas_call(
        expert_kernel,
        name="run_experts",
        out_shape=[jax.ShapeDtypeStruct(s, d) for s, d in shapes],
        grid_spec=pltpu.PrefetchScalarGridSpec(
            num_scalar_prefetch=1,
            grid=(local,),
            in_specs=[whole(t.shape) for t in tokens]
            + [
                whole(pick.shape),
                by_expert((1, model, span2)),
                by_expert((1, span, width)),
                by_expert((1, slots, span)),
            ],
            out_specs=[
                whole(shapes[0][0]),
                by_expert((1, slots, span)),
                by_expert((1, slots, span2)),
            ]
            + [whole(s) for s, _ in shapes[3:]],
            scratch_shapes=[
                pltpu.VMEM((blocks, local * CAP, width), jnp.bfloat16),
                pltpu.VMEM((blocks, local * CAP, width), jnp.bfloat16),
                pltpu.VMEM((blocks, META, width), jnp.float32),
            ],
        ),
    )(place, *tokens, pick, wide, down, back)
    return results[:3], results[3 : 3 + blocks], results[3 + blocks :]


def weight_grads(place, slots, backs, hidden, mixed):
    blocks, total, width = slots.shape
    local, rows, span = hidden.shape
    depth = width // (RING * PAIR * PAIR)
    deep = span // (PAIR * PAIR)
    wide_shape = (RING, 2, local, depth, span)
    down_shape = (local, deep, width)
    results = pl.pallas_call(
        weight_grad_kernel,
        name="weight_grads",
        out_shape=[jax.ShapeDtypeStruct(wide_shape, jnp.bfloat16)] * 4
        + [jax.ShapeDtypeStruct(down_shape, jnp.bfloat16)] * 4,
        grid_spec=pltpu.PrefetchScalarGridSpec(
            num_scalar_prefetch=1,
            grid=(local,),
            in_specs=[
                whole(slots.shape),
                whole(backs.shape),
                by_expert((1, rows, span)),
                by_expert((1, rows, 2 * span)),
            ],
            out_specs=[by_expert((RING, 2, 1, depth, span), 2)] * 4
            + [by_expert((1, deep, width))] * 4,
            scratch_shapes=[
                pltpu.VMEM((width, 2 * span), jnp.float32),
                pltpu.VMEM((span, width), jnp.float32),
            ],
        ),
    )(place, slots, backs, hidden, mixed)
    return results[:4], results[4:]


def add_low(left, right):
    return (left.astype(jnp.float32) + right.astype(jnp.float32)).astype(jnp.bfloat16)


def exchange_expert_weights(gate_weight, up_weight, down_weight, z_place):
    span = gate_weight.shape[2] // RING
    pieces = []
    for step in range(RING):
        start = lax.rem(z_place + step, RING) * span
        piece = jnp.stack(
            [
                lax.dynamic_slice_in_dim(gate_weight, start, span, 2),
                lax.dynamic_slice_in_dim(up_weight, start, span, 2),
            ]
        )
        pieces.append(along_z(piece, step) if step else piece)
    own = jnp.stack(pieces)
    other = across_y(own)
    mixed = [own, other, across_core(own), across_core(other)]
    down_other = across_y(down_weight)
    downs = [down_weight, down_other, across_core(down_weight), across_core(down_other)]
    return mixed, downs


def reduce_expert_grads(mixed, downs, z_place):
    near = add_low(mixed[0], across_core(mixed[2]))
    far = add_low(mixed[1], across_core(mixed[3]))
    mine = add_low(near, across_y(far))
    parts = [mine[0]] + [along_z(mine[step], -step) for step in range(1, RING)]
    columns = []
    for column in range(RING):
        choice = lax.rem(column - z_place + RING, RING)
        chosen = parts[0]
        for step in range(1, RING):
            chosen = jnp.where(choice == step, parts[step], chosen)
        columns.append(chosen)
    both = jnp.concatenate(columns, axis=-1).astype(jnp.float32)
    near = add_low(downs[0], across_core(downs[2]))
    far = add_low(downs[1], across_core(downs[3]))
    down = near.astype(jnp.float32) + across_y(far).astype(jnp.float32)
    return both[0], both[1], down


def body_split(
    tokens,
    segment_ids,
    routes,
    earlier_logits,
    out_cotangent,
    query_weight,
    key_weight,
    value_weight,
    output_weight,
    router_weight,
    const_vectors,
    attn_gain,
    moe_gain,
    gate_weight,
    up_weight,
    down_weight,
):
    _, pos_count, model_width = tokens.shape
    tokens, segment_row, routes = tokens[0], segment_ids[0], routes[0]
    earlier_logits, cotangent_low = earlier_logits[0], out_cotangent[0]
    x_place = lax.axis_index("expert")
    shard_place = lax.axis_index("shard")
    z_place = shard_place // (PAIR * PAIR)
    y_place = lax.rem(shard_place // PAIR, PAIR)
    core_place = lax.rem(shard_place, PAIR)
    order = jnp.arange(4, dtype=jnp.int32)
    place = jnp.where(
        order == 0,
        x_place,
        jnp.where(order == 1, z_place, jnp.where(order == 2, y_place, core_place)),
    ).astype(jnp.int32)
    choices = router_weight.shape[1]
    consts = const_vectors.shape[1]
    small_count = choices + consts + 2
    small = jnp.concatenate(
        [router_weight, const_vectors, attn_gain[:, None], moe_gain[:, None]], axis=1
    )
    small = jnp.pad(small, ((0, 0), (0, 128 - small_count)))
    packed = jnp.concatenate(
        [query_weight, key_weight, value_weight, output_weight, small], axis=1
    )
    gathered = lax.all_gather(packed, "shard", axis=0, tiled=True)
    other_tokens = across_x(tokens)
    routes_low = routes.astype(jnp.bfloat16)
    route_rows = [routes_low[:, 0], routes_low[:, 1]]
    zero_rows = [jnp.zeros_like(route_rows[0])] * 2
    cotangent_blocks = gather_rows(
        jnp.concatenate([cotangent_low, meta_rows(zero_rows + route_rows, model_width)], axis=0)
    )
    mixed_pieces, down_pieces = exchange_expert_weights(
        gate_weight, up_weight, down_weight, z_place
    )
    pick, back_slots, back_hidden, wide_full, down_full = prepare_experts(
        place, cotangent_blocks, mixed_pieces, down_pieces
    )

    joint = 3 * model_width
    joint_weight = gathered[:, :joint]
    output_wide = gathered[:, joint : joint + model_width]
    tail = gathered[:, joint + model_width :].astype(jnp.float32)
    router_low = gathered[:, joint + model_width : joint + model_width + choices]
    router_wide = tail[:, :choices]
    const_wide = tail[:, choices : choices + consts].T
    gain_attn = tail[:, choices + consts]
    gain_moe = tail[:, choices + consts + 1]

    offset = x_place * pos_count
    width_block = math.gcd(pos_count, 128)
    block_count = (x_place + 1) * (pos_count // width_block)
    first_tokens = jnp.where(x_place == 0, tokens, other_tokens)
    second_tokens = jnp.where(x_place == 0, other_tokens, tokens)
    all_wide = jnp.concatenate([first_tokens, second_tokens], axis=0).astype(jnp.float32)
    scaled_all, _ = rms_parts(all_wide)
    normed_all = (scaled_all * gain_attn).astype(jnp.bfloat16)
    tokens_wide = tokens.astype(jnp.float32)
    scaled_one, inverse_one = rms_parts(tokens_wide)
    normed_own = (scaled_one * gain_attn).astype(jnp.bfloat16)
    positions = offset + jnp.arange(pos_count, dtype=jnp.int32)
    all_positions = jnp.arange(PAIR * pos_count, dtype=jnp.int32)
    query_rot = rotary(dot_rows(normed_own, joint_weight[:, :model_width]), positions, 1.0)
    query_rot = query_rot.astype(jnp.bfloat16)
    key_value = dot_rows(normed_all, joint_weight[:, model_width:])
    keys_all = rotary(key_value[:, :model_width], all_positions, 1.0).astype(jnp.bfloat16)
    values_all = key_value[:, model_width:].astype(jnp.bfloat16)
    attention_output, log_total = attend_forward(
        query_rot, keys_all, values_all, segment_row, offset, block_count, width_block
    )
    attention_low = attention_output.astype(jnp.bfloat16)
    middle = tokens_wide + dot_rows(attention_low, output_wide)
    scaled_two, inverse_two = rms_parts(middle)
    normed_two = scaled_two * gain_moe
    normed_low = normed_two.astype(jnp.bfloat16)
    router_logits = dot_rows(normed_low, router_low) + earlier_logits
    choice_ids = jnp.arange(choices, dtype=jnp.int32)
    one_hot = (routes[..., None] == choice_ids).astype(jnp.float32)
    chosen = jnp.sum(one_hot * router_logits[:, None, :], axis=-1)
    gate_probs = jax.nn.softmax(chosen, axis=-1)
    probs_low = gate_probs.astype(jnp.bfloat16)
    token_blocks = gather_rows(
        jnp.concatenate(
            [
                normed_low,
                meta_rows([probs_low[:, 0], probs_low[:, 1]] + route_rows, model_width),
            ],
            axis=0,
        )
    )
    (token_slots, hidden, mixed), grad_parts, out_parts = run_experts(
        place, token_blocks, pick, wide_full, down_full, back_hidden
    )
    grad_total = reduce_rows(grad_parts)
    wide_grads, down_grads = weight_grads(place, token_slots, back_slots, hidden, mixed)
    out_total = reduce_rows(out_parts)
    gate_grad, up_grad, down_grad = reduce_expert_grads(wide_grads, down_grads, z_place)

    cotangent = cotangent_low.astype(jnp.float32)
    copies = jnp.sum(one_hot[..., EXPERTS + 1] * gate_probs, axis=-1)[:, None]
    const_probs = jnp.sum(one_hot[..., EXPERTS + 2 :] * gate_probs[..., None], axis=1)
    const_rows = sum(const_probs[:, i : i + 1] * const_wide[i : i + 1] for i in range(consts))
    layer_out = middle + out_total + copies * normed_two + const_rows
    copy_dot = jnp.sum(cotangent * normed_two, axis=-1)
    const_dot = jnp.stack(
        [jnp.sum(cotangent * const_wide[i], axis=-1) for i in range(consts)], axis=-1
    )
    grad_rows = grad_total[:pos_count]
    expert_dot = jnp.stack(
        [grad_total[pos_count, i * pos_count : (i + 1) * pos_count] for i in range(2)], axis=-1
    )
    grad_gates = (
        expert_dot
        + one_hot[..., EXPERTS + 1] * copy_dot[:, None]
        + jnp.sum(one_hot[..., EXPERTS + 2 :] * const_dot[:, None, :], axis=-1)
    )
    grad_chosen = gate_probs * (
        grad_gates - jnp.sum(gate_probs * grad_gates, axis=-1, keepdims=True)
    )
    prior_logits_gradient = jnp.sum(one_hot * grad_chosen[..., None], axis=1)
    highest = lax.Precision.HIGHEST
    grad_normed_two = (
        grad_rows
        + copies * cotangent
        + jnp.einsum("wk,ok->wo", prior_logits_gradient, router_wide, precision=highest)
    )
    router_part = jnp.einsum(
        "rx,rb->xb", normed_low.astype(jnp.float32), prior_logits_gradient, precision=highest
    )
    const_part = jnp.einsum("rx,rb->xb", cotangent, const_probs, precision=highest)
    moe_gain_part = jnp.sum(grad_normed_two * scaled_two, axis=0)
    grad_middle = cotangent + rms_back(grad_normed_two * gain_moe, middle, inverse_two)
    grad_projected = grad_middle.astype(jnp.bfloat16)
    output_part = dot_tall(attention_low, grad_projected)
    grad_attended = dot_wide(grad_projected, output_wide).astype(jnp.bfloat16)
    delta_sum = jnp.transpose(
        jnp.sum(
            (grad_attended.astype(jnp.float32) * attention_output).reshape(pos_count, HEADS, -1),
            axis=-1,
        )
    )
    grad_query_rot, grad_keys, grad_values = attend_backward(
        query_rot,
        keys_all,
        values_all,
        segment_row,
        log_total,
        delta_sum,
        grad_attended,
        offset,
        block_count,
        width_block,
    )
    grad_query = rotary(grad_query_rot, positions, -1.0).astype(jnp.bfloat16)
    grad_key = rotary(grad_keys, all_positions, -1.0).astype(jnp.bfloat16)
    grad_value = grad_values.astype(jnp.bfloat16)
    grad_key_value = jnp.concatenate([grad_key, grad_value], axis=1)
    grad_normed_all = dot_wide(grad_key_value, joint_weight[:, model_width:])
    first_grad = grad_normed_all[:pos_count]
    shared = lax.ppermute(first_grad.astype(jnp.bfloat16), "expert", [(1, 0)])
    own_grad = jnp.where(x_place == 0, first_grad, grad_normed_all[pos_count:])
    grad_normed_one = (
        dot_wide(grad_query, joint_weight[:, :model_width]) + own_grad + shared.astype(jnp.float32)
    )
    query_part = dot_tall(normed_own, grad_query)
    key_value_part = dot_tall(normed_all, grad_key_value)
    attn_gain_part = jnp.sum(grad_normed_one * scaled_one, axis=0)
    tokens_grad = grad_middle + rms_back(grad_normed_one * gain_attn, tokens_wide, inverse_one)
    small_part = jnp.concatenate(
        [router_part, const_part, attn_gain_part[:, None], moe_gain_part[:, None]], axis=1
    )
    small_part = jnp.pad(small_part, ((0, 0), (0, 128 - small_count)))
    output_sum = lax.psum_scatter(
        output_part.astype(jnp.bfloat16), "shard", scatter_dimension=0, tiled=True
    )
    packed_part = jnp.concatenate([query_part, key_value_part, small_part], axis=1)
    packed_sum = lax.psum_scatter(
        packed_part.astype(jnp.bfloat16), "shard", scatter_dimension=0, tiled=True
    )
    output_grad = output_sum.astype(jnp.float32) + across_x(output_sum).astype(jnp.float32)
    packed_grad = packed_sum.astype(jnp.float32) + across_x(packed_sum).astype(jnp.float32)
    small_grad = packed_grad[:, joint:]
    return (
        layer_out.astype(jnp.bfloat16)[None],
        tokens_grad[None],
        prior_logits_gradient[None],
        packed_grad[:, :model_width],
        packed_grad[:, model_width : 2 * model_width],
        packed_grad[:, 2 * model_width : joint],
        output_grad,
        small_grad[:, :choices],
        small_grad[:, choices : choices + consts],
        small_grad[:, choices + consts],
        small_grad[:, choices + consts + 1],
        gate_grad,
        up_grad,
        down_grad,
    )


def solution(mesh):
    in_specs = (
        P("shard", "expert", None),
        P("shard", None),
        P("shard", "expert", None),
        P("shard", "expert", None),
        P("shard", "expert", None),
        P("shard", None),
        P("shard", None),
        P("shard", None),
        P("shard", None),
        P("shard", None),
        P("shard", None),
        P("shard"),
        P("shard"),
        P("expert", "shard", None),
        P("expert", "shard", None),
        P("expert", "shard", None),
    )
    out_specs = (
        P("shard", "expert", None),
        P("shard", "expert", None),
        P("shard", "expert", None),
        P("shard", None),
        P("shard", None),
        P("shard", None),
        P("shard", None),
        P("shard", None),
        P("shard", None),
        P("shard"),
        P("shard"),
        P("expert", "shard", None),
        P("expert", "shard", None),
        P("expert", "shard", None),
    )
    divided = mesh.shape["expert"] == PAIR and mesh.shape["shard"] == RING * PAIR * PAIR
    chosen = body_split if divided else body
    return jax.shard_map(chosen, mesh=mesh, in_specs=in_specs, out_specs=out_specs, check_vma=False)
```

```python
import math

import jax
import jax.numpy as jnp
from jax import lax
from jax.experimental import pallas as pl
from jax.experimental.pallas import tpu as pltpu
from jax.sharding import PartitionSpec as P

HEADS = 12
EXPERTS = 8
CAP = 64


norm_eps = 1e-06
masked_fill = -1e30


def rotary(values, positions, direction):
    dims_in = values.shape
    heads_view = values.reshape(dims_in[:-1] + (HEADS, dims_in[-1] // HEADS))
    half_size = heads_view.shape[-1] // 2
    frequency = jnp.exp(
        jnp.arange(half_size, dtype=jnp.float32) * (-2.0 * math.log(10000.0) / (2 * half_size))
    )
    angles = positions.astype(jnp.float32)[:, None] * frequency[None, :]
    cosine = jnp.cos(angles)[:, None, :]
    sine_part = direction * jnp.sin(angles)[:, None, :]
    first_half = heads_view[..., :half_size]
    second_half = heads_view[..., half_size:]
    turned = jnp.concatenate(
        [
            first_half * cosine - second_half * sine_part,
            second_half * cosine + first_half * sine_part,
        ],
        axis=-1,
    )
    return turned.reshape(dims_in)


def rms_parts(values):
    inverse = lax.rsqrt(jnp.mean(values * values, axis=-1, keepdims=True) + norm_eps)
    return (values * inverse, inverse)


def rms_back(grad_scaled, values, inverse):
    inner_mean = jnp.mean(grad_scaled * values, axis=-1, keepdims=True)
    return inverse * grad_scaled - values * inverse * inverse * inverse * inner_mean


def block_scores(query_heads, keys_all, segment_row, query_pos, query_seg, key_start, width_block):
    key_block = lax.dynamic_slice_in_dim(keys_all, key_start, width_block, 0)
    key_heads = key_block.reshape(width_block, HEADS, key_block.shape[-1] // HEADS)
    raw_scores = jnp.einsum(
        "qhd,khd->hqk", query_heads, key_heads, preferred_element_type=jnp.float32
    )
    scaled = raw_scores * key_heads.shape[-1] ** (-0.5)
    key_pos = key_start + jnp.arange(width_block, dtype=jnp.int32)
    key_seg = lax.dynamic_slice_in_dim(segment_row, key_start, width_block, 0)
    allowed = (key_pos[None, :] <= query_pos[:, None]) & (key_seg[None, :] == query_seg[:, None])
    return (scaled, allowed[None], key_heads)


def attend_forward(query_rot, keys_all, values_all, segment_row, offset, block_count, width_block):
    row_count = query_rot.shape[0]
    query_heads = query_rot.reshape(row_count, HEADS, -1)
    query_pos = offset + jnp.arange(row_count, dtype=jnp.int32)
    query_seg = lax.dynamic_slice_in_dim(segment_row, offset, row_count, 0)

    def gather_stats(number, state_pair):
        running_max, running_sum = state_pair
        scaled, allowed, key_heads = block_scores(
            query_heads,
            keys_all,
            segment_row,
            query_pos,
            query_seg,
            number * width_block,
            width_block,
        )
        masked = jnp.where(allowed, scaled, masked_fill)
        new_max = jnp.maximum(running_max, jnp.max(masked, axis=-1))
        exp_terms = jnp.where(allowed, jnp.exp(masked - new_max[..., None]), 0.0)
        return (new_max, running_sum * jnp.exp(running_max - new_max) + jnp.sum(exp_terms, axis=-1))

    start_max = jnp.full((HEADS, row_count), masked_fill, jnp.float32)
    start_sum = jnp.zeros((HEADS, row_count), jnp.float32)
    final_max, final_sum = lax.fori_loop(0, block_count, gather_stats, (start_max, start_sum))
    log_total = final_max + jnp.log(final_sum)

    def gather_output(number, running_out):
        key_start = number * width_block
        scaled, allowed, key_heads = block_scores(
            query_heads, keys_all, segment_row, query_pos, query_seg, key_start, width_block
        )
        weights = jnp.where(allowed, jnp.exp(scaled - log_total[..., None]), 0.0).astype(
            jnp.bfloat16
        )
        value_heads = lax.dynamic_slice_in_dim(values_all, key_start, width_block, 0).reshape(
            width_block, HEADS, -1
        )
        return running_out + jnp.einsum(
            "hqk,khd->qhd", weights, value_heads, preferred_element_type=jnp.float32
        )

    start_out = jnp.zeros((row_count, HEADS, query_heads.shape[-1]), jnp.float32)
    attention_output = lax.fori_loop(0, block_count, gather_output, start_out)
    return (attention_output.reshape(row_count, -1), log_total)


def attend_backward(
    query_rot,
    keys_all,
    values_all,
    segment_row,
    log_total,
    delta_sum,
    grad_low,
    offset,
    block_count,
    width_block,
):
    row_count = query_rot.shape[0]
    key_total = keys_all.shape[0]
    model_width = keys_all.shape[1]
    query_heads = query_rot.reshape(row_count, HEADS, -1)
    grad_heads = grad_low.reshape(row_count, HEADS, -1)
    query_pos = offset + jnp.arange(row_count, dtype=jnp.int32)
    query_seg = lax.dynamic_slice_in_dim(segment_row, offset, row_count, 0)
    score_scale = query_heads.shape[-1] ** (-0.5)

    def block_parts(number):
        key_start = number * width_block
        scaled, allowed, key_heads = block_scores(
            query_heads, keys_all, segment_row, query_pos, query_seg, key_start, width_block
        )
        prob_block = jnp.where(allowed, jnp.exp(scaled - log_total[..., None]), 0.0)
        value_heads = lax.dynamic_slice_in_dim(values_all, key_start, width_block, 0).reshape(
            width_block, HEADS, -1
        )
        grad_probs = jnp.einsum(
            "qhd,khd->hqk", grad_heads, value_heads, preferred_element_type=jnp.float32
        )
        grad_raw = (prob_block * (grad_probs - delta_sum[..., None]) * score_scale).astype(
            jnp.bfloat16
        )
        return (key_start, key_heads, prob_block, grad_raw)

    start_query = jnp.zeros((row_count, HEADS, query_heads.shape[-1]), jnp.float32)

    def accumulate(number, state_all):
        grad_query, grad_keys, grad_values = state_all
        key_start, key_heads, prob_block, grad_raw = block_parts(number)
        grad_query = grad_query + jnp.einsum(
            "hqk,khd->qhd", grad_raw, key_heads, preferred_element_type=jnp.float32
        )
        key_part = jnp.einsum(
            "hqk,qhd->khd", grad_raw, query_heads, preferred_element_type=jnp.float32
        )
        value_part = jnp.einsum(
            "hqk,qhd->khd",
            prob_block.astype(jnp.bfloat16),
            grad_heads,
            preferred_element_type=jnp.float32,
        )
        grad_keys = lax.dynamic_update_slice_in_dim(
            grad_keys, key_part.reshape(width_block, -1), key_start, 0
        )
        grad_values = lax.dynamic_update_slice_in_dim(
            grad_values, value_part.reshape(width_block, -1), key_start, 0
        )
        return (grad_query, grad_keys, grad_values)

    start_state = (
        start_query,
        jnp.zeros((key_total, model_width), jnp.float32),
        jnp.zeros((key_total, model_width), jnp.float32),
    )
    grad_query, grad_keys, grad_values = lax.fori_loop(0, block_count, accumulate, start_state)
    return (grad_query.reshape(row_count, -1), grad_keys, grad_values)


def body(
    tokens,
    segment_ids,
    routes,
    earlier_logits,
    out_cotangent,
    query_weight,
    key_weight,
    value_weight,
    output_weight,
    router_weight,
    const_vectors,
    attn_gain,
    moe_gain,
    gate_weight,
    up_weight,
    down_weight,
):
    (
        query_weight_wide,
        key_weight_wide,
        value_weight_wide,
        output_weight_wide,
        router_weight_wide,
        const_full,
        gain_attn,
        gain_moe,
    ) = (
        lax.all_gather(query_weight, "shard", axis=0, tiled=True),
        lax.all_gather(key_weight, "shard", axis=0, tiled=True),
        lax.all_gather(value_weight, "shard", axis=0, tiled=True),
        lax.all_gather(output_weight, "shard", axis=0, tiled=True),
        lax.all_gather(router_weight, "shard", axis=0, tiled=True),
        lax.all_gather(const_vectors, "shard", axis=0, tiled=True),
        lax.all_gather(attn_gain, "shard", axis=0, tiled=True),
        lax.all_gather(moe_gain, "shard", axis=0, tiled=True),
    )
    gate_full, up_full, down_full = (
        lax.all_gather(gate_weight, "shard", axis=1, tiled=True),
        lax.all_gather(up_weight, "shard", axis=1, tiled=True),
        lax.all_gather(down_weight, "shard", axis=1, tiled=True),
    )
    seq_count, pos_count, model_width = tokens.shape
    expert_pos = lax.axis_index("expert")
    offset = expert_pos * pos_count
    width_block = math.gcd(pos_count, 128)
    block_count = (expert_pos + 1) * (pos_count // width_block)
    positions = offset + jnp.arange(pos_count, dtype=jnp.int32)
    tokens_wide = tokens.astype(jnp.float32)
    scaled_one, inverse_one = rms_parts(tokens_wide)
    attn_gain_wide = gain_attn.astype(jnp.float32)
    normalized_first = (scaled_one * attn_gain_wide).astype(jnp.bfloat16)
    query_unrotated = jnp.einsum(
        "ibg,gv->ibv", normalized_first, query_weight_wide, preferred_element_type=jnp.float32
    )
    key_unrotated = jnp.einsum(
        "ibg,gv->ibv", normalized_first, key_weight_wide, preferred_element_type=jnp.float32
    )
    value_projected = jnp.einsum(
        "ibg,gv->ibv", normalized_first, value_weight_wide, preferred_element_type=jnp.float32
    )
    query_rot = rotary(query_unrotated, positions, 1.0).astype(jnp.bfloat16)
    key_rot = rotary(key_unrotated, positions, 1.0).astype(jnp.bfloat16)
    value_low = value_projected.astype(jnp.bfloat16)
    keys_all, values_all = (
        lax.all_gather(key_rot, "expert", axis=1, tiled=True),
        lax.all_gather(value_low, "expert", axis=1, tiled=True),
    )

    def forward_one(packed):
        return attend_forward(
            packed[0], packed[1], packed[2], packed[3], offset, block_count, width_block
        )

    attention_output, log_total = lax.map(
        forward_one, (query_rot, keys_all, values_all, segment_ids)
    )
    attention_output_narrow = attention_output.astype(jnp.bfloat16)
    projected_rows = jnp.einsum(
        "ibg,gv->ibv",
        attention_output_narrow,
        output_weight_wide,
        preferred_element_type=jnp.float32,
    )
    middle = tokens_wide + projected_rows
    scaled_two, inverse_two = rms_parts(middle)
    moe_gain_wide = gain_moe.astype(jnp.float32)
    normed_two = scaled_two * moe_gain_wide
    normalized_narrow = normed_two.astype(jnp.bfloat16)
    router_logits = (
        jnp.einsum(
            "ibg,gv->ibv", normalized_narrow, router_weight_wide, preferred_element_type=jnp.float32
        )
        + earlier_logits
    )
    chosen = jnp.take_along_axis(router_logits, routes, axis=-1)
    gate_probs = jax.nn.softmax(chosen, axis=-1)
    slot_count = seq_count * CAP
    route_entries = routes.reshape(seq_count, pos_count * 2)
    one_hot = (route_entries[..., None] == jnp.arange(EXPERTS, dtype=jnp.int32)).astype(jnp.int32)
    entry_ranks = jnp.cumsum(one_hot, axis=1) - one_hot
    slot_rank = jnp.sum(entry_ranks * one_hot, axis=-1)
    is_real = route_entries < EXPERTS
    destination = jnp.where(
        is_real,
        route_entries * slot_count
        + jnp.arange(seq_count, dtype=jnp.int32)[:, None] * CAP
        + slot_rank,
        EXPERTS * slot_count,
    ).reshape(-1)
    entry_rows = jnp.repeat(normalized_narrow.reshape(-1, model_width), 2, axis=0)
    send_rows = (
        jnp.zeros((EXPERTS * slot_count + 1, model_width), jnp.bfloat16)
        .at[destination]
        .set(entry_rows)[:-1]
        .reshape(EXPERTS, 1, slot_count, model_width)
    )
    received = lax.all_to_all(send_rows, "expert", split_axis=0, concat_axis=1, tiled=True)
    gate_pre = jnp.einsum("ensi,eif->ensf", received, gate_full, preferred_element_type=jnp.float32)
    up_pre = jnp.einsum("ensi,eif->ensf", received, up_full, preferred_element_type=jnp.float32)
    hidden = (jax.nn.silu(gate_pre) * up_pre).astype(jnp.bfloat16)
    result = jnp.einsum(
        "ensf,efi->ensi", hidden, down_full, preferred_element_type=jnp.float32
    ).astype(jnp.bfloat16)
    returned = lax.all_to_all(result, "expert", split_axis=1, concat_axis=0, tiled=True)
    zero_row = jnp.zeros((1, model_width), jnp.bfloat16)
    expert_vals = jnp.concatenate([returned.reshape(-1, model_width), zero_row], axis=0)[
        destination
    ].astype(jnp.float32)
    flat_routes = routes.reshape(-1)
    copy_rows = jnp.repeat(normed_two.reshape(-1, model_width), 2, axis=0)
    const_wide = const_full.astype(jnp.float32)
    is_copy = (flat_routes == EXPERTS + 1)[:, None]
    first_const = (flat_routes == EXPERTS + 2).astype(jnp.float32)[:, None]
    second_const = (flat_routes == EXPERTS + 3).astype(jnp.float32)[:, None]
    entry_vals = (
        expert_vals
        + jnp.where(is_copy, copy_rows, 0.0)
        + first_const * const_wide[:, 0][None, :]
        + second_const * const_wide[:, 1][None, :]
    )
    entry_vals = entry_vals.reshape(seq_count, pos_count, 2, model_width)
    layer_out = middle + jnp.sum(gate_probs[..., None] * entry_vals, axis=2)
    grad_mixed = out_cotangent.astype(jnp.float32)
    grad_gates = jnp.sum(grad_mixed[:, :, None, :] * entry_vals, axis=-1)
    grad_chosen = gate_probs * (
        grad_gates - jnp.sum(gate_probs * grad_gates, axis=-1, keepdims=True)
    )
    choice_ids = jnp.arange(EXPERTS + 4, dtype=jnp.int32)
    prior_logits_gradient = jnp.sum(
        (routes[..., None] == choice_ids).astype(jnp.float32) * grad_chosen[..., None], axis=2
    )
    grad_entries = (gate_probs[..., None] * grad_mixed[:, :, None, :]).reshape(-1, model_width)
    send_grads = (
        jnp.zeros((EXPERTS * slot_count + 1, model_width), jnp.bfloat16)
        .at[destination]
        .set(grad_entries.astype(jnp.bfloat16))[:-1]
        .reshape(EXPERTS, 1, slot_count, model_width)
    )
    owner_grads = lax.all_to_all(send_grads, "expert", split_axis=0, concat_axis=1, tiled=True)
    sigmoid_gate = jax.nn.sigmoid(gate_pre)
    silu_gate = gate_pre * sigmoid_gate
    hidden_back = (silu_gate * up_pre).astype(jnp.bfloat16)
    grad_hidden = jnp.einsum(
        "ensd,efd->ensf", owner_grads, down_full, preferred_element_type=jnp.float32
    )
    grad_gate_pre = (
        grad_hidden * up_pre * sigmoid_gate * (1.0 + gate_pre * (1.0 - sigmoid_gate))
    ).astype(jnp.bfloat16)
    grad_up_pre = (grad_hidden * silu_gate).astype(jnp.bfloat16)
    down_part = jnp.einsum(
        "ensf,ensd->efd", hidden_back, owner_grads, preferred_element_type=jnp.float32
    )
    gate_part = jnp.einsum(
        "ensi,ensf->eif", received, grad_gate_pre, preferred_element_type=jnp.float32
    )
    up_part = jnp.einsum(
        "ensi,ensf->eif", received, grad_up_pre, preferred_element_type=jnp.float32
    )
    grad_rows = (
        jnp.einsum("ensf,eif->ensi", grad_gate_pre, gate_full, preferred_element_type=jnp.float32)
        + jnp.einsum("ensf,eif->ensi", grad_up_pre, up_full, preferred_element_type=jnp.float32)
    ).astype(jnp.bfloat16)
    rows_back = lax.all_to_all(grad_rows, "expert", split_axis=1, concat_axis=0, tiled=True)
    gate_grad, up_grad, down_grad = (
        lax.psum_scatter(
            gate_part.astype(jnp.bfloat16), "shard", scatter_dimension=1, tiled=True
        ).astype(jnp.float32),
        lax.psum_scatter(
            up_part.astype(jnp.bfloat16), "shard", scatter_dimension=1, tiled=True
        ).astype(jnp.float32),
        lax.psum_scatter(
            down_part.astype(jnp.bfloat16), "shard", scatter_dimension=1, tiled=True
        ).astype(jnp.float32),
    )
    grad_row_entries = jnp.concatenate([rows_back.reshape(-1, model_width), zero_row], axis=0)[
        destination
    ].astype(jnp.float32)
    grad_copy = jnp.where(is_copy, grad_entries, 0.0)
    router_widened = router_weight_wide.astype(jnp.float32)
    grad_normed_two = jnp.sum(
        (grad_row_entries + grad_copy).reshape(seq_count, pos_count, 2, model_width), axis=2
    ) + jnp.einsum(
        "hwk,ok->hwo", prior_logits_gradient, router_widened, precision=lax.Precision.HIGHEST
    )
    router_part = jnp.einsum(
        "vrx,vrb->xb",
        normalized_narrow.astype(jnp.float32),
        prior_logits_gradient,
        precision=lax.Precision.HIGHEST,
    )
    const_part = jnp.stack(
        [jnp.sum(first_const * grad_entries, axis=0), jnp.sum(second_const * grad_entries, axis=0)],
        axis=-1,
    )
    moe_gain_part = jnp.sum(grad_normed_two * scaled_two, axis=(0, 1))
    grad_middle = grad_mixed + rms_back(grad_normed_two * moe_gain_wide, middle, inverse_two)
    gradient_projected = grad_middle.astype(jnp.bfloat16)
    output_part = jnp.einsum(
        "vrx,vrb->xb",
        attention_output_narrow,
        gradient_projected,
        preferred_element_type=jnp.float32,
    )
    grad_attended = jnp.einsum(
        "hwk,ok->hwo", gradient_projected, output_weight_wide, preferred_element_type=jnp.float32
    ).astype(jnp.bfloat16)
    delta_rows = jnp.sum(
        (grad_attended.astype(jnp.float32) * attention_output).reshape(
            seq_count, pos_count, HEADS, -1
        ),
        axis=-1,
    )
    delta_sum = jnp.transpose(delta_rows, (0, 2, 1))

    def backward_one(packed):
        return attend_backward(
            packed[0],
            packed[1],
            packed[2],
            packed[3],
            packed[4],
            packed[5],
            packed[6],
            offset,
            block_count,
            width_block,
        )

    grad_query_rot, grad_keys_all, grad_values_all = lax.map(
        backward_one,
        (query_rot, keys_all, values_all, segment_ids, log_total, delta_sum, grad_attended),
    )
    grad_keys, grad_values = (
        lax.psum_scatter(
            grad_keys_all.astype(jnp.bfloat16), "expert", scatter_dimension=1, tiled=True
        ).astype(jnp.float32),
        lax.psum_scatter(
            grad_values_all.astype(jnp.bfloat16), "expert", scatter_dimension=1, tiled=True
        ).astype(jnp.float32),
    )
    gradient_query_unrotated = rotary(grad_query_rot, positions, -1.0).astype(jnp.bfloat16)
    gradient_key_unrotated = rotary(grad_keys, positions, -1.0).astype(jnp.bfloat16)
    gradient_value_narrow = grad_values.astype(jnp.bfloat16)
    query_part = jnp.einsum(
        "vrx,vrb->xb",
        normalized_first,
        gradient_query_unrotated,
        preferred_element_type=jnp.float32,
    )
    key_part = jnp.einsum(
        "vrx,vrb->xb", normalized_first, gradient_key_unrotated, preferred_element_type=jnp.float32
    )
    value_part = jnp.einsum(
        "vrx,vrb->xb", normalized_first, gradient_value_narrow, preferred_element_type=jnp.float32
    )
    grad_normed_one = jnp.einsum(
        "hwk,ok->hwo",
        gradient_query_unrotated,
        query_weight_wide,
        preferred_element_type=jnp.float32,
    )
    grad_normed_one = grad_normed_one + jnp.einsum(
        "hwk,ok->hwo", gradient_key_unrotated, key_weight_wide, preferred_element_type=jnp.float32
    )
    grad_normed_one = grad_normed_one + jnp.einsum(
        "hwk,ok->hwo", gradient_value_narrow, value_weight_wide, preferred_element_type=jnp.float32
    )
    attn_gain_part = jnp.sum(grad_normed_one * scaled_one, axis=(0, 1))
    tokens_grad = grad_middle + rms_back(grad_normed_one * attn_gain_wide, tokens_wide, inverse_one)
    layer_parts = (
        lax.psum_scatter(
            query_part.astype(jnp.bfloat16), "shard", scatter_dimension=0, tiled=True
        ).astype(jnp.float32),
        lax.psum_scatter(
            key_part.astype(jnp.bfloat16), "shard", scatter_dimension=0, tiled=True
        ).astype(jnp.float32),
        lax.psum_scatter(
            value_part.astype(jnp.bfloat16), "shard", scatter_dimension=0, tiled=True
        ).astype(jnp.float32),
        lax.psum_scatter(
            output_part.astype(jnp.bfloat16), "shard", scatter_dimension=0, tiled=True
        ).astype(jnp.float32),
        lax.psum_scatter(
            router_part.astype(jnp.bfloat16), "shard", scatter_dimension=0, tiled=True
        ).astype(jnp.float32),
        lax.psum_scatter(
            const_part.astype(jnp.bfloat16), "shard", scatter_dimension=0, tiled=True
        ).astype(jnp.float32),
        lax.psum_scatter(
            attn_gain_part.astype(jnp.bfloat16), "shard", scatter_dimension=0, tiled=True
        ).astype(jnp.float32),
        lax.psum_scatter(
            moe_gain_part.astype(jnp.bfloat16), "shard", scatter_dimension=0, tiled=True
        ).astype(jnp.float32),
    )
    layer_grads = (
        lax.psum(layer_parts[0].astype(jnp.bfloat16), "expert").astype(jnp.float32),
        lax.psum(layer_parts[1].astype(jnp.bfloat16), "expert").astype(jnp.float32),
        lax.psum(layer_parts[2].astype(jnp.bfloat16), "expert").astype(jnp.float32),
        lax.psum(layer_parts[3].astype(jnp.bfloat16), "expert").astype(jnp.float32),
        lax.psum(layer_parts[4].astype(jnp.bfloat16), "expert").astype(jnp.float32),
        lax.psum(layer_parts[5].astype(jnp.bfloat16), "expert").astype(jnp.float32),
        lax.psum(layer_parts[6].astype(jnp.bfloat16), "expert").astype(jnp.float32),
        lax.psum(layer_parts[7].astype(jnp.bfloat16), "expert").astype(jnp.float32),
    )
    return (
        layer_out.astype(jnp.bfloat16),
        tokens_grad,
        prior_logits_gradient,
        layer_grads[0],
        layer_grads[1],
        layer_grads[2],
        layer_grads[3],
        layer_grads[4],
        layer_grads[5],
        layer_grads[6],
        layer_grads[7],
        gate_grad,
        up_grad,
        down_grad,
    )


RING = 4
PAIR = 2
LOCAL = 4
META = 16


def z_pairs(step):
    lines = PAIR * PAIR
    return [
        (z * lines + rest, (z + step) % RING * lines + rest)
        for z in range(RING)
        for rest in range(lines)
    ]


def along_z(values, step):
    return lax.ppermute(values, "shard", z_pairs(step))


def across_y(values):
    return lax.ppermute(values, "shard", [(s, s ^ PAIR) for s in range(RING * PAIR * PAIR)])


def across_core(values):
    return lax.ppermute(values, "shard", [(s, s ^ 1) for s in range(RING * PAIR * PAIR)])


def across_x(values):
    return lax.ppermute(values, "expert", [(0, 1), (1, 0)])


def together(*values):
    return lax.optimization_barrier(values)


def gather_rows(own):
    ring, crossed = [own], []
    for _ in range(RING - 1):
        following, other = together(along_z(ring[-1], 1), across_x(ring[-1]))
        ring.append(following)
        crossed.append(other)
    return ring + crossed + [across_x(ring[-1])]


def add_all(*values):
    return sum(value.astype(jnp.float32) for value in values)


def reduce_rows(parts, beside):
    other, beside = together(across_x(parts[2 * RING - 1]), beside)
    total = add_all(parts[RING - 1], other)
    for step in reversed(range(RING - 1)):
        passed, other = together(
            along_z(total.astype(jnp.bfloat16), -1), across_x(parts[RING + step])
        )
        total = add_all(parts[step], passed, other)
    return total, beside


def reduce_packed(part, z_place, y_place, core_place):
    rows, width = part.shape
    depth = rows // (RING * PAIR * PAIR)
    part = part.reshape(RING, PAIR, PAIR, depth, width)
    other = jnp.where(core_place == 0, part[:, :, 1], part[:, :, 0]).astype(jnp.bfloat16)
    mine = jnp.where(core_place == 0, part[:, :, 0], part[:, :, 1])
    both = add_low(mine, across_core(other))
    total = None
    for step in reversed(range(RING)):
        block = lax.dynamic_index_in_dim(
            both, lax.rem(z_place - step + RING, RING), 0, keepdims=False
        )
        other = across_y(jnp.where(y_place == 0, block[1], block[0]))
        mine = jnp.where(y_place == 0, block[0], block[1])
        if total is None:
            here = add_all(mine, other)
        else:
            passed, other = together(along_z(total, -1), other)
            here = add_all(mine, passed, other)
        total = here.astype(jnp.bfloat16)
    return add_all(total, across_x(total))


def meta_rows(rows, width):
    filled = jnp.concatenate(rows, axis=-1).reshape(len(rows) // 2, -1)
    return jnp.pad(filled, ((0, META - filled.shape[0]), (0, width - filled.shape[1]))).astype(
        jnp.bfloat16
    )


def dot_rows(left, right):
    return lax.dot_general(left, right, (((1,), (0,)), ((), ())), preferred_element_type=jnp.float32)


def dot_wide(left, right):
    return lax.dot_general(left, right, (((1,), (1,)), ((), ())), preferred_element_type=jnp.float32)


def dot_tall(left, right):
    return lax.dot_general(left, right, (((0,), (0,)), ((), ())), preferred_element_type=jnp.float32)


def owner_index(place, step, side, core):
    return (
        lax.rem(place[1] - step + RING, RING) * (PAIR * PAIR)
        + (place[2] ^ side) * PAIR
        + (place[3] ^ core)
    )


def prepare_kernel(place, *refs):
    block_count = RING * PAIR
    grads = refs[:block_count]
    mixed = refs[block_count : block_count + 8]
    downs = refs[block_count + 8 : block_count + 12]
    pick_ref, slot_ref, back_ref, wide_ref, down_ref = refs[block_count + 12 :]
    number = pl.program_id(0)
    rows = pick_ref.shape[2]

    @pl.when(number == 0)
    def _():
        later = lax.broadcasted_iota(jnp.int32, (rows, rows), 1)
        earlier = lax.broadcasted_iota(jnp.int32, (rows, rows), 0)
        before = jnp.where(earlier < later, 1.0, 0.0).astype(jnp.bfloat16)
        wanted = (lax.broadcasted_iota(jnp.int32, (8, rows), 0) + place[0] * LOCAL).astype(
            jnp.float32
        )
        inside = lax.broadcasted_iota(jnp.int32, (8, rows), 0) < LOCAL
        ranks = lax.broadcasted_iota(jnp.int32, (CAP, rows), 0).astype(jnp.float32)
        for block in range(block_count):
            meta = grads[block][rows : rows + META, :].astype(jnp.float32)
            first = meta[1:2, :rows]
            second = meta[1:2, rows : 2 * rows]
            named = jnp.where(((first == wanted) | (second == wanted)) & inside, 1.0, 0.0)
            rank = dot_rows(named.astype(jnp.bfloat16), before)
            pieces = []
            for expert in range(LOCAL):
                hit = (rank[expert : expert + 1] == ranks) & (named[expert : expert + 1] > 0.5)
                pieces.append(jnp.where(hit, 1.0, 0.0))
            pick = jnp.concatenate(pieces, axis=0).astype(jnp.bfloat16)
            pick_ref[block] = pick
            slot_ref[block] = dot_rows(pick, grads[block][:rows, :]).astype(jnp.bfloat16)

    half = wide_ref.shape[2] // 2
    for core in range(PAIR):
        for side in range(PAIR):
            for step in range(RING):
                piece = mixed[(core * PAIR + side) * 2 + step // 2]
                depth = piece.shape[3]
                start = pl.multiple_of(owner_index(place, step, side, core) * depth, 16)
                wide_ref[0, pl.ds(start, depth), :half] = piece[step % 2, 0, 0]
                wide_ref[0, pl.ds(start, depth), half:] = piece[step % 2, 1, 0]
            own = downs[core * PAIR + side]
            deep = own.shape[1]
            local = (place[2] ^ side) * PAIR + (place[3] ^ core)
            down_ref[0, pl.ds(pl.multiple_of(local * deep, 16), deep), :] = own[0]
    width = slot_ref.shape[2]
    mine = slot_ref[:, pl.ds(pl.multiple_of(number * CAP, CAP), CAP), :]
    back_ref[0] = dot_wide(mine.reshape(block_count * CAP, width), down_ref[0])


def expert_kernel(place, *refs):
    block_count = RING * PAIR
    tokens = refs[:block_count]
    pick_ref, wide_ref, down_ref, back_ref = refs[block_count : block_count + 4]
    rest = refs[block_count + 4 :]
    slot_ref, hidden_ref, mixed_ref = rest[:3]
    grad_refs = rest[3 : 3 + block_count]
    out_refs = rest[3 + block_count : 3 + 2 * block_count]
    out_slots, grad_slots, gate_grads = rest[3 + 2 * block_count :]
    number = pl.program_id(0)
    rows = pick_ref.shape[2]
    width = slot_ref.shape[2]
    half = wide_ref.shape[2] // 2

    @pl.when(number == 0)
    def _():
        gate_grads[...] = jnp.zeros_like(gate_grads)
        for block in range(block_count):
            slot_ref[block] = dot_rows(pick_ref[block], tokens[block][:rows, :]).astype(
                jnp.bfloat16
            )

    span = pl.ds(pl.multiple_of(number * CAP, CAP), CAP)
    mine = slot_ref[:, span, :].reshape(block_count * CAP, width)
    both = dot_rows(mine, wide_ref[0])
    gate = both[:, :half]
    up = both[:, half:]
    sigmoid = 1.0 / (1.0 + jnp.exp(-gate))
    silu = gate * sigmoid
    hidden = silu * up
    back = back_ref[0]
    expert_id = (number + place[0] * LOCAL).astype(jnp.float32)
    chances = []
    product = jnp.sum(hidden * back, axis=1, keepdims=True)
    for block in range(block_count):
        meta = tokens[block][rows : rows + META, :].astype(jnp.float32)
        first = jnp.where(meta[1:2, :rows] == expert_id, 1.0, 0.0)
        second = jnp.where(meta[1:2, rows : 2 * rows] == expert_id, 1.0, 0.0)
        pick = pick_ref[block, span, :].astype(jnp.float32)
        chance = first * meta[0:1, :rows] + second * meta[0:1, rows : 2 * rows]
        chances.append(jnp.sum(pick * chance, axis=1, keepdims=True))
        spread = jnp.sum(
            pick * product[block * CAP : (block + 1) * CAP], axis=0, keepdims=True
        )
        gate_grads[block, 0:1, :rows] += first * spread
        gate_grads[block, 0:1, rows : 2 * rows] += second * spread
    chance = jnp.concatenate(chances, axis=0)
    back = back * chance
    weighted = (hidden * chance).astype(jnp.bfloat16)
    grad_gate = back * up * sigmoid * (1.0 + gate * (1.0 - sigmoid))
    grad_up = back * silu
    mixed = jnp.concatenate([grad_gate, grad_up], axis=1).astype(jnp.bfloat16)
    hidden_ref[0] = weighted
    mixed_ref[0] = mixed
    out_part = dot_rows(weighted, down_ref[0]).astype(jnp.bfloat16)
    out_slots[:, span, :] = out_part.reshape(block_count, CAP, width)
    grad_part = dot_wide(mixed, wide_ref[0]).astype(jnp.bfloat16)
    grad_slots[:, span, :] = grad_part.reshape(block_count, CAP, width)

    @pl.when(number == LOCAL - 1)
    def _():
        for block in range(block_count):
            pick = pick_ref[block]
            grad_refs[block][:rows, :] = dot_tall(pick, grad_slots[block]).astype(jnp.bfloat16)
            grad_refs[block][rows : rows + META, :] = gate_grads[block].astype(jnp.bfloat16)
            out_refs[block][...] = dot_tall(pick, out_slots[block]).astype(jnp.bfloat16)


def weight_grad_kernel(place, *refs):
    slot_ref, back_ref, hidden_ref, mixed_ref = refs[:4]
    wide_refs = refs[4:8]
    down_refs = refs[8:12]
    wide_sum, down_sum = refs[12:]
    number = pl.program_id(0)
    block_count, _, width = slot_ref.shape
    span = pl.ds(pl.multiple_of(number * CAP, CAP), CAP)
    rows = slot_ref[:, span, :].reshape(block_count * CAP, width)
    wide_sum[...] = dot_tall(rows, mixed_ref[0])
    grads = back_ref[:, span, :].reshape(block_count * CAP, width)
    down_sum[...] = dot_tall(hidden_ref[0], grads)
    half = wide_sum.shape[1] // 2
    for core in range(PAIR):
        for side in range(PAIR):
            piece = wide_refs[core * PAIR + side]
            depth = piece.shape[3]
            for step in range(RING):
                start = pl.multiple_of(owner_index(place, step, side, core) * depth, 16)
                part = wide_sum[pl.ds(start, depth), :]
                piece[step, 0, 0] = part[:, :half].astype(jnp.bfloat16)
                piece[step, 1, 0] = part[:, half:].astype(jnp.bfloat16)
            own = down_refs[core * PAIR + side]
            deep = own.shape[1]
            local = (place[2] ^ side) * PAIR + (place[3] ^ core)
            part = down_sum[pl.ds(pl.multiple_of(local * deep, 16), deep), :]
            own[0] = part.astype(jnp.bfloat16)


def whole(shape):
    return pl.BlockSpec(shape, lambda number, place: (0,) * len(shape))


def by_expert(shape, axis=0):
    return pl.BlockSpec(
        shape,
        lambda number, place: tuple(number if d == axis else 0 for d in range(len(shape))),
    )


def prepare_experts(place, grads, mixed, downs):
    padded, width = grads[0].shape
    rows = padded - META
    blocks = len(grads)
    _, _, local, depth, span = mixed[0].shape
    deep = downs[0].shape[1]
    model = depth * RING * PAIR * PAIR
    slots = blocks * CAP
    shapes = [
        ((blocks, local * CAP, rows), jnp.bfloat16),
        ((blocks, local * CAP, width), jnp.bfloat16),
        ((local, slots, span), jnp.float32),
        ((local, model, 2 * span), jnp.bfloat16),
        ((local, deep * PAIR * PAIR, width), jnp.bfloat16),
    ]
    return pl.pallas_call(
        prepare_kernel,
        name="prepare_experts",
        out_shape=[jax.ShapeDtypeStruct(s, d) for s, d in shapes],
        grid_spec=pltpu.PrefetchScalarGridSpec(
            num_scalar_prefetch=1,
            grid=(local,),
            in_specs=[whole(g.shape) for g in grads]
            + [by_expert((2, 2, 1, depth, span), 2)] * 8
            + [by_expert((1, deep, width))] * 4,
            out_specs=[
                whole(shapes[0][0]),
                whole(shapes[1][0]),
                by_expert((1, slots, span)),
                by_expert((1, model, 2 * span)),
                by_expert((1, deep * PAIR * PAIR, width)),
            ],
        ),
    )(place, *grads, *mixed, *downs)


def run_experts(place, tokens, pick, wide, down, back):
    padded, width = tokens[0].shape
    rows = padded - META
    blocks = len(tokens)
    local, model, span2 = wide.shape
    span = span2 // 2
    slots = blocks * CAP
    shapes = [
        ((blocks, local * CAP, width), jnp.bfloat16),
        ((local, slots, span), jnp.bfloat16),
        ((local, slots, span2), jnp.bfloat16),
    ]
    shapes = shapes + [((padded, width), jnp.bfloat16)] * blocks
    shapes = shapes + [((rows, width), jnp.bfloat16)] * blocks
    results = pl.pallas_call(
        expert_kernel,
        name="run_experts",
        out_shape=[jax.ShapeDtypeStruct(s, d) for s, d in shapes],
        grid_spec=pltpu.PrefetchScalarGridSpec(
            num_scalar_prefetch=1,
            grid=(local,),
            in_specs=[whole(t.shape) for t in tokens]
            + [
                whole(pick.shape),
                by_expert((1, model, span2)),
                by_expert((1, span, width)),
                by_expert((1, slots, span)),
            ],
            out_specs=[
                whole(shapes[0][0]),
                by_expert((1, slots, span)),
                by_expert((1, slots, span2)),
            ]
            + [whole(s) for s, _ in shapes[3:]],
            scratch_shapes=[
                pltpu.VMEM((blocks, local * CAP, width), jnp.bfloat16),
                pltpu.VMEM((blocks, local * CAP, width), jnp.bfloat16),
                pltpu.VMEM((blocks, META, width), jnp.float32),
            ],
        ),
    )(place, *tokens, pick, wide, down, back)
    return results[:3], results[3 : 3 + blocks], results[3 + blocks :]


def weight_grads(place, slots, backs, hidden, mixed):
    blocks, total, width = slots.shape
    local, rows, span = hidden.shape
    depth = width // (RING * PAIR * PAIR)
    deep = span // (PAIR * PAIR)
    wide_shape = (RING, 2, local, depth, span)
    down_shape = (local, deep, width)
    results = pl.pallas_call(
        weight_grad_kernel,
        name="weight_grads",
        out_shape=[jax.ShapeDtypeStruct(wide_shape, jnp.bfloat16)] * 4
        + [jax.ShapeDtypeStruct(down_shape, jnp.bfloat16)] * 4,
        grid_spec=pltpu.PrefetchScalarGridSpec(
            num_scalar_prefetch=1,
            grid=(local,),
            in_specs=[
                whole(slots.shape),
                whole(backs.shape),
                by_expert((1, rows, span)),
                by_expert((1, rows, 2 * span)),
            ],
            out_specs=[by_expert((RING, 2, 1, depth, span), 2)] * 4
            + [by_expert((1, deep, width))] * 4,
            scratch_shapes=[
                pltpu.VMEM((width, 2 * span), jnp.float32),
                pltpu.VMEM((span, width), jnp.float32),
            ],
        ),
    )(place, slots, backs, hidden, mixed)
    return results[:4], results[4:]


def add_low(left, right):
    return (left.astype(jnp.float32) + right.astype(jnp.float32)).astype(jnp.bfloat16)


def weight_pieces(gate_weight, up_weight, z_place):
    span = gate_weight.shape[2] // RING
    pieces = []
    for step in range(RING):
        start = lax.rem(z_place + step, RING) * span
        pieces.append(
            jnp.stack(
                [
                    lax.dynamic_slice_in_dim(gate_weight, start, span, 2),
                    lax.dynamic_slice_in_dim(up_weight, start, span, 2),
                ]
            )
        )
    return pieces


def place_columns(parts, z_place):
    columns = []
    for column in range(RING):
        choice = lax.rem(column - z_place + RING, RING)
        chosen = parts[0]
        for step in range(1, RING):
            chosen = jnp.where(choice == step, parts[step], chosen)
        columns.append(chosen)
    both = jnp.concatenate(columns, axis=-1).astype(jnp.float32)
    return both[0], both[1]


def body_split(
    tokens,
    segment_ids,
    routes,
    earlier_logits,
    out_cotangent,
    query_weight,
    key_weight,
    value_weight,
    output_weight,
    router_weight,
    const_vectors,
    attn_gain,
    moe_gain,
    gate_weight,
    up_weight,
    down_weight,
):
    _, pos_count, model_width = tokens.shape
    tokens, segment_row, routes = tokens[0], segment_ids[0], routes[0]
    earlier_logits, cotangent_low = earlier_logits[0], out_cotangent[0]
    x_place = lax.axis_index("expert")
    shard_place = lax.axis_index("shard")
    z_place = shard_place // (PAIR * PAIR)
    y_place = lax.rem(shard_place // PAIR, PAIR)
    core_place = lax.rem(shard_place, PAIR)
    order = jnp.arange(4, dtype=jnp.int32)
    place = jnp.where(
        order == 0,
        x_place,
        jnp.where(order == 1, z_place, jnp.where(order == 2, y_place, core_place)),
    ).astype(jnp.int32)
    choices = router_weight.shape[1]
    consts = const_vectors.shape[1]
    small_count = choices + consts + 2
    small = jnp.concatenate(
        [router_weight, const_vectors, attn_gain[:, None], moe_gain[:, None]], axis=1
    )
    small = jnp.pad(small, ((0, 0), (0, 128 - small_count)))
    packed = jnp.concatenate(
        [query_weight, key_weight, value_weight, output_weight, small], axis=1
    )
    routes_low = routes.astype(jnp.bfloat16)
    route_rows = [routes_low[:, 0], routes_low[:, 1]]
    zero_rows = [jnp.zeros_like(route_rows[0])] * 2
    cotangent_blocks = gather_rows(
        jnp.concatenate([cotangent_low, meta_rows(zero_rows + route_rows, model_width)], axis=0)
    )
    gathered = lax.all_gather(packed, "shard", axis=0, tiled=True)
    other_tokens = across_x(tokens)
    gathered, other_tokens, cotangent_blocks, gate_weight, up_weight, down_weight = together(
        gathered, other_tokens, cotangent_blocks, gate_weight, up_weight, down_weight
    )
    pieces = weight_pieces(gate_weight, up_weight, z_place)
    moved = [along_z(pieces[step], step) for step in range(1, RING)]
    down_other = across_y(down_weight)

    joint = 3 * model_width
    joint_weight = gathered[:, :joint]
    output_wide = gathered[:, joint : joint + model_width]
    tail = gathered[:, joint + model_width :].astype(jnp.float32)
    router_low = gathered[:, joint + model_width : joint + model_width + choices]
    router_wide = tail[:, :choices]
    const_wide = tail[:, choices : choices + consts].T
    gain_attn = tail[:, choices + consts]
    gain_moe = tail[:, choices + consts + 1]

    offset = x_place * pos_count
    width_block = math.gcd(pos_count, 128)
    block_count = (x_place + 1) * (pos_count // width_block)
    first_tokens = jnp.where(x_place == 0, tokens, other_tokens)
    second_tokens = jnp.where(x_place == 0, other_tokens, tokens)
    all_wide = jnp.concatenate([first_tokens, second_tokens], axis=0).astype(jnp.float32)
    scaled_all, _ = rms_parts(all_wide)
    normed_all = (scaled_all * gain_attn).astype(jnp.bfloat16)
    tokens_wide = tokens.astype(jnp.float32)
    scaled_one, inverse_one = rms_parts(tokens_wide)
    normed_own = (scaled_one * gain_attn).astype(jnp.bfloat16)
    positions = offset + jnp.arange(pos_count, dtype=jnp.int32)
    all_positions = jnp.arange(PAIR * pos_count, dtype=jnp.int32)
    query_rot = rotary(dot_rows(normed_own, joint_weight[:, :model_width]), positions, 1.0)
    query_rot = query_rot.astype(jnp.bfloat16)
    key_value = dot_rows(normed_all, joint_weight[:, model_width:])
    keys_all = rotary(key_value[:, :model_width], all_positions, 1.0).astype(jnp.bfloat16)
    values_all = key_value[:, model_width:].astype(jnp.bfloat16)
    query_rot, keys_all, values_all, moved[0] = together(query_rot, keys_all, values_all, moved[0])
    own_first = jnp.stack([pieces[0], moved[0]])
    other_first = across_y(own_first)
    attention_output, log_total = attend_forward(
        query_rot, keys_all, values_all, segment_row, offset, block_count, width_block
    )
    attention_output, moved[1], down_other = together(attention_output, moved[1], down_other)
    attention_low = attention_output.astype(jnp.bfloat16)
    middle = tokens_wide + dot_rows(attention_low, output_wide)
    scaled_two, inverse_two = rms_parts(middle)
    normed_two = scaled_two * gain_moe
    normed_low = normed_two.astype(jnp.bfloat16)
    router_logits = dot_rows(normed_low, router_low) + earlier_logits
    choice_ids = jnp.arange(choices, dtype=jnp.int32)
    one_hot = (routes[..., None] == choice_ids).astype(jnp.float32)
    chosen = jnp.sum(one_hot * router_logits[:, None, :], axis=-1)
    gate_probs = jax.nn.softmax(chosen, axis=-1)
    probs_low = gate_probs.astype(jnp.bfloat16)
    payload = jnp.concatenate(
        [
            normed_low,
            meta_rows([probs_low[:, 0], probs_low[:, 1]] + route_rows, model_width),
        ],
        axis=0,
    )
    payload, moved[2], other_first = together(payload, moved[2], other_first)
    token_blocks = gather_rows(payload)
    own_last = jnp.stack([moved[1], moved[2]])
    other_last = across_y(own_last)
    wide_pieces = [own_first, own_last, other_first, other_last]
    wide_pieces = wide_pieces + [across_core(piece) for piece in wide_pieces]
    down_pieces = [down_weight, down_other, across_core(down_weight), across_core(down_other)]
    pick, back_slots, back_hidden, wide_full, down_full = prepare_experts(
        place, cotangent_blocks, wide_pieces, down_pieces
    )
    (token_slots, hidden, mixed), grad_parts, out_parts = run_experts(
        place, token_blocks, pick, wide_full, down_full, back_hidden
    )
    wide_grads, down_grads = weight_grads(place, token_slots, back_slots, hidden, mixed)
    grad_total, (wide_grads, down_grads) = reduce_rows(grad_parts, (wide_grads, down_grads))
    near = add_low(wide_grads[0], across_core(wide_grads[2]))
    far = add_low(wide_grads[1], across_core(wide_grads[3]))
    down_near = add_low(down_grads[0], across_core(down_grads[2]))
    down_far = add_low(down_grads[1], across_core(down_grads[3]))
    grad_total, near, far, down_near, down_far, out_parts = together(
        grad_total, near, far, down_near, down_far, out_parts
    )
    out_other = across_x(out_parts[7])
    far_last = across_y(far[2:])

    cotangent = cotangent_low.astype(jnp.float32)
    copies = jnp.sum(one_hot[..., EXPERTS + 1] * gate_probs, axis=-1)[:, None]
    const_probs = jnp.sum(one_hot[..., EXPERTS + 2 :] * gate_probs[..., None], axis=1)
    copy_dot = jnp.sum(cotangent * normed_two, axis=-1)
    const_dot = jnp.stack(
        [jnp.sum(cotangent * const_wide[i], axis=-1) for i in range(consts)], axis=-1
    )
    grad_rows = grad_total[:pos_count]
    expert_dot = jnp.stack(
        [grad_total[pos_count, i * pos_count : (i + 1) * pos_count] for i in range(2)], axis=-1
    )
    grad_gates = (
        expert_dot
        + one_hot[..., EXPERTS + 1] * copy_dot[:, None]
        + jnp.sum(one_hot[..., EXPERTS + 2 :] * const_dot[:, None, :], axis=-1)
    )
    grad_chosen = gate_probs * (
        grad_gates - jnp.sum(gate_probs * grad_gates, axis=-1, keepdims=True)
    )
    prior_logits_gradient = jnp.sum(one_hot * grad_chosen[..., None], axis=1)
    highest = lax.Precision.HIGHEST
    grad_normed_two = (
        grad_rows
        + copies * cotangent
        + jnp.einsum("wk,ok->wo", prior_logits_gradient, router_wide, precision=highest)
    )
    router_part = jnp.einsum(
        "rx,rb->xb", normed_low.astype(jnp.float32), prior_logits_gradient, precision=highest
    )
    const_part = jnp.einsum("rx,rb->xb", cotangent, const_probs, precision=highest)
    moe_gain_part = jnp.sum(grad_normed_two * scaled_two, axis=0)
    grad_middle = cotangent + rms_back(grad_normed_two * gain_moe, middle, inverse_two)
    grad_projected = grad_middle.astype(jnp.bfloat16)
    output_part = dot_tall(attention_low, grad_projected).astype(jnp.bfloat16)
    grad_attended = dot_wide(grad_projected, output_wide).astype(jnp.bfloat16)
    delta_sum = jnp.transpose(
        jnp.sum(
            (grad_attended.astype(jnp.float32) * attention_output).reshape(pos_count, HEADS, -1),
            axis=-1,
        )
    )
    grad_attended, delta_sum, output_part, out_other, far_last = together(
        grad_attended, delta_sum, output_part, out_other, far_last
    )
    out_total = add_low(out_parts[3], out_other)
    out_passed, out_other = along_z(out_total, -1), across_x(out_parts[6])
    far_first = across_y(far[:2])
    mine_last = add_low(near[2:], far_last)
    grad_query_rot, grad_keys, grad_values = attend_backward(
        query_rot,
        keys_all,
        values_all,
        segment_row,
        log_total,
        delta_sum,
        grad_attended,
        offset,
        block_count,
        width_block,
    )
    moved_third = along_z(mine_last[1], -3)
    grad_query_rot, grad_keys, grad_values, out_passed, out_other, far_first, moved_third = (
        together(
            grad_query_rot, grad_keys, grad_values, out_passed, out_other, far_first, moved_third
        )
    )
    out_total = add_all(out_parts[2], out_passed, out_other).astype(jnp.bfloat16)
    out_passed, out_other = along_z(out_total, -1), across_x(out_parts[5])
    down_other = across_y(down_far)
    mine_first = add_low(near[:2], far_first)
    moved_first = along_z(mine_first[1], -1)
    grad_query = rotary(grad_query_rot, positions, -1.0).astype(jnp.bfloat16)
    grad_key = rotary(grad_keys, all_positions, -1.0).astype(jnp.bfloat16)
    grad_value = grad_values.astype(jnp.bfloat16)
    grad_key_value = jnp.concatenate([grad_key, grad_value], axis=1)
    grad_normed_all = dot_wide(grad_key_value, joint_weight[:, model_width:])
    grad_normed_one = dot_wide(grad_query, joint_weight[:, :model_width])
    attn_gain_part = jnp.sum(grad_normed_all * scaled_all, axis=0) + jnp.sum(
        grad_normed_one * scaled_one, axis=0
    )
    first_grad = grad_normed_all[:pos_count]
    grad_normed_one = grad_normed_one + jnp.where(
        x_place == 0, first_grad, grad_normed_all[pos_count:]
    )
    first_grad = first_grad.astype(jnp.bfloat16)
    (
        grad_query,
        grad_key_value,
        grad_normed_one,
        first_grad,
        attn_gain_part,
        out_passed,
        out_other,
        down_other,
        moved_first,
    ) = together(
        grad_query,
        grad_key_value,
        grad_normed_one,
        first_grad,
        attn_gain_part,
        out_passed,
        out_other,
        down_other,
        moved_first,
    )
    out_total = add_all(out_parts[1], out_passed, out_other).astype(jnp.bfloat16)
    out_passed, out_other = along_z(out_total, -1), across_x(out_parts[4])
    moved_second = along_z(mine_last[0], -2)
    down_grad = add_all(down_near, down_other)
    query_part = dot_tall(normed_own, grad_query).astype(jnp.bfloat16)
    key_value_part = dot_tall(normed_all, grad_key_value).astype(jnp.bfloat16)
    small_part = jnp.concatenate(
        [router_part, const_part, attn_gain_part[:, None], moe_gain_part[:, None]], axis=1
    ).astype(jnp.bfloat16)
    small_part = jnp.pad(small_part, ((0, 0), (0, 128 - small_count)))
    packed_part = jnp.concatenate([query_part, key_value_part, output_part, small_part], axis=1)
    packed_part, out_passed, out_other, first_grad = together(
        packed_part, out_passed, out_other, first_grad
    )
    shared = lax.ppermute(first_grad, "expert", [(1, 0)])
    packed_grad = reduce_packed(packed_part, z_place, y_place, core_place)
    const_rows = sum(const_probs[:, i : i + 1] * const_wide[i : i + 1] for i in range(consts))
    layer_out = (
        middle
        + add_all(out_parts[0], out_passed, out_other)
        + copies * normed_two
        + const_rows
    )
    grad_normed_one = grad_normed_one + shared.astype(jnp.float32)
    tokens_grad = grad_middle + rms_back(grad_normed_one * gain_attn, tokens_wide, inverse_one)
    gate_grad, up_grad = place_columns(
        [mine_first[0], moved_first, moved_second, moved_third], z_place
    )
    output_grad = packed_grad[:, joint : joint + model_width]
    small_grad = packed_grad[:, joint + model_width :]
    return (
        layer_out.astype(jnp.bfloat16)[None],
        tokens_grad[None],
        prior_logits_gradient[None],
        packed_grad[:, :model_width],
        packed_grad[:, model_width : 2 * model_width],
        packed_grad[:, 2 * model_width : joint],
        output_grad,
        small_grad[:, :choices],
        small_grad[:, choices : choices + consts],
        small_grad[:, choices + consts],
        small_grad[:, choices + consts + 1],
        gate_grad,
        up_grad,
        down_grad,
    )


def solution(mesh):
    in_specs = (
        P("shard", "expert", None),
        P("shard", None),
        P("shard", "expert", None),
        P("shard", "expert", None),
        P("shard", "expert", None),
        P("shard", None),
        P("shard", None),
        P("shard", None),
        P("shard", None),
        P("shard", None),
        P("shard", None),
        P("shard"),
        P("shard"),
        P("expert", "shard", None),
        P("expert", "shard", None),
        P("expert", "shard", None),
    )
    out_specs = (
        P("shard", "expert", None),
        P("shard", "expert", None),
        P("shard", "expert", None),
        P("shard", None),
        P("shard", None),
        P("shard", None),
        P("shard", None),
        P("shard", None),
        P("shard", None),
        P("shard"),
        P("shard"),
        P("expert", "shard", None),
        P("expert", "shard", None),
        P("expert", "shard", None),
    )
    divided = mesh.shape["expert"] == PAIR and mesh.shape["shard"] == RING * PAIR * PAIR
    chosen = body_split if divided else body
    return jax.shard_map(chosen, mesh=mesh, in_specs=in_specs, out_specs=out_specs, check_vma=False)
```

```python
import math

import jax
import jax.numpy as jnp
from jax import lax
from jax.experimental import pallas as pl
from jax.experimental.pallas import tpu as pltpu
from jax.sharding import PartitionSpec as P

HEADS = 12
EXPERTS = 8
CAP = 64


norm_eps = 1e-06
masked_fill = -1e30


def rotary(values, positions, direction):
    dims_in = values.shape
    heads_view = values.reshape(dims_in[:-1] + (HEADS, dims_in[-1] // HEADS))
    half_size = heads_view.shape[-1] // 2
    frequency = jnp.exp(
        jnp.arange(half_size, dtype=jnp.float32) * (-2.0 * math.log(10000.0) / (2 * half_size))
    )
    angles = positions.astype(jnp.float32)[:, None] * frequency[None, :]
    cosine = jnp.cos(angles)[:, None, :]
    sine_part = direction * jnp.sin(angles)[:, None, :]
    first_half = heads_view[..., :half_size]
    second_half = heads_view[..., half_size:]
    turned = jnp.concatenate(
        [
            first_half * cosine - second_half * sine_part,
            second_half * cosine + first_half * sine_part,
        ],
        axis=-1,
    )
    return turned.reshape(dims_in)


def rms_parts(values):
    inverse = lax.rsqrt(jnp.mean(values * values, axis=-1, keepdims=True) + norm_eps)
    return (values * inverse, inverse)


def rms_back(grad_scaled, values, inverse):
    inner_mean = jnp.mean(grad_scaled * values, axis=-1, keepdims=True)
    return inverse * grad_scaled - values * inverse * inverse * inverse * inner_mean


def block_scores(query_heads, keys_all, segment_row, query_pos, query_seg, key_start, width_block):
    key_block = lax.dynamic_slice_in_dim(keys_all, key_start, width_block, 0)
    key_heads = key_block.reshape(width_block, HEADS, key_block.shape[-1] // HEADS)
    raw_scores = jnp.einsum(
        "qhd,khd->hqk", query_heads, key_heads, preferred_element_type=jnp.float32
    )
    scaled = raw_scores * key_heads.shape[-1] ** (-0.5)
    key_pos = key_start + jnp.arange(width_block, dtype=jnp.int32)
    key_seg = lax.dynamic_slice_in_dim(segment_row, key_start, width_block, 0)
    allowed = (key_pos[None, :] <= query_pos[:, None]) & (key_seg[None, :] == query_seg[:, None])
    return (scaled, allowed[None], key_heads)


def attend_forward(query_rot, keys_all, values_all, segment_row, offset, block_count, width_block):
    row_count = query_rot.shape[0]
    query_heads = query_rot.reshape(row_count, HEADS, -1)
    query_pos = offset + jnp.arange(row_count, dtype=jnp.int32)
    query_seg = lax.dynamic_slice_in_dim(segment_row, offset, row_count, 0)

    def gather_stats(number, state_pair):
        running_max, running_sum = state_pair
        scaled, allowed, key_heads = block_scores(
            query_heads,
            keys_all,
            segment_row,
            query_pos,
            query_seg,
            number * width_block,
            width_block,
        )
        masked = jnp.where(allowed, scaled, masked_fill)
        new_max = jnp.maximum(running_max, jnp.max(masked, axis=-1))
        exp_terms = jnp.where(allowed, jnp.exp(masked - new_max[..., None]), 0.0)
        return (new_max, running_sum * jnp.exp(running_max - new_max) + jnp.sum(exp_terms, axis=-1))

    start_max = jnp.full((HEADS, row_count), masked_fill, jnp.float32)
    start_sum = jnp.zeros((HEADS, row_count), jnp.float32)
    final_max, final_sum = lax.fori_loop(0, block_count, gather_stats, (start_max, start_sum))
    log_total = final_max + jnp.log(final_sum)

    def gather_output(number, running_out):
        key_start = number * width_block
        scaled, allowed, key_heads = block_scores(
            query_heads, keys_all, segment_row, query_pos, query_seg, key_start, width_block
        )
        weights = jnp.where(allowed, jnp.exp(scaled - log_total[..., None]), 0.0).astype(
            jnp.bfloat16
        )
        value_heads = lax.dynamic_slice_in_dim(values_all, key_start, width_block, 0).reshape(
            width_block, HEADS, -1
        )
        return running_out + jnp.einsum(
            "hqk,khd->qhd", weights, value_heads, preferred_element_type=jnp.float32
        )

    start_out = jnp.zeros((row_count, HEADS, query_heads.shape[-1]), jnp.float32)
    attention_output = lax.fori_loop(0, block_count, gather_output, start_out)
    return (attention_output.reshape(row_count, -1), log_total)


def attend_backward(
    query_rot,
    keys_all,
    values_all,
    segment_row,
    log_total,
    delta_sum,
    grad_low,
    offset,
    block_count,
    width_block,
):
    row_count = query_rot.shape[0]
    key_total = keys_all.shape[0]
    model_width = keys_all.shape[1]
    query_heads = query_rot.reshape(row_count, HEADS, -1)
    grad_heads = grad_low.reshape(row_count, HEADS, -1)
    query_pos = offset + jnp.arange(row_count, dtype=jnp.int32)
    query_seg = lax.dynamic_slice_in_dim(segment_row, offset, row_count, 0)
    score_scale = query_heads.shape[-1] ** (-0.5)

    def block_parts(number):
        key_start = number * width_block
        scaled, allowed, key_heads = block_scores(
            query_heads, keys_all, segment_row, query_pos, query_seg, key_start, width_block
        )
        prob_block = jnp.where(allowed, jnp.exp(scaled - log_total[..., None]), 0.0)
        value_heads = lax.dynamic_slice_in_dim(values_all, key_start, width_block, 0).reshape(
            width_block, HEADS, -1
        )
        grad_probs = jnp.einsum(
            "qhd,khd->hqk", grad_heads, value_heads, preferred_element_type=jnp.float32
        )
        grad_raw = (prob_block * (grad_probs - delta_sum[..., None]) * score_scale).astype(
            jnp.bfloat16
        )
        return (key_start, key_heads, prob_block, grad_raw)

    start_query = jnp.zeros((row_count, HEADS, query_heads.shape[-1]), jnp.float32)

    def accumulate(number, state_all):
        grad_query, grad_keys, grad_values = state_all
        key_start, key_heads, prob_block, grad_raw = block_parts(number)
        grad_query = grad_query + jnp.einsum(
            "hqk,khd->qhd", grad_raw, key_heads, preferred_element_type=jnp.float32
        )
        key_part = jnp.einsum(
            "hqk,qhd->khd", grad_raw, query_heads, preferred_element_type=jnp.float32
        )
        value_part = jnp.einsum(
            "hqk,qhd->khd",
            prob_block.astype(jnp.bfloat16),
            grad_heads,
            preferred_element_type=jnp.float32,
        )
        grad_keys = lax.dynamic_update_slice_in_dim(
            grad_keys, key_part.reshape(width_block, -1), key_start, 0
        )
        grad_values = lax.dynamic_update_slice_in_dim(
            grad_values, value_part.reshape(width_block, -1), key_start, 0
        )
        return (grad_query, grad_keys, grad_values)

    start_state = (
        start_query,
        jnp.zeros((key_total, model_width), jnp.float32),
        jnp.zeros((key_total, model_width), jnp.float32),
    )
    grad_query, grad_keys, grad_values = lax.fori_loop(0, block_count, accumulate, start_state)
    return (grad_query.reshape(row_count, -1), grad_keys, grad_values)


def body(
    tokens,
    segment_ids,
    routes,
    earlier_logits,
    out_cotangent,
    query_weight,
    key_weight,
    value_weight,
    output_weight,
    router_weight,
    const_vectors,
    attn_gain,
    moe_gain,
    gate_weight,
    up_weight,
    down_weight,
):
    (
        query_weight_wide,
        key_weight_wide,
        value_weight_wide,
        output_weight_wide,
        router_weight_wide,
        const_full,
        gain_attn,
        gain_moe,
    ) = (
        lax.all_gather(query_weight, "shard", axis=0, tiled=True),
        lax.all_gather(key_weight, "shard", axis=0, tiled=True),
        lax.all_gather(value_weight, "shard", axis=0, tiled=True),
        lax.all_gather(output_weight, "shard", axis=0, tiled=True),
        lax.all_gather(router_weight, "shard", axis=0, tiled=True),
        lax.all_gather(const_vectors, "shard", axis=0, tiled=True),
        lax.all_gather(attn_gain, "shard", axis=0, tiled=True),
        lax.all_gather(moe_gain, "shard", axis=0, tiled=True),
    )
    gate_full, up_full, down_full = (
        lax.all_gather(gate_weight, "shard", axis=1, tiled=True),
        lax.all_gather(up_weight, "shard", axis=1, tiled=True),
        lax.all_gather(down_weight, "shard", axis=1, tiled=True),
    )
    seq_count, pos_count, model_width = tokens.shape
    expert_pos = lax.axis_index("expert")
    offset = expert_pos * pos_count
    width_block = math.gcd(pos_count, 128)
    block_count = (expert_pos + 1) * (pos_count // width_block)
    positions = offset + jnp.arange(pos_count, dtype=jnp.int32)
    tokens_wide = tokens.astype(jnp.float32)
    scaled_one, inverse_one = rms_parts(tokens_wide)
    attn_gain_wide = gain_attn.astype(jnp.float32)
    normalized_first = (scaled_one * attn_gain_wide).astype(jnp.bfloat16)
    query_unrotated = jnp.einsum(
        "ibg,gv->ibv", normalized_first, query_weight_wide, preferred_element_type=jnp.float32
    )
    key_unrotated = jnp.einsum(
        "ibg,gv->ibv", normalized_first, key_weight_wide, preferred_element_type=jnp.float32
    )
    value_projected = jnp.einsum(
        "ibg,gv->ibv", normalized_first, value_weight_wide, preferred_element_type=jnp.float32
    )
    query_rot = rotary(query_unrotated, positions, 1.0).astype(jnp.bfloat16)
    key_rot = rotary(key_unrotated, positions, 1.0).astype(jnp.bfloat16)
    value_low = value_projected.astype(jnp.bfloat16)
    keys_all, values_all = (
        lax.all_gather(key_rot, "expert", axis=1, tiled=True),
        lax.all_gather(value_low, "expert", axis=1, tiled=True),
    )

    def forward_one(packed):
        return attend_forward(
            packed[0], packed[1], packed[2], packed[3], offset, block_count, width_block
        )

    attention_output, log_total = lax.map(
        forward_one, (query_rot, keys_all, values_all, segment_ids)
    )
    attention_output_narrow = attention_output.astype(jnp.bfloat16)
    projected_rows = jnp.einsum(
        "ibg,gv->ibv",
        attention_output_narrow,
        output_weight_wide,
        preferred_element_type=jnp.float32,
    )
    middle = tokens_wide + projected_rows
    scaled_two, inverse_two = rms_parts(middle)
    moe_gain_wide = gain_moe.astype(jnp.float32)
    normed_two = scaled_two * moe_gain_wide
    normalized_narrow = normed_two.astype(jnp.bfloat16)
    router_logits = (
        jnp.einsum(
            "ibg,gv->ibv", normalized_narrow, router_weight_wide, preferred_element_type=jnp.float32
        )
        + earlier_logits
    )
    chosen = jnp.take_along_axis(router_logits, routes, axis=-1)
    gate_probs = jax.nn.softmax(chosen, axis=-1)
    slot_count = seq_count * CAP
    route_entries = routes.reshape(seq_count, pos_count * 2)
    one_hot = (route_entries[..., None] == jnp.arange(EXPERTS, dtype=jnp.int32)).astype(jnp.int32)
    entry_ranks = jnp.cumsum(one_hot, axis=1) - one_hot
    slot_rank = jnp.sum(entry_ranks * one_hot, axis=-1)
    is_real = route_entries < EXPERTS
    destination = jnp.where(
        is_real,
        route_entries * slot_count
        + jnp.arange(seq_count, dtype=jnp.int32)[:, None] * CAP
        + slot_rank,
        EXPERTS * slot_count,
    ).reshape(-1)
    entry_rows = jnp.repeat(normalized_narrow.reshape(-1, model_width), 2, axis=0)
    send_rows = (
        jnp.zeros((EXPERTS * slot_count + 1, model_width), jnp.bfloat16)
        .at[destination]
        .set(entry_rows)[:-1]
        .reshape(EXPERTS, 1, slot_count, model_width)
    )
    received = lax.all_to_all(send_rows, "expert", split_axis=0, concat_axis=1, tiled=True)
    gate_pre = jnp.einsum("ensi,eif->ensf", received, gate_full, preferred_element_type=jnp.float32)
    up_pre = jnp.einsum("ensi,eif->ensf", received, up_full, preferred_element_type=jnp.float32)
    hidden = (jax.nn.silu(gate_pre) * up_pre).astype(jnp.bfloat16)
    result = jnp.einsum(
        "ensf,efi->ensi", hidden, down_full, preferred_element_type=jnp.float32
    ).astype(jnp.bfloat16)
    returned = lax.all_to_all(result, "expert", split_axis=1, concat_axis=0, tiled=True)
    zero_row = jnp.zeros((1, model_width), jnp.bfloat16)
    expert_vals = jnp.concatenate([returned.reshape(-1, model_width), zero_row], axis=0)[
        destination
    ].astype(jnp.float32)
    flat_routes = routes.reshape(-1)
    copy_rows = jnp.repeat(normed_two.reshape(-1, model_width), 2, axis=0)
    const_wide = const_full.astype(jnp.float32)
    is_copy = (flat_routes == EXPERTS + 1)[:, None]
    first_const = (flat_routes == EXPERTS + 2).astype(jnp.float32)[:, None]
    second_const = (flat_routes == EXPERTS + 3).astype(jnp.float32)[:, None]
    entry_vals = (
        expert_vals
        + jnp.where(is_copy, copy_rows, 0.0)
        + first_const * const_wide[:, 0][None, :]
        + second_const * const_wide[:, 1][None, :]
    )
    entry_vals = entry_vals.reshape(seq_count, pos_count, 2, model_width)
    layer_out = middle + jnp.sum(gate_probs[..., None] * entry_vals, axis=2)
    grad_mixed = out_cotangent.astype(jnp.float32)
    grad_gates = jnp.sum(grad_mixed[:, :, None, :] * entry_vals, axis=-1)
    grad_chosen = gate_probs * (
        grad_gates - jnp.sum(gate_probs * grad_gates, axis=-1, keepdims=True)
    )
    choice_ids = jnp.arange(EXPERTS + 4, dtype=jnp.int32)
    prior_logits_gradient = jnp.sum(
        (routes[..., None] == choice_ids).astype(jnp.float32) * grad_chosen[..., None], axis=2
    )
    grad_entries = (gate_probs[..., None] * grad_mixed[:, :, None, :]).reshape(-1, model_width)
    send_grads = (
        jnp.zeros((EXPERTS * slot_count + 1, model_width), jnp.bfloat16)
        .at[destination]
        .set(grad_entries.astype(jnp.bfloat16))[:-1]
        .reshape(EXPERTS, 1, slot_count, model_width)
    )
    owner_grads = lax.all_to_all(send_grads, "expert", split_axis=0, concat_axis=1, tiled=True)
    sigmoid_gate = jax.nn.sigmoid(gate_pre)
    silu_gate = gate_pre * sigmoid_gate
    hidden_back = (silu_gate * up_pre).astype(jnp.bfloat16)
    grad_hidden = jnp.einsum(
        "ensd,efd->ensf", owner_grads, down_full, preferred_element_type=jnp.float32
    )
    grad_gate_pre = (
        grad_hidden * up_pre * sigmoid_gate * (1.0 + gate_pre * (1.0 - sigmoid_gate))
    ).astype(jnp.bfloat16)
    grad_up_pre = (grad_hidden * silu_gate).astype(jnp.bfloat16)
    down_part = jnp.einsum(
        "ensf,ensd->efd", hidden_back, owner_grads, preferred_element_type=jnp.float32
    )
    gate_part = jnp.einsum(
        "ensi,ensf->eif", received, grad_gate_pre, preferred_element_type=jnp.float32
    )
    up_part = jnp.einsum(
        "ensi,ensf->eif", received, grad_up_pre, preferred_element_type=jnp.float32
    )
    grad_rows = (
        jnp.einsum("ensf,eif->ensi", grad_gate_pre, gate_full, preferred_element_type=jnp.float32)
        + jnp.einsum("ensf,eif->ensi", grad_up_pre, up_full, preferred_element_type=jnp.float32)
    ).astype(jnp.bfloat16)
    rows_back = lax.all_to_all(grad_rows, "expert", split_axis=1, concat_axis=0, tiled=True)
    gate_grad, up_grad, down_grad = (
        lax.psum_scatter(
            gate_part.astype(jnp.bfloat16), "shard", scatter_dimension=1, tiled=True
        ).astype(jnp.float32),
        lax.psum_scatter(
            up_part.astype(jnp.bfloat16), "shard", scatter_dimension=1, tiled=True
        ).astype(jnp.float32),
        lax.psum_scatter(
            down_part.astype(jnp.bfloat16), "shard", scatter_dimension=1, tiled=True
        ).astype(jnp.float32),
    )
    grad_row_entries = jnp.concatenate([rows_back.reshape(-1, model_width), zero_row], axis=0)[
        destination
    ].astype(jnp.float32)
    grad_copy = jnp.where(is_copy, grad_entries, 0.0)
    router_widened = router_weight_wide.astype(jnp.float32)
    grad_normed_two = jnp.sum(
        (grad_row_entries + grad_copy).reshape(seq_count, pos_count, 2, model_width), axis=2
    ) + jnp.einsum(
        "hwk,ok->hwo", prior_logits_gradient, router_widened, precision=lax.Precision.HIGHEST
    )
    router_part = jnp.einsum(
        "vrx,vrb->xb",
        normalized_narrow.astype(jnp.float32),
        prior_logits_gradient,
        precision=lax.Precision.HIGHEST,
    )
    const_part = jnp.stack(
        [jnp.sum(first_const * grad_entries, axis=0), jnp.sum(second_const * grad_entries, axis=0)],
        axis=-1,
    )
    moe_gain_part = jnp.sum(grad_normed_two * scaled_two, axis=(0, 1))
    grad_middle = grad_mixed + rms_back(grad_normed_two * moe_gain_wide, middle, inverse_two)
    gradient_projected = grad_middle.astype(jnp.bfloat16)
    output_part = jnp.einsum(
        "vrx,vrb->xb",
        attention_output_narrow,
        gradient_projected,
        preferred_element_type=jnp.float32,
    )
    grad_attended = jnp.einsum(
        "hwk,ok->hwo", gradient_projected, output_weight_wide, preferred_element_type=jnp.float32
    ).astype(jnp.bfloat16)
    delta_rows = jnp.sum(
        (grad_attended.astype(jnp.float32) * attention_output).reshape(
            seq_count, pos_count, HEADS, -1
        ),
        axis=-1,
    )
    delta_sum = jnp.transpose(delta_rows, (0, 2, 1))

    def backward_one(packed):
        return attend_backward(
            packed[0],
            packed[1],
            packed[2],
            packed[3],
            packed[4],
            packed[5],
            packed[6],
            offset,
            block_count,
            width_block,
        )

    grad_query_rot, grad_keys_all, grad_values_all = lax.map(
        backward_one,
        (query_rot, keys_all, values_all, segment_ids, log_total, delta_sum, grad_attended),
    )
    grad_keys, grad_values = (
        lax.psum_scatter(
            grad_keys_all.astype(jnp.bfloat16), "expert", scatter_dimension=1, tiled=True
        ).astype(jnp.float32),
        lax.psum_scatter(
            grad_values_all.astype(jnp.bfloat16), "expert", scatter_dimension=1, tiled=True
        ).astype(jnp.float32),
    )
    gradient_query_unrotated = rotary(grad_query_rot, positions, -1.0).astype(jnp.bfloat16)
    gradient_key_unrotated = rotary(grad_keys, positions, -1.0).astype(jnp.bfloat16)
    gradient_value_narrow = grad_values.astype(jnp.bfloat16)
    query_part = jnp.einsum(
        "vrx,vrb->xb",
        normalized_first,
        gradient_query_unrotated,
        preferred_element_type=jnp.float32,
    )
    key_part = jnp.einsum(
        "vrx,vrb->xb", normalized_first, gradient_key_unrotated, preferred_element_type=jnp.float32
    )
    value_part = jnp.einsum(
        "vrx,vrb->xb", normalized_first, gradient_value_narrow, preferred_element_type=jnp.float32
    )
    grad_normed_one = jnp.einsum(
        "hwk,ok->hwo",
        gradient_query_unrotated,
        query_weight_wide,
        preferred_element_type=jnp.float32,
    )
    grad_normed_one = grad_normed_one + jnp.einsum(
        "hwk,ok->hwo", gradient_key_unrotated, key_weight_wide, preferred_element_type=jnp.float32
    )
    grad_normed_one = grad_normed_one + jnp.einsum(
        "hwk,ok->hwo", gradient_value_narrow, value_weight_wide, preferred_element_type=jnp.float32
    )
    attn_gain_part = jnp.sum(grad_normed_one * scaled_one, axis=(0, 1))
    tokens_grad = grad_middle + rms_back(grad_normed_one * attn_gain_wide, tokens_wide, inverse_one)
    layer_parts = (
        lax.psum_scatter(
            query_part.astype(jnp.bfloat16), "shard", scatter_dimension=0, tiled=True
        ).astype(jnp.float32),
        lax.psum_scatter(
            key_part.astype(jnp.bfloat16), "shard", scatter_dimension=0, tiled=True
        ).astype(jnp.float32),
        lax.psum_scatter(
            value_part.astype(jnp.bfloat16), "shard", scatter_dimension=0, tiled=True
        ).astype(jnp.float32),
        lax.psum_scatter(
            output_part.astype(jnp.bfloat16), "shard", scatter_dimension=0, tiled=True
        ).astype(jnp.float32),
        lax.psum_scatter(
            router_part.astype(jnp.bfloat16), "shard", scatter_dimension=0, tiled=True
        ).astype(jnp.float32),
        lax.psum_scatter(
            const_part.astype(jnp.bfloat16), "shard", scatter_dimension=0, tiled=True
        ).astype(jnp.float32),
        lax.psum_scatter(
            attn_gain_part.astype(jnp.bfloat16), "shard", scatter_dimension=0, tiled=True
        ).astype(jnp.float32),
        lax.psum_scatter(
            moe_gain_part.astype(jnp.bfloat16), "shard", scatter_dimension=0, tiled=True
        ).astype(jnp.float32),
    )
    layer_grads = (
        lax.psum(layer_parts[0].astype(jnp.bfloat16), "expert").astype(jnp.float32),
        lax.psum(layer_parts[1].astype(jnp.bfloat16), "expert").astype(jnp.float32),
        lax.psum(layer_parts[2].astype(jnp.bfloat16), "expert").astype(jnp.float32),
        lax.psum(layer_parts[3].astype(jnp.bfloat16), "expert").astype(jnp.float32),
        lax.psum(layer_parts[4].astype(jnp.bfloat16), "expert").astype(jnp.float32),
        lax.psum(layer_parts[5].astype(jnp.bfloat16), "expert").astype(jnp.float32),
        lax.psum(layer_parts[6].astype(jnp.bfloat16), "expert").astype(jnp.float32),
        lax.psum(layer_parts[7].astype(jnp.bfloat16), "expert").astype(jnp.float32),
    )
    return (
        layer_out.astype(jnp.bfloat16),
        tokens_grad,
        prior_logits_gradient,
        layer_grads[0],
        layer_grads[1],
        layer_grads[2],
        layer_grads[3],
        layer_grads[4],
        layer_grads[5],
        layer_grads[6],
        layer_grads[7],
        gate_grad,
        up_grad,
        down_grad,
    )


RING = 4
PAIR = 2
LOCAL = 4
META = 16


def z_pairs(step):
    lines = PAIR * PAIR
    return [
        (z * lines + rest, (z + step) % RING * lines + rest)
        for z in range(RING)
        for rest in range(lines)
    ]


def along_z(values, step):
    return lax.ppermute(values, "shard", z_pairs(step))


def across_y(values):
    return lax.ppermute(values, "shard", [(s, s ^ PAIR) for s in range(RING * PAIR * PAIR)])


def across_core(values):
    return lax.ppermute(values, "shard", [(s, s ^ 1) for s in range(RING * PAIR * PAIR)])


def across_x(values):
    return lax.ppermute(values, "expert", [(0, 1), (1, 0)])


def together(*values):
    return lax.optimization_barrier(values)


def gather_rows(own, beside=()):
    ring, crossed = [own], []
    for step in range(RING - 1):
        following, other = along_z(ring[-1], 1), across_x(ring[-1])
        if step == 1 and beside:
            following, other, beside = together(following, other, beside)
        else:
            following, other = together(following, other)
        ring.append(following)
        crossed.append(other)
    return ring + crossed + [across_x(ring[-1])], beside


def add_all(*values):
    return sum(value.astype(jnp.float32) for value in values)


def reduce_rows(parts, beside, late):
    other, beside = together(across_x(parts[2 * RING - 1]), beside)
    total = add_all(parts[RING - 1], other)
    for step in reversed(range(RING - 1)):
        passed, other = along_z(total.astype(jnp.bfloat16), -1), across_x(parts[RING + step])
        if step == 1:
            passed, other, late = together(passed, other, late)
        else:
            passed, other = together(passed, other)
        total = add_all(parts[step], passed, other)
    return total, beside, late


def plane_groups():
    lines = PAIR * PAIR
    return [[z * lines + i for i in range(lines)] for z in range(RING)]


def scatter_plane(part):
    return lax.psum_scatter(
        part, "shard", scatter_dimension=0, axis_index_groups=plane_groups(), tiled=False
    )


def gather_plane(part):
    return lax.all_gather(part, "shard", axis=0, axis_index_groups=plane_groups(), tiled=False)


def split_core(part, core_place):
    rows, width = part.shape
    part = part.reshape(RING, PAIR, PAIR, rows // (RING * PAIR * PAIR), width)
    mine = jnp.where(core_place == 0, part[:, :, 0], part[:, :, 1])
    other = jnp.where(core_place == 0, part[:, :, 1], part[:, :, 0])
    return mine, other


def reduce_packed(parts, z_place, y_place, first_grad, late):
    total = None
    for step in reversed(range(RING)):
        owner = lax.rem(z_place - step + RING, RING)
        blocks = [lax.dynamic_index_in_dim(part, owner, 0, keepdims=False) for part in parts]
        block = jnp.concatenate(blocks, axis=-1)
        other = across_y(jnp.where(y_place == 0, block[1], block[0]))
        mine = jnp.where(y_place == 0, block[0], block[1])
        if total is None:
            other, first_grad = together(other, first_grad)
            here = add_all(mine, other)
            shared = lax.ppermute(first_grad, "expert", [(1, 0)])
        else:
            passed, other = together(along_z(total, -1), other)
            if step == 1:
                passed, shared, late = together(passed, shared, late)
            here = add_all(mine, passed, other)
        total = here.astype(jnp.bfloat16)
    return add_all(total, across_x(total)), shared, late


def meta_rows(rows, width):
    filled = jnp.concatenate(rows, axis=-1).reshape(len(rows) // 2, -1)
    return jnp.pad(filled, ((0, META - filled.shape[0]), (0, width - filled.shape[1]))).astype(
        jnp.bfloat16
    )


def dot_rows(left, right):
    return lax.dot_general(left, right, (((1,), (0,)), ((), ())), preferred_element_type=jnp.float32)


def dot_wide(left, right):
    return lax.dot_general(left, right, (((1,), (1,)), ((), ())), preferred_element_type=jnp.float32)


def dot_tall(left, right):
    return lax.dot_general(left, right, (((0,), (0,)), ((), ())), preferred_element_type=jnp.float32)


def pick_kernel(place, *refs):
    block_count = RING * PAIR
    grads = refs[:block_count]
    pick_ref, slot_ref = refs[block_count:]
    rows = pick_ref.shape[2]
    later = lax.broadcasted_iota(jnp.int32, (rows, rows), 1)
    earlier = lax.broadcasted_iota(jnp.int32, (rows, rows), 0)
    before = jnp.where(earlier < later, 1.0, 0.0).astype(jnp.bfloat16)
    wanted = (lax.broadcasted_iota(jnp.int32, (8, rows), 0) + place[0] * LOCAL).astype(
        jnp.float32
    )
    inside = lax.broadcasted_iota(jnp.int32, (8, rows), 0) < LOCAL
    ranks = lax.broadcasted_iota(jnp.int32, (CAP, rows), 0).astype(jnp.float32)
    for block in range(block_count):
        meta = grads[block][rows : rows + META, :].astype(jnp.float32)
        first = meta[1:2, :rows]
        second = meta[1:2, rows : 2 * rows]
        named = jnp.where(((first == wanted) | (second == wanted)) & inside, 1.0, 0.0)
        rank = dot_rows(named.astype(jnp.bfloat16), before)
        pieces = []
        for expert in range(LOCAL):
            hit = (rank[expert : expert + 1] == ranks) & (named[expert : expert + 1] > 0.5)
            pieces.append(jnp.where(hit, 1.0, 0.0))
        pick = jnp.concatenate(pieces, axis=0).astype(jnp.bfloat16)
        pick_ref[block] = pick
        slot_ref[block] = dot_rows(pick, grads[block][:rows, :]).astype(jnp.bfloat16)


def prepare_kernel(place, slot_ref, own_ref, moved_ref, *refs):
    downs = refs[:4]
    back_ref, wide_ref, down_ref = refs[4:]
    number = pl.program_id(0)
    block_count = slot_ref.shape[0]
    half = wide_ref.shape[2] // 2
    depth = own_ref.shape[3]
    for line in range(PAIR * PAIR):
        for step in range(RING):
            owner = lax.rem(place[1] - step + RING, RING) * (PAIR * PAIR) + line
            start = pl.multiple_of(owner * depth, 16)
            for side in range(2):
                piece = own_ref[line, side, 0] if step == 0 else moved_ref[line, step - 1, side, 0]
                wide_ref[0, pl.ds(start, depth), side * half : (side + 1) * half] = piece
        part = downs[line]
        deep = part.shape[1]
        source = (place[2] ^ (line % PAIR)) * PAIR + (place[3] ^ (line // PAIR))
        down_ref[0, pl.ds(pl.multiple_of(source * deep, 16), deep), :] = part[0]
    width = slot_ref.shape[2]
    mine = slot_ref[:, pl.ds(pl.multiple_of(number * CAP, CAP), CAP), :]
    back_ref[0] = dot_wide(mine.reshape(block_count * CAP, width), down_ref[0])


def expert_kernel(place, *refs):
    block_count = RING * PAIR
    tokens = refs[:block_count]
    pick_ref, wide_ref, down_ref, back_ref = refs[block_count : block_count + 4]
    rest = refs[block_count + 4 :]
    slot_ref, hidden_ref, mixed_ref = rest[:3]
    grad_refs = rest[3 : 3 + block_count]
    out_refs = rest[3 + block_count : 3 + 2 * block_count]
    out_slots, grad_slots, gate_grads = rest[3 + 2 * block_count :]
    number = pl.program_id(0)
    rows = pick_ref.shape[2]
    width = slot_ref.shape[2]
    half = wide_ref.shape[2] // 2

    @pl.when(number == 0)
    def _():
        gate_grads[...] = jnp.zeros_like(gate_grads)
        for block in range(block_count):
            slot_ref[block] = dot_rows(pick_ref[block], tokens[block][:rows, :]).astype(
                jnp.bfloat16
            )

    span = pl.ds(pl.multiple_of(number * CAP, CAP), CAP)
    mine = slot_ref[:, span, :].reshape(block_count * CAP, width)
    both = dot_rows(mine, wide_ref[0])
    gate = both[:, :half]
    up = both[:, half:]
    sigmoid = 1.0 / (1.0 + jnp.exp(-gate))
    silu = gate * sigmoid
    hidden = silu * up
    back = back_ref[0]
    expert_id = (number + place[0] * LOCAL).astype(jnp.float32)
    chances = []
    product = jnp.sum(hidden * back, axis=1, keepdims=True)
    for block in range(block_count):
        meta = tokens[block][rows : rows + META, :].astype(jnp.float32)
        first = jnp.where(meta[1:2, :rows] == expert_id, 1.0, 0.0)
        second = jnp.where(meta[1:2, rows : 2 * rows] == expert_id, 1.0, 0.0)
        pick = pick_ref[block, span, :].astype(jnp.float32)
        chance = first * meta[0:1, :rows] + second * meta[0:1, rows : 2 * rows]
        chances.append(jnp.sum(pick * chance, axis=1, keepdims=True))
        spread = jnp.sum(
            pick * product[block * CAP : (block + 1) * CAP], axis=0, keepdims=True
        )
        gate_grads[block, 0:1, :rows] += first * spread
        gate_grads[block, 0:1, rows : 2 * rows] += second * spread
    chance = jnp.concatenate(chances, axis=0)
    back = back * chance
    weighted = (hidden * chance).astype(jnp.bfloat16)
    grad_gate = back * up * sigmoid * (1.0 + gate * (1.0 - sigmoid))
    grad_up = back * silu
    mixed = jnp.concatenate([grad_gate, grad_up], axis=1).astype(jnp.bfloat16)
    hidden_ref[0] = weighted
    mixed_ref[0] = mixed
    out_part = dot_rows(weighted, down_ref[0]).astype(jnp.bfloat16)
    out_slots[:, span, :] = out_part.reshape(block_count, CAP, width)
    grad_part = dot_wide(mixed, wide_ref[0]).astype(jnp.bfloat16)
    grad_slots[:, span, :] = grad_part.reshape(block_count, CAP, width)

    @pl.when(number == LOCAL - 1)
    def _():
        for block in range(block_count):
            pick = pick_ref[block]
            grad_refs[block][:rows, :] = dot_tall(pick, grad_slots[block]).astype(jnp.bfloat16)
            grad_refs[block][rows : rows + META, :] = gate_grads[block].astype(jnp.bfloat16)
            out_refs[block][...] = dot_tall(pick, out_slots[block]).astype(jnp.bfloat16)


def weight_grad_kernel(place, *refs):
    slot_ref, back_ref, hidden_ref, mixed_ref, wide_ref, down_ref, wide_sum = refs
    number = pl.program_id(0)
    block_count, _, width = slot_ref.shape
    span = pl.ds(pl.multiple_of(number * CAP, CAP), CAP)
    rows = slot_ref[:, span, :].reshape(block_count * CAP, width)
    wide_sum[...] = dot_tall(rows, mixed_ref[0])
    grads = back_ref[:, span, :].reshape(block_count * CAP, width)
    half = wide_sum.shape[1] // 2
    deep = down_ref.shape[2]
    depth = wide_ref.shape[4]
    for line in range(PAIR * PAIR):
        for step in range(RING):
            owner = lax.rem(place[1] - step + RING, RING) * (PAIR * PAIR) + line
            part = wide_sum[pl.ds(pl.multiple_of(owner * depth, 16), depth), :]
            wide_ref[line, step, 0, 0] = part[:, :half].astype(jnp.bfloat16)
            wide_ref[line, step, 1, 0] = part[:, half:].astype(jnp.bfloat16)
        columns = hidden_ref[0, :, line * deep : (line + 1) * deep]
        down_ref[line, 0] = dot_tall(columns, grads).astype(jnp.bfloat16)


def busy(microseconds):
    return pl.CostEstimate(
        flops=microseconds * 400_000_000,
        transcendentals=0,
        bytes_accessed=microseconds * 3_000_000,
    )


def whole(shape):
    return pl.BlockSpec(shape, lambda number, place: (0,) * len(shape))


def by_expert(shape, axis=0):
    return pl.BlockSpec(
        shape,
        lambda number, place: tuple(number if d == axis else 0 for d in range(len(shape))),
    )


def pick_slots(place, grads):
    padded, width = grads[0].shape
    rows = padded - META
    blocks = len(grads)
    shapes = [(blocks, LOCAL * CAP, rows), (blocks, LOCAL * CAP, width)]
    return pl.pallas_call(
        pick_kernel,
        name="pick_slots",
        cost_estimate=busy(4),
        out_shape=[jax.ShapeDtypeStruct(shape, jnp.bfloat16) for shape in shapes],
        grid_spec=pltpu.PrefetchScalarGridSpec(
            num_scalar_prefetch=1,
            grid=(1,),
            in_specs=[whole(g.shape) for g in grads],
            out_specs=[whole(shape) for shape in shapes],
        ),
    )(place, *grads)


def prepare_experts(place, slot_rows, own, moved, downs):
    blocks, _, width = slot_rows.shape
    lines, _, local, depth, span = own.shape
    deep = downs[0].shape[1]
    model = depth * RING * lines
    slots = blocks * CAP
    shapes = [
        ((local, slots, span), jnp.float32),
        ((local, model, 2 * span), jnp.bfloat16),
        ((local, deep * lines, width), jnp.bfloat16),
    ]
    return pl.pallas_call(
        prepare_kernel,
        name="prepare_experts",
        cost_estimate=busy(10),
        out_shape=[jax.ShapeDtypeStruct(s, d) for s, d in shapes],
        grid_spec=pltpu.PrefetchScalarGridSpec(
            num_scalar_prefetch=1,
            grid=(local,),
            in_specs=[
                whole(slot_rows.shape),
                by_expert((lines, 2, 1, depth, span), 2),
                by_expert((lines, RING - 1, 2, 1, depth, span), 3),
            ]
            + [by_expert((1, deep, width))] * 4,
            out_specs=[
                by_expert((1, slots, span)),
                by_expert((1, model, 2 * span)),
                by_expert((1, deep * lines, width)),
            ],
        ),
    )(place, slot_rows, own, moved, *downs)


def run_experts(place, tokens, pick, wide, down, back):
    padded, width = tokens[0].shape
    rows = padded - META
    blocks = len(tokens)
    local, model, span2 = wide.shape
    span = span2 // 2
    slots = blocks * CAP
    shapes = [
        ((blocks, local * CAP, width), jnp.bfloat16),
        ((local, slots, span), jnp.bfloat16),
        ((local, slots, span2), jnp.bfloat16),
    ]
    shapes = shapes + [((padded, width), jnp.bfloat16)] * blocks
    shapes = shapes + [((rows, width), jnp.bfloat16)] * blocks
    results = pl.pallas_call(
        expert_kernel,
        name="run_experts",
        cost_estimate=busy(22),
        out_shape=[jax.ShapeDtypeStruct(s, d) for s, d in shapes],
        grid_spec=pltpu.PrefetchScalarGridSpec(
            num_scalar_prefetch=1,
            grid=(local,),
            in_specs=[whole(t.shape) for t in tokens]
            + [
                whole(pick.shape),
                by_expert((1, model, span2)),
                by_expert((1, span, width)),
                by_expert((1, slots, span)),
            ],
            out_specs=[
                whole(shapes[0][0]),
                by_expert((1, slots, span)),
                by_expert((1, slots, span2)),
            ]
            + [whole(s) for s, _ in shapes[3:]],
            scratch_shapes=[
                pltpu.VMEM((blocks, local * CAP, width), jnp.bfloat16),
                pltpu.VMEM((blocks, local * CAP, width), jnp.bfloat16),
                pltpu.VMEM((blocks, META, width), jnp.float32),
            ],
        ),
    )(place, *tokens, pick, wide, down, back)
    return results[:3], results[3 : 3 + blocks], results[3 + blocks :]


def weight_grads(place, slots, backs, hidden, mixed):
    blocks, total, width = slots.shape
    local, rows, span = hidden.shape
    lines = PAIR * PAIR
    depth = width // (RING * lines)
    deep = span // lines
    return pl.pallas_call(
        weight_grad_kernel,
        name="weight_grads",
        cost_estimate=busy(12),
        out_shape=[
            jax.ShapeDtypeStruct((lines, RING, 2, local, depth, span), jnp.bfloat16),
            jax.ShapeDtypeStruct((lines, local, deep, width), jnp.bfloat16),
        ],
        grid_spec=pltpu.PrefetchScalarGridSpec(
            num_scalar_prefetch=1,
            grid=(local,),
            in_specs=[
                whole(slots.shape),
                whole(backs.shape),
                by_expert((1, rows, span)),
                by_expert((1, rows, 2 * span)),
            ],
            out_specs=[
                by_expert((lines, RING, 2, 1, depth, span), 3),
                by_expert((lines, 1, deep, width), 1),
            ],
            scratch_shapes=[pltpu.VMEM((width, 2 * span), jnp.float32)],
        ),
    )(place, slots, backs, hidden, mixed)


def add_low(left, right):
    return (left.astype(jnp.float32) + right.astype(jnp.float32)).astype(jnp.bfloat16)


def turn_pairs(values, cosine, sine):
    half = values.shape[1] // 4
    lane = lax.rem(lax.broadcasted_iota(jnp.int32, values.shape, 1), 2 * half)
    swapped = jnp.where(
        lane < half,
        pltpu.roll(values, 3 * half, 1),
        pltpu.roll(values, half, 1),
    )
    return values * cosine + swapped * sine


def mask_bias(x_place, rows, columns, row_segments, column_segments):
    row = lax.broadcasted_iota(jnp.int32, (rows, columns), 0) + x_place * rows
    column = lax.broadcasted_iota(jnp.int32, (rows, columns), 1)
    return jnp.where((column <= row) & (row_segments == column_segments), 0.0, masked_fill)


def attention_forward_kernel(
    place,
    normed_ref,
    query_weight,
    key_weight,
    value_weight,
    output_weight,
    cosine_ref,
    sine_ref,
    column_ref,
    row_ref,
    query_ref,
    key_ref,
    value_ref,
    mixed_ref,
    total_ref,
    result_ref,
    bias_ref,
):
    rows, columns = bias_ref.shape
    own = pl.ds(pl.multiple_of(place[0] * rows, rows), rows)

    @pl.when(pl.program_id(0) == 0)
    def _():
        bias_ref[...] = mask_bias(place[0], rows, columns, column_ref[own, :], row_ref[...])
        result_ref[...] = jnp.zeros_like(result_ref)

    normed = normed_ref[...]
    query = dot_rows(normed_ref[own, :], query_weight[...])
    query = turn_pairs(query, cosine_ref[own, :], sine_ref[own, :]).astype(jnp.bfloat16)
    key = turn_pairs(dot_rows(normed, key_weight[...]), cosine_ref[...], sine_ref[...])
    key = key.astype(jnp.bfloat16)
    value = dot_rows(normed, value_weight[...]).astype(jnp.bfloat16)
    query_ref[...] = query
    key_ref[...] = key
    value_ref[...] = value
    width = query.shape[1]
    low = lax.broadcasted_iota(jnp.int32, (rows, width), 1) < width // 2
    scale = (width // 2) ** (-0.5)
    sides = []
    for side in range(2):
        keep = low if side == 0 else jnp.logical_not(low)
        scores = dot_wide(jnp.where(keep, query, 0), key) * scale + bias_ref[...]
        top = jnp.max(scores, axis=1, keepdims=True)
        terms = jnp.exp(scores - top)
        count = jnp.sum(terms, axis=1, keepdims=True)
        probs = (terms * (1.0 / count)).astype(jnp.bfloat16)
        sides.append((dot_rows(probs, value), top + jnp.log(count)))
    mixed = jnp.where(low, sides[0][0], sides[1][0])
    mixed_ref[...] = mixed
    total_ref[0] = jnp.where(low, sides[0][1], sides[1][1])
    result_ref[...] += dot_rows(mixed.astype(jnp.bfloat16), output_weight[...])


def attention_backward_kernel(
    place,
    normed_ref,
    query_weight,
    key_weight,
    value_weight,
    output_weight,
    cosine_ref,
    sine_ref,
    column_ref,
    row_ref,
    query_ref,
    key_ref,
    value_ref,
    mixed_ref,
    total_ref,
    grad_ref,
    weight_mine,
    weight_other,
    result_ref,
    bias_ref,
    weight_ref,
):
    rows, columns = bias_ref.shape
    own = pl.ds(pl.multiple_of(place[0] * rows, rows), rows)

    @pl.when(pl.program_id(0) == 0)
    def _():
        bias_ref[...] = mask_bias(place[0], rows, columns, column_ref[own, :], row_ref[...])
        result_ref[...] = jnp.zeros_like(result_ref)

    normed = normed_ref[...]
    grad = grad_ref[...]
    query, key, value, mixed = query_ref[...], key_ref[...], value_ref[...], mixed_ref[...]
    attended = dot_wide(grad, output_weight[...]).astype(jnp.bfloat16)
    product = attended.astype(jnp.float32) * mixed
    width = query.shape[1]
    low = lax.broadcasted_iota(jnp.int32, (rows, width), 1) < width // 2
    low_keys = lax.broadcasted_iota(jnp.int32, (columns, width), 1) < width // 2
    scale = (width // 2) ** (-0.5)
    sides = []
    for side in range(2):
        keep = low if side == 0 else jnp.logical_not(low)
        start = side * (width // 2)
        delta = jnp.sum(jnp.where(keep, product, 0.0), axis=1, keepdims=True)
        scores = dot_wide(jnp.where(keep, query, 0), key) * scale + bias_ref[...]
        probs = jnp.exp(scores - total_ref[0, :, start : start + 1])
        grad_probs = dot_wide(jnp.where(keep, attended, 0), value)
        grad_scores = (probs * (grad_probs - delta) * scale).astype(jnp.bfloat16)
        sides.append(
            (
                dot_rows(grad_scores, key),
                dot_tall(grad_scores, query),
                dot_tall(probs.astype(jnp.bfloat16), attended),
            )
        )
    grad_query = jnp.where(low, sides[0][0], sides[1][0])
    grad_key = jnp.where(low_keys, sides[0][1], sides[1][1])
    grad_value = jnp.where(low_keys, sides[0][2], sides[1][2]).astype(jnp.bfloat16)
    grad_query = turn_pairs(grad_query, cosine_ref[own, :], -sine_ref[own, :])
    grad_query = grad_query.astype(jnp.bfloat16)
    grad_key = turn_pairs(grad_key, cosine_ref[...], -sine_ref[...]).astype(jnp.bfloat16)
    result_ref[...] += dot_wide(grad_key, key_weight[...]) + dot_wide(
        grad_value, value_weight[...]
    )
    result_ref[own, :] += dot_wide(grad_query, query_weight[...])
    weight_ref[:, :width] = dot_tall(normed_ref[own, :], grad_query)
    weight_ref[:, width : 2 * width] = dot_tall(normed, grad_key)
    weight_ref[:, 2 * width :] = dot_tall(normed, grad_value)
    depth = weight_mine.shape[3]
    for z in range(RING):
        for y in range(PAIR):
            pair = (z * PAIR + y) * PAIR
            near = pl.ds(pl.multiple_of((pair + place[3]) * depth, 16), depth)
            far = pl.ds(pl.multiple_of((pair + 1 - place[3]) * depth, 16), depth)
            for kind in range(3):
                span = slice(kind * width, (kind + 1) * width)
                weight_mine[kind, z, y] = weight_ref[near, span].astype(jnp.bfloat16)
                weight_other[kind, z, y] = weight_ref[far, span].astype(jnp.bfloat16)


def attention_specs(normed, weights, cosine, column, row, first):
    columns, model = normed.shape
    pairs = HEADS // 2
    width = model // pairs

    def block(shape, index):
        return pl.BlockSpec(shape, lambda number, place: index(number + first))

    return [
        whole(normed.shape),
        block((model, width), lambda n: (0, n)),
        block((model, width), lambda n: (0, pairs + n)),
        block((model, width), lambda n: (0, 2 * pairs + n)),
        block((width, model), lambda n: (n, 3)),
        whole(cosine.shape),
        whole(cosine.shape),
        whole(column.shape),
        whole(row.shape),
    ]


def attention_forward(place, normed, weights, cosine, sine, column, row):
    columns, model = normed.shape
    rows = columns // PAIR
    pairs = HEADS // 2
    width = model // pairs
    across = lambda size: pl.BlockSpec((size, width), lambda number, place: (0, number))
    return pl.pallas_call(
        attention_forward_kernel,
        name="attention_forward",
        cost_estimate=busy(15),
        out_shape=[
            jax.ShapeDtypeStruct((rows, model), jnp.bfloat16),
            jax.ShapeDtypeStruct((columns, model), jnp.bfloat16),
            jax.ShapeDtypeStruct((columns, model), jnp.bfloat16),
            jax.ShapeDtypeStruct((rows, model), jnp.float32),
            jax.ShapeDtypeStruct((pairs, rows, width), jnp.float32),
            jax.ShapeDtypeStruct((rows, model), jnp.float32),
        ],
        grid_spec=pltpu.PrefetchScalarGridSpec(
            num_scalar_prefetch=1,
            grid=(pairs,),
            in_specs=attention_specs(normed, weights, cosine, column, row, 0),
            out_specs=[
                across(rows),
                across(columns),
                across(columns),
                across(rows),
                by_expert((1, rows, width)),
                whole((rows, model)),
            ],
            scratch_shapes=[pltpu.VMEM((rows, columns), jnp.float32)],
        ),
    )(place, normed, weights, weights, weights, weights, cosine, sine, column, row)


def attention_backward(place, normed, weights, cosine, sine, column, row, kept, grad, first, count):
    columns, model = normed.shape
    rows = columns // PAIR
    width = model // (HEADS // 2)
    depth = model // (RING * PAIR * PAIR)
    across = lambda size: pl.BlockSpec((size, width), lambda number, place: (0, number + first))
    return pl.pallas_call(
        attention_backward_kernel,
        name="attention_backward",
        cost_estimate=busy(9),
        out_shape=[
            jax.ShapeDtypeStruct((3, RING, PAIR, depth, width * count), jnp.bfloat16),
            jax.ShapeDtypeStruct((3, RING, PAIR, depth, width * count), jnp.bfloat16),
            jax.ShapeDtypeStruct((columns, model), jnp.float32),
        ],
        grid_spec=pltpu.PrefetchScalarGridSpec(
            num_scalar_prefetch=1,
            grid=(count,),
            in_specs=attention_specs(normed, weights, cosine, column, row, first)
            + [
                across(rows),
                across(columns),
                across(columns),
                across(rows),
                pl.BlockSpec((1, rows, width), lambda number, place: (number + first, 0, 0)),
                whole(grad.shape),
            ],
            out_specs=[
                pl.BlockSpec((3, RING, PAIR, depth, width), lambda n, place: (0, 0, 0, 0, n)),
                pl.BlockSpec((3, RING, PAIR, depth, width), lambda n, place: (0, 0, 0, 0, n)),
                whole((columns, model)),
            ],
            scratch_shapes=[
                pltpu.VMEM((rows, columns), jnp.float32),
                pltpu.VMEM((model, 3 * width), jnp.float32),
            ],
        ),
    )(place, normed, weights, weights, weights, weights, cosine, sine, column, row, *kept, grad)


def weight_pieces(gate_weight, up_weight, z_place):
    span = gate_weight.shape[2] // RING
    pieces = []
    for step in range(RING):
        start = lax.rem(z_place + step, RING) * span
        pieces.append(
            jnp.stack(
                [
                    lax.dynamic_slice_in_dim(gate_weight, start, span, 2),
                    lax.dynamic_slice_in_dim(up_weight, start, span, 2),
                ]
            )
        )
    return pieces


def place_columns(parts, z_place):
    columns = []
    for column in range(RING):
        choice = lax.rem(column - z_place + RING, RING)
        chosen = parts[0]
        for step in range(1, RING):
            chosen = jnp.where(choice == step, parts[step], chosen)
        columns.append(chosen)
    both = jnp.concatenate(columns, axis=-1).astype(jnp.float32)
    return both[0], both[1]


def body_split(
    tokens,
    segment_ids,
    routes,
    earlier_logits,
    out_cotangent,
    query_weight,
    key_weight,
    value_weight,
    output_weight,
    router_weight,
    const_vectors,
    attn_gain,
    moe_gain,
    gate_weight,
    up_weight,
    down_weight,
):
    _, pos_count, model_width = tokens.shape
    tokens, segment_row, routes = tokens[0], segment_ids[0], routes[0]
    earlier_logits, cotangent_low = earlier_logits[0], out_cotangent[0]
    x_place = lax.axis_index("expert")
    shard_place = lax.axis_index("shard")
    z_place = shard_place // (PAIR * PAIR)
    y_place = lax.rem(shard_place // PAIR, PAIR)
    core_place = lax.rem(shard_place, PAIR)
    order = jnp.arange(4, dtype=jnp.int32)
    place = jnp.where(
        order == 0,
        x_place,
        jnp.where(order == 1, z_place, jnp.where(order == 2, y_place, core_place)),
    ).astype(jnp.int32)
    choices = router_weight.shape[1]
    consts = const_vectors.shape[1]
    small_count = choices + consts + 2
    small = jnp.concatenate(
        [router_weight, const_vectors, attn_gain[:, None], moe_gain[:, None]], axis=1
    )
    small = jnp.pad(small, ((0, 0), (0, 128 - small_count)))
    packed = jnp.concatenate(
        [query_weight, key_weight, value_weight, output_weight, small], axis=1
    )
    routes_low = routes.astype(jnp.bfloat16)
    route_rows = [routes_low[:, 0], routes_low[:, 1]]
    zero_rows = [jnp.zeros_like(route_rows[0])] * 2
    cotangent_blocks, _ = gather_rows(
        jnp.concatenate([cotangent_low, meta_rows(zero_rows + route_rows, model_width)], axis=0)
    )
    gathered = lax.all_gather(packed, "shard", axis=0, tiled=True)
    other_tokens = across_x(tokens)
    frequency = jnp.exp(
        (jnp.arange(128, dtype=jnp.int32) % 32).astype(jnp.float32) * (-2.0 * math.log(10000.0) / 64)
    )
    angles = jnp.arange(PAIR * pos_count, dtype=jnp.float32)[:, None] * frequency[None, :]
    cosine = jnp.cos(angles)
    sine = jnp.sin(angles) * jnp.where(jnp.arange(128) % 64 < 32, -1.0, 1.0)
    segment_low = segment_row.astype(jnp.float32)[None, :]
    segment_column = segment_row.astype(jnp.float32)[:, None]
    cosine, sine, gathered, other_tokens, cotangent_blocks = together(
        cosine, sine, gathered, other_tokens, cotangent_blocks
    )
    pieces = weight_pieces(gate_weight, up_weight, z_place)
    down_other = across_y(down_weight)
    moved = [along_z(pieces[1], 1)]
    gathered, other_tokens, cotangent_blocks, pieces, down_other, moved = together(
        gathered, other_tokens, cotangent_blocks, pieces, down_other, moved
    )
    own_wide = gather_plane(pieces[0])
    downs = [down_weight, down_other, across_core(down_weight), across_core(down_other)]
    moved = moved + [along_z(pieces[step], step) for step in range(2, RING)]

    joint = 3 * model_width
    tail = gathered[:, joint + model_width :].astype(jnp.float32)
    router_low = gathered[:, joint + model_width : joint + model_width + choices]
    router_wide = tail[:, :choices]
    const_wide = tail[:, choices : choices + consts].T
    gain_attn = tail[:, choices + consts]
    gain_moe = tail[:, choices + consts + 1]

    first_tokens = jnp.where(x_place == 0, tokens, other_tokens)
    second_tokens = jnp.where(x_place == 0, other_tokens, tokens)
    all_wide = jnp.concatenate([first_tokens, second_tokens], axis=0).astype(jnp.float32)
    scaled_all, _ = rms_parts(all_wide)
    normed_all = (scaled_all * gain_attn).astype(jnp.bfloat16)
    tokens_wide = tokens.astype(jnp.float32)
    _, inverse_one = rms_parts(tokens_wide)
    query_rot, keys_all, values_all, mixed_heads, totals, projected = attention_forward(
        place, normed_all, gathered, cosine, sine, segment_column, segment_low
    )
    projected, moved = together(projected, moved)
    moved_wide = gather_plane(jnp.stack(moved))
    middle = tokens_wide + projected
    scaled_two, inverse_two = rms_parts(middle)
    normed_two = scaled_two * gain_moe
    normed_low = normed_two.astype(jnp.bfloat16)
    router_logits = dot_rows(normed_low, router_low) + earlier_logits
    choice_ids = jnp.arange(choices, dtype=jnp.int32)
    one_hot = (routes[..., None] == choice_ids).astype(jnp.float32)
    chosen = jnp.sum(one_hot * router_logits[:, None, :], axis=-1)
    gate_probs = jax.nn.softmax(chosen, axis=-1)
    probs_low = gate_probs.astype(jnp.bfloat16)
    payload = jnp.concatenate(
        [
            normed_low,
            meta_rows([probs_low[:, 0], probs_low[:, 1]] + route_rows, model_width),
        ],
        axis=0,
    )
    payload, cotangent_blocks = together(payload, cotangent_blocks)
    token_blocks, (pick, back_slots) = gather_rows(
        payload, tuple(pick_slots(place, cotangent_blocks))
    )
    back_hidden, wide_full, down_full = prepare_experts(
        place, back_slots, own_wide, moved_wide, downs
    )
    (token_slots, hidden, mixed), grad_parts, out_parts = run_experts(
        place, token_blocks, pick, wide_full, down_full, back_hidden
    )

    grad_total, (wide_grads, down_grads), out_parts = reduce_rows(
        grad_parts, weight_grads(place, token_slots, back_slots, hidden, mixed), out_parts
    )
    wide_sum = scatter_plane(wide_grads)
    wide_sum, down_grads = together(wide_sum, down_grads)
    down_sum = scatter_plane(down_grads)
    out_other = across_x(out_parts[7])

    cotangent = cotangent_low.astype(jnp.float32)
    copies = jnp.sum(one_hot[..., EXPERTS + 1] * gate_probs, axis=-1)[:, None]
    const_probs = jnp.sum(one_hot[..., EXPERTS + 2 :] * gate_probs[..., None], axis=1)
    copy_dot = jnp.sum(cotangent * normed_two, axis=-1)
    const_dot = jnp.stack(
        [jnp.sum(cotangent * const_wide[i], axis=-1) for i in range(consts)], axis=-1
    )
    grad_rows = grad_total[:pos_count]
    expert_dot = jnp.stack(
        [grad_total[pos_count, i * pos_count : (i + 1) * pos_count] for i in range(2)], axis=-1
    )
    grad_gates = (
        expert_dot
        + one_hot[..., EXPERTS + 1] * copy_dot[:, None]
        + jnp.sum(one_hot[..., EXPERTS + 2 :] * const_dot[:, None, :], axis=-1)
    )
    grad_chosen = gate_probs * (
        grad_gates - jnp.sum(gate_probs * grad_gates, axis=-1, keepdims=True)
    )
    prior_logits_gradient = jnp.sum(one_hot * grad_chosen[..., None], axis=1)
    highest = lax.Precision.HIGHEST
    grad_normed_two = (
        grad_rows
        + copies * cotangent
        + jnp.einsum("wk,ok->wo", prior_logits_gradient, router_wide, precision=highest)
    )
    router_part = jnp.einsum(
        "rx,rb->xb", normed_low.astype(jnp.float32), prior_logits_gradient, precision=highest
    )
    const_part = jnp.einsum("rx,rb->xb", cotangent, const_probs, precision=highest)
    moe_gain_part = jnp.sum(grad_normed_two * scaled_two, axis=0)
    grad_middle = cotangent + rms_back(grad_normed_two * gain_moe, middle, inverse_two)
    grad_projected = grad_middle.astype(jnp.bfloat16)
    small_early = jnp.concatenate(
        [router_part, const_part, jnp.zeros_like(moe_gain_part)[:, None], moe_gain_part[:, None]],
        axis=1,
    )
    small_early = jnp.pad(small_early, ((0, 0), (0, 128 - small_count)))
    output_part = dot_tall(mixed_heads.astype(jnp.bfloat16), grad_projected)
    output_mine, output_other = split_core(output_part.astype(jnp.bfloat16), core_place)
    grad_projected, out_other, output_mine, output_other, small_early = together(
        grad_projected, out_other, output_mine, output_other, small_early
    )
    kept = [query_rot, keys_all, values_all, mixed_heads, totals]
    shared_args = [place, normed_all, gathered, cosine, sine, segment_column, segment_low, kept]
    out_total = add_low(out_parts[3], out_other)
    out_passed, out_other = along_z(out_total, -1), across_x(out_parts[6])
    output_other = across_core(output_other)
    grads_a = attention_backward(*shared_args, grad_projected, 0, 2)
    grad_projected, grads_a, out_passed, out_other, output_other, wide_sum = together(
        grad_projected, grads_a, out_passed, out_other, output_other, wide_sum
    )
    moved_back = [wide_sum[0], along_z(wide_sum[1], -1)]
    out_total = add_all(out_parts[2], out_passed, out_other).astype(jnp.bfloat16)
    output_sum = add_low(output_mine, output_other)
    out_passed, out_other = along_z(out_total, -1), across_x(out_parts[5])
    other_a = across_core(grads_a[1])
    grads_b = attention_backward(*shared_args, grad_projected, 2, 2)
    grad_projected, grads_b, out_passed, out_other, other_a = together(
        grad_projected, grads_b, out_passed, out_other, other_a
    )
    out_total = add_all(out_parts[1], out_passed, out_other).astype(jnp.bfloat16)
    sum_a = add_low(grads_a[0], other_a)
    out_passed, out_other = along_z(out_total, -1), across_x(out_parts[4])
    moved_third = along_z(wide_sum[3], -3)
    other_b = across_core(grads_b[1])
    grads_c = attention_backward(*shared_args, grad_projected, 4, 2)
    grads_c, sum_a, out_passed, out_other, other_b, wide_sum = together(
        grads_c, sum_a, out_passed, out_other, other_b, wide_sum
    )
    moved_back = moved_back + [along_z(wide_sum[2], -2), moved_third]
    down_grad = down_sum.astype(jnp.float32)
    other_c = across_core(grads_c[1])
    sum_b = add_low(grads_b[0], other_b)
    grad_normed_all = grads_a[2] + grads_b[2] + grads_c[2]
    gain_lane = choices + consts
    chosen_lane = jnp.where(jnp.arange(128) == gain_lane, 1.0, 0.0).astype(jnp.bfloat16)
    gain_part = dot_tall(
        (grad_normed_all * scaled_all).astype(jnp.bfloat16),
        jnp.broadcast_to(chosen_lane, (grad_normed_all.shape[0], 128)),
    )
    first_grad = grad_normed_all[:pos_count]
    grad_normed_one = jnp.where(x_place == 0, first_grad, grad_normed_all[pos_count:])
    first_grad = first_grad.astype(jnp.bfloat16)
    small_part = (small_early + gain_part).astype(jnp.bfloat16)
    small_mine, small_other = split_core(small_part, core_place)
    small_sum = add_low(small_mine, across_core(small_other))
    sum_c = add_low(grads_c[0], other_c)
    packed_parts = [part[kind] for kind in range(3) for part in (sum_a, sum_b, sum_c)]
    packed_parts = packed_parts + [output_sum, small_sum]
    packed_grad, shared, moved_back = reduce_packed(
        packed_parts, z_place, y_place, first_grad, moved_back
    )
    const_rows = sum(const_probs[:, i : i + 1] * const_wide[i : i + 1] for i in range(consts))
    layer_out = (
        middle
        + add_all(out_parts[0], out_passed, out_other)
        + copies * normed_two
        + const_rows
    )
    grad_normed_one = grad_normed_one + shared.astype(jnp.float32)
    tokens_grad = grad_middle + rms_back(grad_normed_one * gain_attn, tokens_wide, inverse_one)
    gate_grad, up_grad = place_columns(moved_back, z_place)
    output_grad = packed_grad[:, joint : joint + model_width]
    small_grad = packed_grad[:, joint + model_width :]
    query_grad, key_grad, value_grad = (
        packed_grad[:, i * model_width : (i + 1) * model_width] for i in range(3)
    )
    return (
        layer_out.astype(jnp.bfloat16)[None],
        tokens_grad[None],
        prior_logits_gradient[None],
        query_grad,
        key_grad,
        value_grad,
        output_grad,
        small_grad[:, :choices],
        small_grad[:, choices : choices + consts],
        small_grad[:, choices + consts],
        small_grad[:, choices + consts + 1],
        gate_grad,
        up_grad,
        down_grad,
    )


def solution(mesh):
    in_specs = (
        P("shard", "expert", None),
        P("shard", None),
        P("shard", "expert", None),
        P("shard", "expert", None),
        P("shard", "expert", None),
        P("shard", None),
        P("shard", None),
        P("shard", None),
        P("shard", None),
        P("shard", None),
        P("shard", None),
        P("shard"),
        P("shard"),
        P("expert", "shard", None),
        P("expert", "shard", None),
        P("expert", "shard", None),
    )
    out_specs = (
        P("shard", "expert", None),
        P("shard", "expert", None),
        P("shard", "expert", None),
        P("shard", None),
        P("shard", None),
        P("shard", None),
        P("shard", None),
        P("shard", None),
        P("shard", None),
        P("shard"),
        P("shard"),
        P("expert", "shard", None),
        P("expert", "shard", None),
        P("expert", "shard", None),
    )
    divided = mesh.shape["expert"] == PAIR and mesh.shape["shard"] == RING * PAIR * PAIR
    chosen = body_split if divided else body
    return jax.shard_map(chosen, mesh=mesh, in_specs=in_specs, out_specs=out_specs, check_vma=False)
```

```python
import math

import jax
import jax.numpy as jnp
from jax import lax
from jax.experimental import pallas as pl
from jax.experimental.pallas import tpu as pltpu
from jax.sharding import PartitionSpec as P

HEADS = 12
EXPERTS = 8
CAP = 64


norm_eps = 1e-06
masked_fill = -1e30


def rotary(values, positions, direction):
    dims_in = values.shape
    heads_view = values.reshape(dims_in[:-1] + (HEADS, dims_in[-1] // HEADS))
    half_size = heads_view.shape[-1] // 2
    frequency = jnp.exp(
        jnp.arange(half_size, dtype=jnp.float32) * (-2.0 * math.log(10000.0) / (2 * half_size))
    )
    angles = positions.astype(jnp.float32)[:, None] * frequency[None, :]
    cosine = jnp.cos(angles)[:, None, :]
    sine_part = direction * jnp.sin(angles)[:, None, :]
    first_half = heads_view[..., :half_size]
    second_half = heads_view[..., half_size:]
    turned = jnp.concatenate(
        [
            first_half * cosine - second_half * sine_part,
            second_half * cosine + first_half * sine_part,
        ],
        axis=-1,
    )
    return turned.reshape(dims_in)


def rms_parts(values):
    inverse = lax.rsqrt(jnp.mean(values * values, axis=-1, keepdims=True) + norm_eps)
    return (values * inverse, inverse)


def rms_back(grad_scaled, values, inverse):
    inner_mean = jnp.mean(grad_scaled * values, axis=-1, keepdims=True)
    return inverse * grad_scaled - values * inverse * inverse * inverse * inner_mean


def block_scores(query_heads, keys_all, segment_row, query_pos, query_seg, key_start, width_block):
    key_block = lax.dynamic_slice_in_dim(keys_all, key_start, width_block, 0)
    key_heads = key_block.reshape(width_block, HEADS, key_block.shape[-1] // HEADS)
    raw_scores = jnp.einsum(
        "qhd,khd->hqk", query_heads, key_heads, preferred_element_type=jnp.float32
    )
    scaled = raw_scores * key_heads.shape[-1] ** (-0.5)
    key_pos = key_start + jnp.arange(width_block, dtype=jnp.int32)
    key_seg = lax.dynamic_slice_in_dim(segment_row, key_start, width_block, 0)
    allowed = (key_pos[None, :] <= query_pos[:, None]) & (key_seg[None, :] == query_seg[:, None])
    return (scaled, allowed[None], key_heads)


def attend_forward(query_rot, keys_all, values_all, segment_row, offset, block_count, width_block):
    row_count = query_rot.shape[0]
    query_heads = query_rot.reshape(row_count, HEADS, -1)
    query_pos = offset + jnp.arange(row_count, dtype=jnp.int32)
    query_seg = lax.dynamic_slice_in_dim(segment_row, offset, row_count, 0)

    def gather_stats(number, state_pair):
        running_max, running_sum = state_pair
        scaled, allowed, key_heads = block_scores(
            query_heads,
            keys_all,
            segment_row,
            query_pos,
            query_seg,
            number * width_block,
            width_block,
        )
        masked = jnp.where(allowed, scaled, masked_fill)
        new_max = jnp.maximum(running_max, jnp.max(masked, axis=-1))
        exp_terms = jnp.where(allowed, jnp.exp(masked - new_max[..., None]), 0.0)
        return (new_max, running_sum * jnp.exp(running_max - new_max) + jnp.sum(exp_terms, axis=-1))

    start_max = jnp.full((HEADS, row_count), masked_fill, jnp.float32)
    start_sum = jnp.zeros((HEADS, row_count), jnp.float32)
    final_max, final_sum = lax.fori_loop(0, block_count, gather_stats, (start_max, start_sum))
    log_total = final_max + jnp.log(final_sum)

    def gather_output(number, running_out):
        key_start = number * width_block
        scaled, allowed, key_heads = block_scores(
            query_heads, keys_all, segment_row, query_pos, query_seg, key_start, width_block
        )
        weights = jnp.where(allowed, jnp.exp(scaled - log_total[..., None]), 0.0).astype(
            jnp.bfloat16
        )
        value_heads = lax.dynamic_slice_in_dim(values_all, key_start, width_block, 0).reshape(
            width_block, HEADS, -1
        )
        return running_out + jnp.einsum(
            "hqk,khd->qhd", weights, value_heads, preferred_element_type=jnp.float32
        )

    start_out = jnp.zeros((row_count, HEADS, query_heads.shape[-1]), jnp.float32)
    attention_output = lax.fori_loop(0, block_count, gather_output, start_out)
    return (attention_output.reshape(row_count, -1), log_total)


def attend_backward(
    query_rot,
    keys_all,
    values_all,
    segment_row,
    log_total,
    delta_sum,
    grad_low,
    offset,
    block_count,
    width_block,
):
    row_count = query_rot.shape[0]
    key_total = keys_all.shape[0]
    model_width = keys_all.shape[1]
    query_heads = query_rot.reshape(row_count, HEADS, -1)
    grad_heads = grad_low.reshape(row_count, HEADS, -1)
    query_pos = offset + jnp.arange(row_count, dtype=jnp.int32)
    query_seg = lax.dynamic_slice_in_dim(segment_row, offset, row_count, 0)
    score_scale = query_heads.shape[-1] ** (-0.5)

    def block_parts(number):
        key_start = number * width_block
        scaled, allowed, key_heads = block_scores(
            query_heads, keys_all, segment_row, query_pos, query_seg, key_start, width_block
        )
        prob_block = jnp.where(allowed, jnp.exp(scaled - log_total[..., None]), 0.0)
        value_heads = lax.dynamic_slice_in_dim(values_all, key_start, width_block, 0).reshape(
            width_block, HEADS, -1
        )
        grad_probs = jnp.einsum(
            "qhd,khd->hqk", grad_heads, value_heads, preferred_element_type=jnp.float32
        )
        grad_raw = (prob_block * (grad_probs - delta_sum[..., None]) * score_scale).astype(
            jnp.bfloat16
        )
        return (key_start, key_heads, prob_block, grad_raw)

    start_query = jnp.zeros((row_count, HEADS, query_heads.shape[-1]), jnp.float32)

    def accumulate(number, state_all):
        grad_query, grad_keys, grad_values = state_all
        key_start, key_heads, prob_block, grad_raw = block_parts(number)
        grad_query = grad_query + jnp.einsum(
            "hqk,khd->qhd", grad_raw, key_heads, preferred_element_type=jnp.float32
        )
        key_part = jnp.einsum(
            "hqk,qhd->khd", grad_raw, query_heads, preferred_element_type=jnp.float32
        )
        value_part = jnp.einsum(
            "hqk,qhd->khd",
            prob_block.astype(jnp.bfloat16),
            grad_heads,
            preferred_element_type=jnp.float32,
        )
        grad_keys = lax.dynamic_update_slice_in_dim(
            grad_keys, key_part.reshape(width_block, -1), key_start, 0
        )
        grad_values = lax.dynamic_update_slice_in_dim(
            grad_values, value_part.reshape(width_block, -1), key_start, 0
        )
        return (grad_query, grad_keys, grad_values)

    start_state = (
        start_query,
        jnp.zeros((key_total, model_width), jnp.float32),
        jnp.zeros((key_total, model_width), jnp.float32),
    )
    grad_query, grad_keys, grad_values = lax.fori_loop(0, block_count, accumulate, start_state)
    return (grad_query.reshape(row_count, -1), grad_keys, grad_values)


def body(
    tokens,
    segment_ids,
    routes,
    earlier_logits,
    out_cotangent,
    query_weight,
    key_weight,
    value_weight,
    output_weight,
    router_weight,
    const_vectors,
    attn_gain,
    moe_gain,
    gate_weight,
    up_weight,
    down_weight,
):
    (
        query_weight_wide,
        key_weight_wide,
        value_weight_wide,
        output_weight_wide,
        router_weight_wide,
        const_full,
        gain_attn,
        gain_moe,
    ) = (
        lax.all_gather(query_weight, "shard", axis=0, tiled=True),
        lax.all_gather(key_weight, "shard", axis=0, tiled=True),
        lax.all_gather(value_weight, "shard", axis=0, tiled=True),
        lax.all_gather(output_weight, "shard", axis=0, tiled=True),
        lax.all_gather(router_weight, "shard", axis=0, tiled=True),
        lax.all_gather(const_vectors, "shard", axis=0, tiled=True),
        lax.all_gather(attn_gain, "shard", axis=0, tiled=True),
        lax.all_gather(moe_gain, "shard", axis=0, tiled=True),
    )
    gate_full, up_full, down_full = (
        lax.all_gather(gate_weight, "shard", axis=1, tiled=True),
        lax.all_gather(up_weight, "shard", axis=1, tiled=True),
        lax.all_gather(down_weight, "shard", axis=1, tiled=True),
    )
    seq_count, pos_count, model_width = tokens.shape
    expert_pos = lax.axis_index("expert")
    offset = expert_pos * pos_count
    width_block = math.gcd(pos_count, 128)
    block_count = (expert_pos + 1) * (pos_count // width_block)
    positions = offset + jnp.arange(pos_count, dtype=jnp.int32)
    tokens_wide = tokens.astype(jnp.float32)
    scaled_one, inverse_one = rms_parts(tokens_wide)
    attn_gain_wide = gain_attn.astype(jnp.float32)
    normalized_first = (scaled_one * attn_gain_wide).astype(jnp.bfloat16)
    query_unrotated = jnp.einsum(
        "ibg,gv->ibv", normalized_first, query_weight_wide, preferred_element_type=jnp.float32
    )
    key_unrotated = jnp.einsum(
        "ibg,gv->ibv", normalized_first, key_weight_wide, preferred_element_type=jnp.float32
    )
    value_projected = jnp.einsum(
        "ibg,gv->ibv", normalized_first, value_weight_wide, preferred_element_type=jnp.float32
    )
    query_rot = rotary(query_unrotated, positions, 1.0).astype(jnp.bfloat16)
    key_rot = rotary(key_unrotated, positions, 1.0).astype(jnp.bfloat16)
    value_low = value_projected.astype(jnp.bfloat16)
    keys_all, values_all = (
        lax.all_gather(key_rot, "expert", axis=1, tiled=True),
        lax.all_gather(value_low, "expert", axis=1, tiled=True),
    )

    def forward_one(packed):
        return attend_forward(
            packed[0], packed[1], packed[2], packed[3], offset, block_count, width_block
        )

    attention_output, log_total = lax.map(
        forward_one, (query_rot, keys_all, values_all, segment_ids)
    )
    attention_output_narrow = attention_output.astype(jnp.bfloat16)
    projected_rows = jnp.einsum(
        "ibg,gv->ibv",
        attention_output_narrow,
        output_weight_wide,
        preferred_element_type=jnp.float32,
    )
    middle = tokens_wide + projected_rows
    scaled_two, inverse_two = rms_parts(middle)
    moe_gain_wide = gain_moe.astype(jnp.float32)
    normed_two = scaled_two * moe_gain_wide
    normalized_narrow = normed_two.astype(jnp.bfloat16)
    router_logits = (
        jnp.einsum(
            "ibg,gv->ibv", normalized_narrow, router_weight_wide, preferred_element_type=jnp.float32
        )
        + earlier_logits
    )
    chosen = jnp.take_along_axis(router_logits, routes, axis=-1)
    gate_probs = jax.nn.softmax(chosen, axis=-1)
    slot_count = seq_count * CAP
    route_entries = routes.reshape(seq_count, pos_count * 2)
    one_hot = (route_entries[..., None] == jnp.arange(EXPERTS, dtype=jnp.int32)).astype(jnp.int32)
    entry_ranks = jnp.cumsum(one_hot, axis=1) - one_hot
    slot_rank = jnp.sum(entry_ranks * one_hot, axis=-1)
    is_real = route_entries < EXPERTS
    destination = jnp.where(
        is_real,
        route_entries * slot_count
        + jnp.arange(seq_count, dtype=jnp.int32)[:, None] * CAP
        + slot_rank,
        EXPERTS * slot_count,
    ).reshape(-1)
    entry_rows = jnp.repeat(normalized_narrow.reshape(-1, model_width), 2, axis=0)
    send_rows = (
        jnp.zeros((EXPERTS * slot_count + 1, model_width), jnp.bfloat16)
        .at[destination]
        .set(entry_rows)[:-1]
        .reshape(EXPERTS, 1, slot_count, model_width)
    )
    received = lax.all_to_all(send_rows, "expert", split_axis=0, concat_axis=1, tiled=True)
    gate_pre = jnp.einsum("ensi,eif->ensf", received, gate_full, preferred_element_type=jnp.float32)
    up_pre = jnp.einsum("ensi,eif->ensf", received, up_full, preferred_element_type=jnp.float32)
    hidden = (jax.nn.silu(gate_pre) * up_pre).astype(jnp.bfloat16)
    result = jnp.einsum(
        "ensf,efi->ensi", hidden, down_full, preferred_element_type=jnp.float32
    ).astype(jnp.bfloat16)
    returned = lax.all_to_all(result, "expert", split_axis=1, concat_axis=0, tiled=True)
    zero_row = jnp.zeros((1, model_width), jnp.bfloat16)
    expert_vals = jnp.concatenate([returned.reshape(-1, model_width), zero_row], axis=0)[
        destination
    ].astype(jnp.float32)
    flat_routes = routes.reshape(-1)
    copy_rows = jnp.repeat(normed_two.reshape(-1, model_width), 2, axis=0)
    const_wide = const_full.astype(jnp.float32)
    is_copy = (flat_routes == EXPERTS + 1)[:, None]
    first_const = (flat_routes == EXPERTS + 2).astype(jnp.float32)[:, None]
    second_const = (flat_routes == EXPERTS + 3).astype(jnp.float32)[:, None]
    entry_vals = (
        expert_vals
        + jnp.where(is_copy, copy_rows, 0.0)
        + first_const * const_wide[:, 0][None, :]
        + second_const * const_wide[:, 1][None, :]
    )
    entry_vals = entry_vals.reshape(seq_count, pos_count, 2, model_width)
    layer_out = middle + jnp.sum(gate_probs[..., None] * entry_vals, axis=2)
    grad_mixed = out_cotangent.astype(jnp.float32)
    grad_gates = jnp.sum(grad_mixed[:, :, None, :] * entry_vals, axis=-1)
    grad_chosen = gate_probs * (
        grad_gates - jnp.sum(gate_probs * grad_gates, axis=-1, keepdims=True)
    )
    choice_ids = jnp.arange(EXPERTS + 4, dtype=jnp.int32)
    prior_logits_gradient = jnp.sum(
        (routes[..., None] == choice_ids).astype(jnp.float32) * grad_chosen[..., None], axis=2
    )
    grad_entries = (gate_probs[..., None] * grad_mixed[:, :, None, :]).reshape(-1, model_width)
    send_grads = (
        jnp.zeros((EXPERTS * slot_count + 1, model_width), jnp.bfloat16)
        .at[destination]
        .set(grad_entries.astype(jnp.bfloat16))[:-1]
        .reshape(EXPERTS, 1, slot_count, model_width)
    )
    owner_grads = lax.all_to_all(send_grads, "expert", split_axis=0, concat_axis=1, tiled=True)
    sigmoid_gate = jax.nn.sigmoid(gate_pre)
    silu_gate = gate_pre * sigmoid_gate
    hidden_back = (silu_gate * up_pre).astype(jnp.bfloat16)
    grad_hidden = jnp.einsum(
        "ensd,efd->ensf", owner_grads, down_full, preferred_element_type=jnp.float32
    )
    grad_gate_pre = (
        grad_hidden * up_pre * sigmoid_gate * (1.0 + gate_pre * (1.0 - sigmoid_gate))
    ).astype(jnp.bfloat16)
    grad_up_pre = (grad_hidden * silu_gate).astype(jnp.bfloat16)
    down_part = jnp.einsum(
        "ensf,ensd->efd", hidden_back, owner_grads, preferred_element_type=jnp.float32
    )
    gate_part = jnp.einsum(
        "ensi,ensf->eif", received, grad_gate_pre, preferred_element_type=jnp.float32
    )
    up_part = jnp.einsum(
        "ensi,ensf->eif", received, grad_up_pre, preferred_element_type=jnp.float32
    )
    grad_rows = (
        jnp.einsum("ensf,eif->ensi", grad_gate_pre, gate_full, preferred_element_type=jnp.float32)
        + jnp.einsum("ensf,eif->ensi", grad_up_pre, up_full, preferred_element_type=jnp.float32)
    ).astype(jnp.bfloat16)
    rows_back = lax.all_to_all(grad_rows, "expert", split_axis=1, concat_axis=0, tiled=True)
    gate_grad, up_grad, down_grad = (
        lax.psum_scatter(
            gate_part.astype(jnp.bfloat16), "shard", scatter_dimension=1, tiled=True
        ).astype(jnp.float32),
        lax.psum_scatter(
            up_part.astype(jnp.bfloat16), "shard", scatter_dimension=1, tiled=True
        ).astype(jnp.float32),
        lax.psum_scatter(
            down_part.astype(jnp.bfloat16), "shard", scatter_dimension=1, tiled=True
        ).astype(jnp.float32),
    )
    grad_row_entries = jnp.concatenate([rows_back.reshape(-1, model_width), zero_row], axis=0)[
        destination
    ].astype(jnp.float32)
    grad_copy = jnp.where(is_copy, grad_entries, 0.0)
    router_widened = router_weight_wide.astype(jnp.float32)
    grad_normed_two = jnp.sum(
        (grad_row_entries + grad_copy).reshape(seq_count, pos_count, 2, model_width), axis=2
    ) + jnp.einsum(
        "hwk,ok->hwo", prior_logits_gradient, router_widened, precision=lax.Precision.HIGHEST
    )
    router_part = jnp.einsum(
        "vrx,vrb->xb",
        normalized_narrow.astype(jnp.float32),
        prior_logits_gradient,
        precision=lax.Precision.HIGHEST,
    )
    const_part = jnp.stack(
        [jnp.sum(first_const * grad_entries, axis=0), jnp.sum(second_const * grad_entries, axis=0)],
        axis=-1,
    )
    moe_gain_part = jnp.sum(grad_normed_two * scaled_two, axis=(0, 1))
    grad_middle = grad_mixed + rms_back(grad_normed_two * moe_gain_wide, middle, inverse_two)
    gradient_projected = grad_middle.astype(jnp.bfloat16)
    output_part = jnp.einsum(
        "vrx,vrb->xb",
        attention_output_narrow,
        gradient_projected,
        preferred_element_type=jnp.float32,
    )
    grad_attended = jnp.einsum(
        "hwk,ok->hwo", gradient_projected, output_weight_wide, preferred_element_type=jnp.float32
    ).astype(jnp.bfloat16)
    delta_rows = jnp.sum(
        (grad_attended.astype(jnp.float32) * attention_output).reshape(
            seq_count, pos_count, HEADS, -1
        ),
        axis=-1,
    )
    delta_sum = jnp.transpose(delta_rows, (0, 2, 1))

    def backward_one(packed):
        return attend_backward(
            packed[0],
            packed[1],
            packed[2],
            packed[3],
            packed[4],
            packed[5],
            packed[6],
            offset,
            block_count,
            width_block,
        )

    grad_query_rot, grad_keys_all, grad_values_all = lax.map(
        backward_one,
        (query_rot, keys_all, values_all, segment_ids, log_total, delta_sum, grad_attended),
    )
    grad_keys, grad_values = (
        lax.psum_scatter(
            grad_keys_all.astype(jnp.bfloat16), "expert", scatter_dimension=1, tiled=True
        ).astype(jnp.float32),
        lax.psum_scatter(
            grad_values_all.astype(jnp.bfloat16), "expert", scatter_dimension=1, tiled=True
        ).astype(jnp.float32),
    )
    gradient_query_unrotated = rotary(grad_query_rot, positions, -1.0).astype(jnp.bfloat16)
    gradient_key_unrotated = rotary(grad_keys, positions, -1.0).astype(jnp.bfloat16)
    gradient_value_narrow = grad_values.astype(jnp.bfloat16)
    query_part = jnp.einsum(
        "vrx,vrb->xb",
        normalized_first,
        gradient_query_unrotated,
        preferred_element_type=jnp.float32,
    )
    key_part = jnp.einsum(
        "vrx,vrb->xb", normalized_first, gradient_key_unrotated, preferred_element_type=jnp.float32
    )
    value_part = jnp.einsum(
        "vrx,vrb->xb", normalized_first, gradient_value_narrow, preferred_element_type=jnp.float32
    )
    grad_normed_one = jnp.einsum(
        "hwk,ok->hwo",
        gradient_query_unrotated,
        query_weight_wide,
        preferred_element_type=jnp.float32,
    )
    grad_normed_one = grad_normed_one + jnp.einsum(
        "hwk,ok->hwo", gradient_key_unrotated, key_weight_wide, preferred_element_type=jnp.float32
    )
    grad_normed_one = grad_normed_one + jnp.einsum(
        "hwk,ok->hwo", gradient_value_narrow, value_weight_wide, preferred_element_type=jnp.float32
    )
    attn_gain_part = jnp.sum(grad_normed_one * scaled_one, axis=(0, 1))
    tokens_grad = grad_middle + rms_back(grad_normed_one * attn_gain_wide, tokens_wide, inverse_one)
    layer_parts = (
        lax.psum_scatter(
            query_part.astype(jnp.bfloat16), "shard", scatter_dimension=0, tiled=True
        ).astype(jnp.float32),
        lax.psum_scatter(
            key_part.astype(jnp.bfloat16), "shard", scatter_dimension=0, tiled=True
        ).astype(jnp.float32),
        lax.psum_scatter(
            value_part.astype(jnp.bfloat16), "shard", scatter_dimension=0, tiled=True
        ).astype(jnp.float32),
        lax.psum_scatter(
            output_part.astype(jnp.bfloat16), "shard", scatter_dimension=0, tiled=True
        ).astype(jnp.float32),
        lax.psum_scatter(
            router_part.astype(jnp.bfloat16), "shard", scatter_dimension=0, tiled=True
        ).astype(jnp.float32),
        lax.psum_scatter(
            const_part.astype(jnp.bfloat16), "shard", scatter_dimension=0, tiled=True
        ).astype(jnp.float32),
        lax.psum_scatter(
            attn_gain_part.astype(jnp.bfloat16), "shard", scatter_dimension=0, tiled=True
        ).astype(jnp.float32),
        lax.psum_scatter(
            moe_gain_part.astype(jnp.bfloat16), "shard", scatter_dimension=0, tiled=True
        ).astype(jnp.float32),
    )
    layer_grads = (
        lax.psum(layer_parts[0].astype(jnp.bfloat16), "expert").astype(jnp.float32),
        lax.psum(layer_parts[1].astype(jnp.bfloat16), "expert").astype(jnp.float32),
        lax.psum(layer_parts[2].astype(jnp.bfloat16), "expert").astype(jnp.float32),
        lax.psum(layer_parts[3].astype(jnp.bfloat16), "expert").astype(jnp.float32),
        lax.psum(layer_parts[4].astype(jnp.bfloat16), "expert").astype(jnp.float32),
        lax.psum(layer_parts[5].astype(jnp.bfloat16), "expert").astype(jnp.float32),
        lax.psum(layer_parts[6].astype(jnp.bfloat16), "expert").astype(jnp.float32),
        lax.psum(layer_parts[7].astype(jnp.bfloat16), "expert").astype(jnp.float32),
    )
    return (
        layer_out.astype(jnp.bfloat16),
        tokens_grad,
        prior_logits_gradient,
        layer_grads[0],
        layer_grads[1],
        layer_grads[2],
        layer_grads[3],
        layer_grads[4],
        layer_grads[5],
        layer_grads[6],
        layer_grads[7],
        gate_grad,
        up_grad,
        down_grad,
    )


RING = 4
PAIR = 2
LOCAL = 4
META = 16


def z_pairs(step):
    lines = PAIR * PAIR
    return [
        (z * lines + rest, (z + step) % RING * lines + rest)
        for z in range(RING)
        for rest in range(lines)
    ]


def along_z(values, step):
    return lax.ppermute(values, "shard", z_pairs(step))


def across_y(values):
    return lax.ppermute(values, "shard", [(s, s ^ PAIR) for s in range(RING * PAIR * PAIR)])


def across_core(values):
    return lax.ppermute(values, "shard", [(s, s ^ 1) for s in range(RING * PAIR * PAIR)])


def across_x(values):
    return lax.ppermute(values, "expert", [(0, 1), (1, 0)])


def together(*values):
    return lax.optimization_barrier(values)


def gather_rows(own, beside=()):
    ring, crossed = [own], []
    for step in range(RING - 1):
        following, other = along_z(ring[-1], 1), across_x(ring[-1])
        if step == 1 and beside:
            following, other, beside = together(following, other, beside)
        else:
            following, other = together(following, other)
        ring.append(following)
        crossed.append(other)
    return ring + crossed + [across_x(ring[-1])], beside


def add_all(*values):
    return sum(value.astype(jnp.float32) for value in values)


def reduce_rows(parts, beside, late):
    other, beside = together(across_x(parts[2 * RING - 1]), beside)
    total = add_all(parts[RING - 1], other)
    for step in reversed(range(RING - 1)):
        passed, other = along_z(total.astype(jnp.bfloat16), -1), across_x(parts[RING + step])
        if step == 1:
            passed, other, late = together(passed, other, late)
        else:
            passed, other = together(passed, other)
        total = add_all(parts[step], passed, other)
    return total, beside, late


def plane_groups():
    lines = PAIR * PAIR
    return [[z * lines + i for i in range(lines)] for z in range(RING)]


def scatter_plane(part):
    return lax.psum_scatter(
        part, "shard", scatter_dimension=0, axis_index_groups=plane_groups(), tiled=False
    )


def gather_plane(part):
    return lax.all_gather(part, "shard", axis=0, axis_index_groups=plane_groups(), tiled=False)


def split_core(part, core_place):
    rows, width = part.shape
    part = part.reshape(RING, PAIR, PAIR, rows // (RING * PAIR * PAIR), width)
    mine = jnp.where(core_place == 0, part[:, :, 0], part[:, :, 1])
    other = jnp.where(core_place == 0, part[:, :, 1], part[:, :, 0])
    return mine, other


def reduce_packed(parts, z_place, y_place, first_grad, late, finish):
    total = None
    for step in reversed(range(RING)):
        owner = lax.rem(z_place - step + RING, RING)
        blocks = [lax.dynamic_index_in_dim(part, owner, 0, keepdims=False) for part in parts]
        block = jnp.concatenate(blocks, axis=-1)
        other = across_y(jnp.where(y_place == 0, block[1], block[0]))
        mine = jnp.where(y_place == 0, block[0], block[1])
        if total is None:
            other, first_grad, passed = together(other, first_grad, late[1])
            late = (late[0], passed)
            here = add_all(mine, other)
            shared = lax.ppermute(first_grad, "expert", [(1, 0)])
        else:
            passed, other = together(along_z(total, -1), other)
            if step == 1:
                passed, shared, late = together(passed, shared, late)
            if step == 0:
                passed, late = together(passed, finish(late))
            here = add_all(mine, passed, other)
        total = here.astype(jnp.bfloat16)
    return add_all(total, across_x(total)), shared, late


def meta_rows(rows, width):
    filled = jnp.concatenate(rows, axis=-1).reshape(len(rows) // 2, -1)
    return jnp.pad(filled, ((0, META - filled.shape[0]), (0, width - filled.shape[1]))).astype(
        jnp.bfloat16
    )


def dot_rows(left, right):
    return lax.dot_general(left, right, (((1,), (0,)), ((), ())), preferred_element_type=jnp.float32)


def dot_wide(left, right):
    return lax.dot_general(left, right, (((1,), (1,)), ((), ())), preferred_element_type=jnp.float32)


def dot_tall(left, right):
    return lax.dot_general(left, right, (((0,), (0,)), ((), ())), preferred_element_type=jnp.float32)


def pick_kernel(place, *refs):
    block_count = RING * PAIR
    grads = refs[:block_count]
    pick_ref, slot_ref, stage = refs[block_count:]
    rows = pick_ref.shape[2]
    later = lax.broadcasted_iota(jnp.int32, (rows, rows), 1)
    earlier = lax.broadcasted_iota(jnp.int32, (rows, rows), 0)
    before = jnp.where(earlier < later, 1.0, 0.0).astype(jnp.bfloat16)
    wanted = (lax.broadcasted_iota(jnp.int32, (8, rows), 0) + place[0] * LOCAL).astype(
        jnp.float32
    )
    inside = lax.broadcasted_iota(jnp.int32, (8, rows), 0) < LOCAL
    ranks = lax.broadcasted_iota(jnp.int32, (CAP, rows), 0).astype(jnp.float32)
    for block in range(block_count):
        stage[block] = grads[block][...]

    def fill(block, nothing):
        meta = stage[block, rows : rows + META, :].astype(jnp.float32)
        first = meta[1:2, :rows]
        second = meta[1:2, rows : 2 * rows]
        named = jnp.where(((first == wanted) | (second == wanted)) & inside, 1.0, 0.0)
        rank = dot_rows(named.astype(jnp.bfloat16), before)
        pieces = []
        for expert in range(LOCAL):
            hit = (rank[expert : expert + 1] == ranks) & (named[expert : expert + 1] > 0.5)
            pieces.append(jnp.where(hit, 1.0, 0.0))
        pick = jnp.concatenate(pieces, axis=0).astype(jnp.bfloat16)
        pick_ref[block] = pick
        slot_ref[block] = dot_rows(pick, stage[block, :rows, :]).astype(jnp.bfloat16)
        return nothing

    lax.fori_loop(0, block_count, fill, 0)


def prepare_kernel(place, slot_ref, own_ref, moved_ref, *refs):
    downs = refs[:4]
    back_ref, wide_ref, down_ref = refs[4:]
    number = pl.program_id(0)
    block_count = slot_ref.shape[0]
    half = wide_ref.shape[2] // 2
    depth = own_ref.shape[3]
    for line in range(PAIR * PAIR):
        for step in range(RING):
            owner = lax.rem(place[1] - step + RING, RING) * (PAIR * PAIR) + line
            start = pl.multiple_of(owner * depth, 16)
            for side in range(2):
                piece = own_ref[line, side, 0] if step == 0 else moved_ref[line, step - 1, side, 0]
                wide_ref[0, pl.ds(start, depth), side * half : (side + 1) * half] = piece
        part = downs[line]
        deep = part.shape[1]
        source = (place[2] ^ (line % PAIR)) * PAIR + (place[3] ^ (line // PAIR))
        down_ref[0, pl.ds(pl.multiple_of(source * deep, 16), deep), :] = part[0]
    width = slot_ref.shape[2]
    mine = slot_ref[:, pl.ds(pl.multiple_of(number * CAP, CAP), CAP), :]
    back_ref[0] = dot_wide(mine.reshape(block_count * CAP, width), down_ref[0])


def expert_kernel(place, *refs):
    block_count = RING * PAIR
    tokens = refs[:block_count]
    pick_ref, wide_ref, down_ref, back_ref = refs[block_count : block_count + 4]
    rest = refs[block_count + 4 :]
    slot_ref, hidden_ref, mixed_ref = rest[:3]
    grad_refs = rest[3 : 3 + block_count]
    out_refs = rest[3 + block_count : 3 + 2 * block_count]
    out_slots, grad_slots, gate_grads, stage, product_ref, chance_ref = rest[3 + 2 * block_count :]
    number = pl.program_id(0)
    rows = pick_ref.shape[2]
    width = slot_ref.shape[2]
    half = wide_ref.shape[2] // 2

    @pl.when(number == 0)
    def _():
        gate_grads[...] = jnp.zeros_like(gate_grads)
        for block in range(block_count):
            stage[block] = tokens[block][...]

        def gather(block, nothing):
            slot_ref[block] = dot_rows(pick_ref[block], stage[block, :rows, :]).astype(
                jnp.bfloat16
            )
            return nothing

        lax.fori_loop(0, block_count, gather, 0)

    span = pl.ds(pl.multiple_of(number * CAP, CAP), CAP)
    mine = slot_ref[:, span, :].reshape(block_count * CAP, width)
    both = dot_rows(mine, wide_ref[0])
    gate = both[:, :half]
    up = both[:, half:]
    sigmoid = 1.0 / (1.0 + jnp.exp(-gate))
    silu = gate * sigmoid
    hidden = silu * up
    back = back_ref[0]
    expert_id = (number + place[0] * LOCAL).astype(jnp.float32)
    product_ref[...] = jnp.sum(hidden * back, axis=1, keepdims=True)

    def spread_block(block, nothing):
        meta = stage[block, rows : rows + META, :].astype(jnp.float32)
        first = jnp.where(meta[1:2, :rows] == expert_id, 1.0, 0.0)
        second = jnp.where(meta[1:2, rows : 2 * rows] == expert_id, 1.0, 0.0)
        pick = pick_ref[block, span, :].astype(jnp.float32)
        chance = first * meta[0:1, :rows] + second * meta[0:1, rows : 2 * rows]
        slots = pl.ds(pl.multiple_of(block * CAP, CAP), CAP)
        chance_ref[slots, :] = jnp.sum(pick * chance, axis=1, keepdims=True)
        spread = jnp.sum(pick * product_ref[slots, :], axis=0, keepdims=True)
        gate_grads[block, 0:1, :rows] += first * spread
        gate_grads[block, 0:1, rows : 2 * rows] += second * spread
        return nothing

    lax.fori_loop(0, block_count, spread_block, 0, unroll=4)
    chance = chance_ref[...]
    back = back * chance
    weighted = (hidden * chance).astype(jnp.bfloat16)
    grad_gate = back * up * sigmoid * (1.0 + gate * (1.0 - sigmoid))
    grad_up = back * silu
    mixed = jnp.concatenate([grad_gate, grad_up], axis=1).astype(jnp.bfloat16)
    hidden_ref[0] = weighted
    mixed_ref[0] = mixed
    out_part = dot_rows(weighted, down_ref[0]).astype(jnp.bfloat16)
    out_slots[:, span, :] = out_part.reshape(block_count, CAP, width)
    grad_part = dot_wide(mixed, wide_ref[0]).astype(jnp.bfloat16)
    grad_slots[:, span, :] = grad_part.reshape(block_count, CAP, width)

    @pl.when(number == LOCAL - 1)
    def _():
        def scatter(block, nothing):
            pick = pick_ref[block]
            grad_slots[block] = dot_tall(pick, grad_slots[block]).astype(jnp.bfloat16)
            out_slots[block] = dot_tall(pick, out_slots[block]).astype(jnp.bfloat16)
            return nothing

        lax.fori_loop(0, block_count, scatter, 0)
        for block in range(block_count):
            grad_refs[block][:rows, :] = grad_slots[block]
            grad_refs[block][rows : rows + META, :] = gate_grads[block].astype(jnp.bfloat16)
            out_refs[block][...] = out_slots[block]


def weight_grad_kernel(place, *refs):
    slot_ref, back_ref, hidden_ref, mixed_ref, wide_ref, near_ref, core_ref, wide_sum = refs
    number = pl.program_id(0)
    block_count, _, width = slot_ref.shape
    span = pl.ds(pl.multiple_of(number * CAP, CAP), CAP)
    rows = slot_ref[:, span, :].reshape(block_count * CAP, width)
    wide_sum[...] = dot_tall(rows, mixed_ref[0])
    grads = back_ref[:, span, :].reshape(block_count * CAP, width)
    half = wide_sum.shape[1] // 2
    deep = near_ref.shape[2]
    depth = wide_ref.shape[4]
    for line in range(PAIR * PAIR):
        for step in range(RING):
            owner = lax.rem(place[1] - step + RING, RING) * (PAIR * PAIR) + line
            part = wide_sum[pl.ds(pl.multiple_of(owner * depth, 16), depth), :]
            wide_ref[line, step, 0, 0] = part[:, :half].astype(jnp.bfloat16)
            wide_ref[line, step, 1, 0] = part[:, half:].astype(jnp.bfloat16)
        side, core = line % PAIR, line // PAIR
        source = (place[2] ^ side) * PAIR + (place[3] ^ core)
        columns = hidden_ref[0, :, pl.ds(pl.multiple_of(source * deep, deep), deep)]
        target = core_ref if core else near_ref
        target[side, 0] = dot_tall(columns, grads).astype(jnp.bfloat16)


def busy(microseconds):
    return pl.CostEstimate(
        flops=microseconds * 400_000_000,
        transcendentals=0,
        bytes_accessed=microseconds * 3_000_000,
    )


def whole(shape):
    return pl.BlockSpec(shape, lambda number, place: (0,) * len(shape))


def by_expert(shape, axis=0):
    return pl.BlockSpec(
        shape,
        lambda number, place: tuple(number if d == axis else 0 for d in range(len(shape))),
    )


def pick_slots(place, grads):
    padded, width = grads[0].shape
    rows = padded - META
    blocks = len(grads)
    shapes = [(blocks, LOCAL * CAP, rows), (blocks, LOCAL * CAP, width)]
    return pl.pallas_call(
        pick_kernel,
        name="pick_slots",
        cost_estimate=busy(4),
        out_shape=[jax.ShapeDtypeStruct(shape, jnp.bfloat16) for shape in shapes],
        grid_spec=pltpu.PrefetchScalarGridSpec(
            num_scalar_prefetch=1,
            grid=(1,),
            in_specs=[whole(g.shape) for g in grads],
            out_specs=[whole(shape) for shape in shapes],
            scratch_shapes=[pltpu.VMEM((blocks, padded, width), jnp.bfloat16)],
        ),
    )(place, *grads)


def prepare_experts(place, slot_rows, own, moved, downs):
    blocks, _, width = slot_rows.shape
    lines, _, local, depth, span = own.shape
    deep = downs[0].shape[1]
    model = depth * RING * lines
    slots = blocks * CAP
    shapes = [
        ((local, slots, span), jnp.float32),
        ((local, model, 2 * span), jnp.bfloat16),
        ((local, deep * lines, width), jnp.bfloat16),
    ]
    return pl.pallas_call(
        prepare_kernel,
        name="prepare_experts",
        cost_estimate=busy(10),
        out_shape=[jax.ShapeDtypeStruct(s, d) for s, d in shapes],
        grid_spec=pltpu.PrefetchScalarGridSpec(
            num_scalar_prefetch=1,
            grid=(local,),
            in_specs=[
                whole(slot_rows.shape),
                by_expert((lines, 2, 1, depth, span), 2),
                by_expert((lines, RING - 1, 2, 1, depth, span), 3),
            ]
            + [by_expert((1, deep, width))] * 4,
            out_specs=[
                by_expert((1, slots, span)),
                by_expert((1, model, 2 * span)),
                by_expert((1, deep * lines, width)),
            ],
        ),
    )(place, slot_rows, own, moved, *downs)


def run_experts(place, tokens, pick, wide, down, back):
    padded, width = tokens[0].shape
    rows = padded - META
    blocks = len(tokens)
    local, model, span2 = wide.shape
    span = span2 // 2
    slots = blocks * CAP
    shapes = [
        ((blocks, local * CAP, width), jnp.bfloat16),
        ((local, slots, span), jnp.bfloat16),
        ((local, slots, span2), jnp.bfloat16),
    ]
    shapes = shapes + [((padded, width), jnp.bfloat16)] * blocks
    shapes = shapes + [((rows, width), jnp.bfloat16)] * blocks
    results = pl.pallas_call(
        expert_kernel,
        name="run_experts",
        cost_estimate=busy(22),
        out_shape=[jax.ShapeDtypeStruct(s, d) for s, d in shapes],
        grid_spec=pltpu.PrefetchScalarGridSpec(
            num_scalar_prefetch=1,
            grid=(local,),
            in_specs=[whole(t.shape) for t in tokens]
            + [
                whole(pick.shape),
                by_expert((1, model, span2)),
                by_expert((1, span, width)),
                by_expert((1, slots, span)),
            ],
            out_specs=[
                whole(shapes[0][0]),
                by_expert((1, slots, span)),
                by_expert((1, slots, span2)),
            ]
            + [whole(s) for s, _ in shapes[3:]],
            scratch_shapes=[
                pltpu.VMEM((blocks, local * CAP, width), jnp.bfloat16),
                pltpu.VMEM((blocks, local * CAP, width), jnp.bfloat16),
                pltpu.VMEM((blocks, META, width), jnp.float32),
                pltpu.VMEM((blocks, padded, width), jnp.bfloat16),
                pltpu.VMEM((slots, 1), jnp.float32),
                pltpu.VMEM((slots, 1), jnp.float32),
            ],
        ),
    )(place, *tokens, pick, wide, down, back)
    return results[:3], results[3 : 3 + blocks], results[3 + blocks :]


def weight_grads(place, slots, backs, hidden, mixed):
    blocks, total, width = slots.shape
    local, rows, span = hidden.shape
    lines = PAIR * PAIR
    depth = width // (RING * lines)
    deep = span // lines
    return pl.pallas_call(
        weight_grad_kernel,
        name="weight_grads",
        cost_estimate=busy(12),
        out_shape=[
            jax.ShapeDtypeStruct((lines, RING, 2, local, depth, span), jnp.bfloat16),
            jax.ShapeDtypeStruct((PAIR, local, deep, width), jnp.bfloat16),
            jax.ShapeDtypeStruct((PAIR, local, deep, width), jnp.bfloat16),
        ],
        grid_spec=pltpu.PrefetchScalarGridSpec(
            num_scalar_prefetch=1,
            grid=(local,),
            in_specs=[
                whole(slots.shape),
                whole(backs.shape),
                by_expert((1, rows, span)),
                by_expert((1, rows, 2 * span)),
            ],
            out_specs=[
                by_expert((lines, RING, 2, 1, depth, span), 3),
                by_expert((PAIR, 1, deep, width), 1),
                by_expert((PAIR, 1, deep, width), 1),
            ],
            scratch_shapes=[pltpu.VMEM((width, 2 * span), jnp.float32)],
        ),
    )(place, slots, backs, hidden, mixed)


def add_low(left, right):
    return (left.astype(jnp.float32) + right.astype(jnp.float32)).astype(jnp.bfloat16)


def turn_pairs(values, cosine, sine):
    half = values.shape[1] // 4
    lane = lax.rem(lax.broadcasted_iota(jnp.int32, values.shape, 1), 2 * half)
    swapped = jnp.where(
        lane < half,
        pltpu.roll(values, 3 * half, 1),
        pltpu.roll(values, half, 1),
    )
    return values * cosine + swapped * sine


def mask_bias(x_place, rows, columns, row_segments, column_segments):
    row = lax.broadcasted_iota(jnp.int32, (rows, columns), 0) + x_place * rows
    column = lax.broadcasted_iota(jnp.int32, (rows, columns), 1)
    return jnp.where((column <= row) & (row_segments == column_segments), 0.0, masked_fill)


def attention_forward_kernel(
    place,
    normed_ref,
    query_weight,
    key_weight,
    value_weight,
    output_weight,
    cosine_ref,
    sine_ref,
    column_ref,
    row_ref,
    query_ref,
    key_ref,
    value_ref,
    mixed_ref,
    total_ref,
    result_ref,
    bias_ref,
):
    rows, columns = bias_ref.shape
    own = pl.ds(pl.multiple_of(place[0] * rows, rows), rows)

    @pl.when(pl.program_id(0) == 0)
    def _():
        bias_ref[...] = mask_bias(place[0], rows, columns, column_ref[own, :], row_ref[...])
        result_ref[...] = jnp.zeros_like(result_ref)

    normed = normed_ref[...]
    query = dot_rows(normed_ref[own, :], query_weight[...])
    query = turn_pairs(query, cosine_ref[own, :], sine_ref[own, :]).astype(jnp.bfloat16)
    key = turn_pairs(dot_rows(normed, key_weight[...]), cosine_ref[...], sine_ref[...])
    key = key.astype(jnp.bfloat16)
    value = dot_rows(normed, value_weight[...]).astype(jnp.bfloat16)
    query_ref[...] = query
    key_ref[...] = key
    value_ref[...] = value
    width = query.shape[1]
    low = lax.broadcasted_iota(jnp.int32, (rows, width), 1) < width // 2
    scale = (width // 2) ** (-0.5)
    sides = []
    for side in range(2):
        keep = low if side == 0 else jnp.logical_not(low)
        scores = dot_wide(jnp.where(keep, query, 0), key) * scale + bias_ref[...]
        top = jnp.max(scores, axis=1, keepdims=True)
        terms = jnp.exp(scores - top)
        count = jnp.sum(terms, axis=1, keepdims=True)
        probs = (terms * (1.0 / count)).astype(jnp.bfloat16)
        sides.append((dot_rows(probs, value), top + jnp.log(count)))
    mixed = jnp.where(low, sides[0][0], sides[1][0])
    mixed_ref[...] = mixed
    total_ref[0] = jnp.where(low, sides[0][1], sides[1][1])
    result_ref[...] += dot_rows(mixed.astype(jnp.bfloat16), output_weight[...])


def attention_backward_kernel(
    place,
    normed_ref,
    query_weight,
    key_weight,
    value_weight,
    output_weight,
    cosine_ref,
    sine_ref,
    column_ref,
    row_ref,
    query_ref,
    key_ref,
    value_ref,
    mixed_ref,
    total_ref,
    grad_ref,
    carried_ref,
    weight_mine,
    weight_other,
    result_ref,
    bias_ref,
    weight_ref,
):
    rows, columns = bias_ref.shape
    own = pl.ds(pl.multiple_of(place[0] * rows, rows), rows)

    @pl.when(pl.program_id(0) == 0)
    def _():
        bias_ref[...] = mask_bias(place[0], rows, columns, column_ref[own, :], row_ref[...])
        result_ref[...] = carried_ref[...]

    normed = normed_ref[...]
    grad = grad_ref[...]
    query, key, value, mixed = query_ref[...], key_ref[...], value_ref[...], mixed_ref[...]
    attended = dot_wide(grad, output_weight[...]).astype(jnp.bfloat16)
    product = attended.astype(jnp.float32) * mixed
    width = query.shape[1]
    low = lax.broadcasted_iota(jnp.int32, (rows, width), 1) < width // 2
    low_keys = lax.broadcasted_iota(jnp.int32, (columns, width), 1) < width // 2
    scale = (width // 2) ** (-0.5)
    sides = []
    for side in range(2):
        keep = low if side == 0 else jnp.logical_not(low)
        start = side * (width // 2)
        delta = jnp.sum(jnp.where(keep, product, 0.0), axis=1, keepdims=True)
        scores = dot_wide(jnp.where(keep, query, 0), key) * scale + bias_ref[...]
        probs = jnp.exp(scores - total_ref[0, :, start : start + 1])
        grad_probs = dot_wide(jnp.where(keep, attended, 0), value)
        grad_scores = (probs * (grad_probs - delta) * scale).astype(jnp.bfloat16)
        sides.append(
            (
                dot_rows(grad_scores, key),
                dot_tall(grad_scores, query),
                dot_tall(probs.astype(jnp.bfloat16), attended),
            )
        )
    grad_query = jnp.where(low, sides[0][0], sides[1][0])
    grad_key = jnp.where(low_keys, sides[0][1], sides[1][1])
    grad_value = jnp.where(low_keys, sides[0][2], sides[1][2]).astype(jnp.bfloat16)
    grad_query = turn_pairs(grad_query, cosine_ref[own, :], -sine_ref[own, :])
    grad_query = grad_query.astype(jnp.bfloat16)
    grad_key = turn_pairs(grad_key, cosine_ref[...], -sine_ref[...]).astype(jnp.bfloat16)
    result_ref[...] += dot_wide(grad_key, key_weight[...]) + dot_wide(
        grad_value, value_weight[...]
    )
    result_ref[own, :] += dot_wide(grad_query, query_weight[...])
    weight_ref[:, :width] = dot_tall(normed_ref[own, :], grad_query)
    weight_ref[:, width : 2 * width] = dot_tall(normed, grad_key)
    weight_ref[:, 2 * width :] = dot_tall(normed, grad_value)
    depth = weight_mine.shape[3]
    for z in range(RING):
        for y in range(PAIR):
            pair = (z * PAIR + y) * PAIR
            near = pl.ds(pl.multiple_of((pair + place[3]) * depth, 16), depth)
            far = pl.ds(pl.multiple_of((pair + 1 - place[3]) * depth, 16), depth)
            for kind in range(3):
                span = slice(kind * width, (kind + 1) * width)
                weight_mine[kind, z, y] = weight_ref[near, span].astype(jnp.bfloat16)
                weight_other[kind, z, y] = weight_ref[far, span].astype(jnp.bfloat16)


def attention_specs(normed, weights, cosine, column, row, first):
    columns, model = normed.shape
    pairs = HEADS // 2
    width = model // pairs

    def block(shape, index):
        return pl.BlockSpec(shape, lambda number, place: index(number + first))

    return [
        whole(normed.shape),
        block((model, width), lambda n: (0, n)),
        block((model, width), lambda n: (0, pairs + n)),
        block((model, width), lambda n: (0, 2 * pairs + n)),
        block((width, model), lambda n: (n, 3)),
        whole(cosine.shape),
        whole(cosine.shape),
        whole(column.shape),
        whole(row.shape),
    ]


def attention_forward(place, normed, weights, cosine, sine, column, row):
    columns, model = normed.shape
    rows = columns // PAIR
    pairs = HEADS // 2
    width = model // pairs
    across = lambda size: pl.BlockSpec((size, width), lambda number, place: (0, number))
    return pl.pallas_call(
        attention_forward_kernel,
        name="attention_forward",
        cost_estimate=busy(15),
        out_shape=[
            jax.ShapeDtypeStruct((rows, model), jnp.bfloat16),
            jax.ShapeDtypeStruct((columns, model), jnp.bfloat16),
            jax.ShapeDtypeStruct((columns, model), jnp.bfloat16),
            jax.ShapeDtypeStruct((rows, model), jnp.float32),
            jax.ShapeDtypeStruct((pairs, rows, width), jnp.float32),
            jax.ShapeDtypeStruct((rows, model), jnp.float32),
        ],
        grid_spec=pltpu.PrefetchScalarGridSpec(
            num_scalar_prefetch=1,
            grid=(pairs,),
            in_specs=attention_specs(normed, weights, cosine, column, row, 0),
            out_specs=[
                across(rows),
                across(columns),
                across(columns),
                across(rows),
                by_expert((1, rows, width)),
                whole((rows, model)),
            ],
            scratch_shapes=[pltpu.VMEM((rows, columns), jnp.float32)],
        ),
    )(place, normed, weights, weights, weights, weights, cosine, sine, column, row)


def attention_backward(
    place, normed, weights, cosine, sine, column, row, kept, grad, carried, first, count
):
    columns, model = normed.shape
    rows = columns // PAIR
    width = model // (HEADS // 2)
    depth = model // (RING * PAIR * PAIR)
    across = lambda size: pl.BlockSpec((size, width), lambda number, place: (0, number + first))
    return pl.pallas_call(
        attention_backward_kernel,
        name="attention_backward",
        cost_estimate=busy(14),
        out_shape=[
            jax.ShapeDtypeStruct((3, RING, PAIR, depth, width * count), jnp.bfloat16),
            jax.ShapeDtypeStruct((3, RING, PAIR, depth, width * count), jnp.bfloat16),
            jax.ShapeDtypeStruct((columns, model), jnp.float32),
        ],
        grid_spec=pltpu.PrefetchScalarGridSpec(
            num_scalar_prefetch=1,
            grid=(count,),
            in_specs=attention_specs(normed, weights, cosine, column, row, first)
            + [
                across(rows),
                across(columns),
                across(columns),
                across(rows),
                pl.BlockSpec((1, rows, width), lambda number, place: (number + first, 0, 0)),
                whole(grad.shape),
                whole(carried.shape),
            ],
            out_specs=[
                pl.BlockSpec((3, RING, PAIR, depth, width), lambda n, place: (0, 0, 0, 0, n)),
                pl.BlockSpec((3, RING, PAIR, depth, width), lambda n, place: (0, 0, 0, 0, n)),
                whole((columns, model)),
            ],
            scratch_shapes=[
                pltpu.VMEM((rows, columns), jnp.float32),
                pltpu.VMEM((model, 3 * width), jnp.float32),
            ],
        ),
    )(place, normed, weights, weights, weights, weights, cosine, sine, column, row, *kept, grad, carried)


def weight_pieces(gate_weight, up_weight, z_place):
    span = gate_weight.shape[2] // RING
    pieces = []
    for step in range(RING):
        start = lax.rem(z_place + step, RING) * span
        pieces.append(
            jnp.stack(
                [
                    lax.dynamic_slice_in_dim(gate_weight, start, span, 2),
                    lax.dynamic_slice_in_dim(up_weight, start, span, 2),
                ]
            )
        )
    return pieces


def place_columns(parts, z_place):
    columns = []
    for column in range(RING):
        choice = lax.rem(column - z_place + RING, RING)
        chosen = parts[0]
        for step in range(1, RING):
            chosen = jnp.where(choice == step, parts[step], chosen)
        columns.append(chosen)
    both = jnp.concatenate(columns, axis=-1).astype(jnp.float32)
    return both[0], both[1]


def body_split(
    tokens,
    segment_ids,
    routes,
    earlier_logits,
    out_cotangent,
    query_weight,
    key_weight,
    value_weight,
    output_weight,
    router_weight,
    const_vectors,
    attn_gain,
    moe_gain,
    gate_weight,
    up_weight,
    down_weight,
):
    _, pos_count, model_width = tokens.shape
    tokens, segment_row, routes = tokens[0], segment_ids[0], routes[0]
    earlier_logits, cotangent_low = earlier_logits[0], out_cotangent[0]
    x_place = lax.axis_index("expert")
    shard_place = lax.axis_index("shard")
    z_place = shard_place // (PAIR * PAIR)
    y_place = lax.rem(shard_place // PAIR, PAIR)
    core_place = lax.rem(shard_place, PAIR)
    order = jnp.arange(4, dtype=jnp.int32)
    place = jnp.where(
        order == 0,
        x_place,
        jnp.where(order == 1, z_place, jnp.where(order == 2, y_place, core_place)),
    ).astype(jnp.int32)
    choices = router_weight.shape[1]
    consts = const_vectors.shape[1]
    small_count = choices + consts + 2
    small = jnp.concatenate(
        [router_weight, const_vectors, attn_gain[:, None], moe_gain[:, None]], axis=1
    )
    small = jnp.pad(small, ((0, 0), (0, 128 - small_count)))
    packed = jnp.concatenate(
        [query_weight, key_weight, value_weight, output_weight, small], axis=1
    )
    routes_low = routes.astype(jnp.bfloat16)
    route_rows = [routes_low[:, 0], routes_low[:, 1]]
    zero_rows = [jnp.zeros_like(route_rows[0])] * 2
    cotangent_blocks, _ = gather_rows(
        jnp.concatenate([cotangent_low, meta_rows(zero_rows + route_rows, model_width)], axis=0)
    )
    gathered = lax.all_gather(packed, "shard", axis=0, tiled=True)
    other_tokens = across_x(tokens)
    frequency = jnp.exp(
        (jnp.arange(128, dtype=jnp.int32) % 32).astype(jnp.float32) * (-2.0 * math.log(10000.0) / 64)
    )
    angles = jnp.arange(PAIR * pos_count, dtype=jnp.float32)[:, None] * frequency[None, :]
    cosine = jnp.cos(angles)
    sine = jnp.sin(angles) * jnp.where(jnp.arange(128) % 64 < 32, -1.0, 1.0)
    segment_low = segment_row.astype(jnp.float32)[None, :]
    segment_column = segment_row.astype(jnp.float32)[:, None]
    cosine, sine, gathered, other_tokens, cotangent_blocks = together(
        cosine, sine, gathered, other_tokens, cotangent_blocks
    )
    pieces = weight_pieces(gate_weight, up_weight, z_place)
    down_other = across_y(down_weight)
    moved = [along_z(pieces[1], 1)]
    gathered, other_tokens, cotangent_blocks, pieces, down_other, moved = together(
        gathered, other_tokens, cotangent_blocks, pieces, down_other, moved
    )
    own_wide = gather_plane(pieces[0])
    downs = [down_weight, down_other, across_core(down_weight), across_core(down_other)]
    moved = moved + [along_z(pieces[step], step) for step in range(2, RING)]

    joint = 3 * model_width
    tail = gathered[:, joint + model_width :].astype(jnp.float32)
    router_low = gathered[:, joint + model_width : joint + model_width + choices]
    const_wide = tail[:, choices : choices + consts].T
    gain_attn = tail[:, choices + consts]
    gain_moe = tail[:, choices + consts + 1]

    first_tokens = jnp.where(x_place == 0, tokens, other_tokens)
    second_tokens = jnp.where(x_place == 0, other_tokens, tokens)
    all_wide = jnp.concatenate([first_tokens, second_tokens], axis=0).astype(jnp.float32)
    scaled_all, _ = rms_parts(all_wide)
    normed_all = (scaled_all * gain_attn).astype(jnp.bfloat16)
    tokens_wide = tokens.astype(jnp.float32)
    _, inverse_one = rms_parts(tokens_wide)
    query_rot, keys_all, values_all, mixed_heads, totals, projected = attention_forward(
        place, normed_all, gathered, cosine, sine, segment_column, segment_low
    )
    projected, moved = together(projected, moved)
    moved_wide = gather_plane(jnp.stack(moved))
    middle = tokens_wide + projected
    scaled_two, inverse_two = rms_parts(middle)
    normed_two = scaled_two * gain_moe
    normed_low = normed_two.astype(jnp.bfloat16)
    router_logits = dot_rows(normed_low, router_low) + earlier_logits
    choice_ids = jnp.arange(choices, dtype=jnp.int32)
    one_hot = (routes[..., None] == choice_ids).astype(jnp.float32)
    chosen = jnp.sum(one_hot * router_logits[:, None, :], axis=-1)
    gate_probs = jax.nn.softmax(chosen, axis=-1)
    probs_low = gate_probs.astype(jnp.bfloat16)
    payload = jnp.concatenate(
        [
            normed_low,
            meta_rows([probs_low[:, 0], probs_low[:, 1]] + route_rows, model_width),
        ],
        axis=0,
    )
    payload, cotangent_blocks = together(payload, cotangent_blocks)
    token_blocks, (pick, back_slots) = gather_rows(
        payload, tuple(pick_slots(place, cotangent_blocks))
    )
    back_hidden, wide_full, down_full = prepare_experts(
        place, back_slots, own_wide, moved_wide, downs
    )
    (token_slots, hidden, mixed), grad_parts, out_parts = run_experts(
        place, token_blocks, pick, wide_full, down_full, back_hidden
    )

    grad_total, (wide_grads, down_near, down_core), out_parts = reduce_rows(
        grad_parts, weight_grads(place, token_slots, back_slots, hidden, mixed), out_parts
    )
    wide_sum = scatter_plane(wide_grads)
    down_core = across_core(down_core)
    down_far = add_low(down_near[1], down_core[1])
    out_other = across_x(out_parts[7])

    cotangent = cotangent_low.astype(jnp.float32)
    copies = jnp.sum(one_hot[..., EXPERTS + 1] * gate_probs, axis=-1)[:, None]
    const_probs = jnp.sum(one_hot[..., EXPERTS + 2 :] * gate_probs[..., None], axis=1)
    copy_dot = jnp.sum(cotangent * normed_two, axis=-1)
    const_dot = jnp.stack(
        [jnp.sum(cotangent * const_wide[i], axis=-1) for i in range(consts)], axis=-1
    )
    grad_rows = grad_total[:pos_count]
    expert_dot = jnp.stack(
        [grad_total[pos_count, i * pos_count : (i + 1) * pos_count] for i in range(2)], axis=-1
    )
    grad_gates = (
        expert_dot
        + one_hot[..., EXPERTS + 1] * copy_dot[:, None]
        + jnp.sum(one_hot[..., EXPERTS + 2 :] * const_dot[:, None, :], axis=-1)
    )
    grad_chosen = gate_probs * (
        grad_gates - jnp.sum(gate_probs * grad_gates, axis=-1, keepdims=True)
    )
    prior_logits_gradient = jnp.sum(one_hot * grad_chosen[..., None], axis=1)
    prior_low = prior_logits_gradient.astype(jnp.bfloat16)
    grad_normed_two = (
        grad_rows
        + copies * cotangent
        + dot_wide(prior_low, router_low)
    )
    router_part = dot_tall(normed_low, prior_low)
    const_part = dot_tall(cotangent_low, const_probs.astype(jnp.bfloat16))
    moe_gain_part = jnp.sum(grad_normed_two * scaled_two, axis=0)
    grad_middle = cotangent + rms_back(grad_normed_two * gain_moe, middle, inverse_two)
    grad_projected = grad_middle.astype(jnp.bfloat16)
    small_early = jnp.concatenate(
        [router_part, const_part, jnp.zeros_like(moe_gain_part)[:, None], moe_gain_part[:, None]],
        axis=1,
    )
    small_early = jnp.pad(small_early, ((0, 0), (0, 128 - small_count)))
    output_part = dot_tall(mixed_heads.astype(jnp.bfloat16), grad_projected)
    output_mine, output_other = split_core(output_part.astype(jnp.bfloat16), core_place)
    grad_projected, out_other, output_mine, output_other, small_early = together(
        grad_projected, out_other, output_mine, output_other, small_early
    )
    kept = [query_rot, keys_all, values_all, mixed_heads, totals]
    shared_args = [place, normed_all, gathered, cosine, sine, segment_column, segment_low, kept]
    out_total = add_low(out_parts[3], out_other)
    out_passed, out_other = along_z(out_total, -1), across_x(out_parts[6])
    output_other = across_core(output_other)
    nothing = jnp.zeros(normed_all.shape, jnp.float32)
    grads_a = attention_backward(*shared_args, grad_projected, nothing, 0, 3)
    grad_projected, grads_a, out_passed, out_other, output_other, wide_sum, down_far = together(
        grad_projected, grads_a, out_passed, out_other, output_other, wide_sum, down_far
    )
    down_far = across_y(down_far)
    moved_first = along_z(wide_sum[1], -1)
    out_total = add_all(out_parts[2], out_passed, out_other).astype(jnp.bfloat16)
    output_sum = add_low(output_mine, output_other)
    out_passed, out_other = along_z(out_total, -1), across_x(out_parts[5])
    other_a = across_core(grads_a[1])
    grads_b = attention_backward(*shared_args, grad_projected, grads_a[2], 3, 3)
    grads_b, out_passed, out_other, other_a, wide_sum, down_far, moved_first = together(
        grads_b, out_passed, out_other, other_a, wide_sum, down_far, moved_first
    )
    moved_third = along_z(wide_sum[3], -3)
    out_total = add_all(out_parts[1], out_passed, out_other).astype(jnp.bfloat16)
    out_passed, out_other = along_z(out_total, -1), across_x(out_parts[4])
    moved_back = [wide_sum[0], moved_first, along_z(wide_sum[2], -2), moved_third]
    other_b = across_core(grads_b[1])
    sum_a = add_low(grads_a[0], other_a)
    grad_normed_all = grads_b[2]
    gain_lane = choices + consts
    chosen_lane = jnp.where(jnp.arange(128) == gain_lane, 1.0, 0.0).astype(jnp.bfloat16)
    gain_part = dot_tall(
        (grad_normed_all * scaled_all).astype(jnp.bfloat16),
        jnp.broadcast_to(chosen_lane, (grad_normed_all.shape[0], 128)),
    )
    first_grad = grad_normed_all[:pos_count]
    grad_normed_one = jnp.where(x_place == 0, first_grad, grad_normed_all[pos_count:])
    first_grad = first_grad.astype(jnp.bfloat16)
    small_part = (small_early + gain_part).astype(jnp.bfloat16)
    small_mine, small_other = split_core(small_part, core_place)
    small_sum = add_low(small_mine, across_core(small_other))
    sum_b = add_low(grads_b[0], other_b)
    packed_parts = [part[kind] for kind in range(3) for part in (sum_a, sum_b)]
    packed_parts = packed_parts + [output_sum, small_sum]

    def finish(late):
        moved_back = late[0]
        return (
            *place_columns(moved_back, z_place),
            add_all(down_near[0], down_core[0], down_far),
            add_all(out_parts[0], *late[1]),
        )

    packed_grad, shared, (gate_grad, up_grad, down_grad, out_total) = reduce_packed(
        packed_parts,
        z_place,
        y_place,
        first_grad,
        (moved_back, (out_passed, out_other)),
        finish,
    )
    const_rows = sum(const_probs[:, i : i + 1] * const_wide[i : i + 1] for i in range(consts))
    layer_out = (
        middle
        + out_total
        + copies * normed_two
        + const_rows
    )
    grad_normed_one = grad_normed_one + shared.astype(jnp.float32)
    tokens_grad = grad_middle + rms_back(grad_normed_one * gain_attn, tokens_wide, inverse_one)
    output_grad = packed_grad[:, joint : joint + model_width]
    small_grad = packed_grad[:, joint + model_width :]
    query_grad, key_grad, value_grad = (
        packed_grad[:, i * model_width : (i + 1) * model_width] for i in range(3)
    )
    return (
        layer_out.astype(jnp.bfloat16)[None],
        tokens_grad[None],
        prior_logits_gradient[None],
        query_grad,
        key_grad,
        value_grad,
        output_grad,
        small_grad[:, :choices],
        small_grad[:, choices : choices + consts],
        small_grad[:, choices + consts],
        small_grad[:, choices + consts + 1],
        gate_grad,
        up_grad,
        down_grad,
    )


def solution(mesh):
    in_specs = (
        P("shard", "expert", None),
        P("shard", None),
        P("shard", "expert", None),
        P("shard", "expert", None),
        P("shard", "expert", None),
        P("shard", None),
        P("shard", None),
        P("shard", None),
        P("shard", None),
        P("shard", None),
        P("shard", None),
        P("shard"),
        P("shard"),
        P("expert", "shard", None),
        P("expert", "shard", None),
        P("expert", "shard", None),
    )
    out_specs = (
        P("shard", "expert", None),
        P("shard", "expert", None),
        P("shard", "expert", None),
        P("shard", None),
        P("shard", None),
        P("shard", None),
        P("shard", None),
        P("shard", None),
        P("shard", None),
        P("shard"),
        P("shard"),
        P("expert", "shard", None),
        P("expert", "shard", None),
        P("expert", "shard", None),
    )
    divided = mesh.shape["expert"] == PAIR and mesh.shape["shard"] == RING * PAIR * PAIR
    chosen = body_split if divided else body
    return jax.shard_map(chosen, mesh=mesh, in_specs=in_specs, out_specs=out_specs, check_vma=False)
```

```python
import math

import jax
import jax.numpy as jnp
from jax import lax
from jax.experimental import pallas as pl
from jax.experimental.pallas import tpu as pltpu
from jax.sharding import PartitionSpec as P

HEADS = 12
EXPERTS = 8
CAP = 64


norm_eps = 1e-06
masked_fill = -1e30


def rotary(values, positions, direction):
    dims_in = values.shape
    heads_view = values.reshape(dims_in[:-1] + (HEADS, dims_in[-1] // HEADS))
    half_size = heads_view.shape[-1] // 2
    frequency = jnp.exp(
        jnp.arange(half_size, dtype=jnp.float32) * (-2.0 * math.log(10000.0) / (2 * half_size))
    )
    angles = positions.astype(jnp.float32)[:, None] * frequency[None, :]
    cosine = jnp.cos(angles)[:, None, :]
    sine_part = direction * jnp.sin(angles)[:, None, :]
    first_half = heads_view[..., :half_size]
    second_half = heads_view[..., half_size:]
    turned = jnp.concatenate(
        [
            first_half * cosine - second_half * sine_part,
            second_half * cosine + first_half * sine_part,
        ],
        axis=-1,
    )
    return turned.reshape(dims_in)


def rms_parts(values):
    inverse = lax.rsqrt(jnp.mean(values * values, axis=-1, keepdims=True) + norm_eps)
    return (values * inverse, inverse)


def rms_back(grad_scaled, values, inverse):
    inner_mean = jnp.mean(grad_scaled * values, axis=-1, keepdims=True)
    return inverse * grad_scaled - values * inverse * inverse * inverse * inner_mean


def block_scores(query_heads, keys_all, segment_row, query_pos, query_seg, key_start, width_block):
    key_block = lax.dynamic_slice_in_dim(keys_all, key_start, width_block, 0)
    key_heads = key_block.reshape(width_block, HEADS, key_block.shape[-1] // HEADS)
    raw_scores = jnp.einsum(
        "qhd,khd->hqk", query_heads, key_heads, preferred_element_type=jnp.float32
    )
    scaled = raw_scores * key_heads.shape[-1] ** (-0.5)
    key_pos = key_start + jnp.arange(width_block, dtype=jnp.int32)
    key_seg = lax.dynamic_slice_in_dim(segment_row, key_start, width_block, 0)
    allowed = (key_pos[None, :] <= query_pos[:, None]) & (key_seg[None, :] == query_seg[:, None])
    return (scaled, allowed[None], key_heads)


def attend_forward(query_rot, keys_all, values_all, segment_row, offset, block_count, width_block):
    row_count = query_rot.shape[0]
    query_heads = query_rot.reshape(row_count, HEADS, -1)
    query_pos = offset + jnp.arange(row_count, dtype=jnp.int32)
    query_seg = lax.dynamic_slice_in_dim(segment_row, offset, row_count, 0)

    def gather_stats(number, state_pair):
        running_max, running_sum = state_pair
        scaled, allowed, key_heads = block_scores(
            query_heads,
            keys_all,
            segment_row,
            query_pos,
            query_seg,
            number * width_block,
            width_block,
        )
        masked = jnp.where(allowed, scaled, masked_fill)
        new_max = jnp.maximum(running_max, jnp.max(masked, axis=-1))
        exp_terms = jnp.where(allowed, jnp.exp(masked - new_max[..., None]), 0.0)
        return (new_max, running_sum * jnp.exp(running_max - new_max) + jnp.sum(exp_terms, axis=-1))

    start_max = jnp.full((HEADS, row_count), masked_fill, jnp.float32)
    start_sum = jnp.zeros((HEADS, row_count), jnp.float32)
    final_max, final_sum = lax.fori_loop(0, block_count, gather_stats, (start_max, start_sum))
    log_total = final_max + jnp.log(final_sum)

    def gather_output(number, running_out):
        key_start = number * width_block
        scaled, allowed, key_heads = block_scores(
            query_heads, keys_all, segment_row, query_pos, query_seg, key_start, width_block
        )
        weights = jnp.where(allowed, jnp.exp(scaled - log_total[..., None]), 0.0).astype(
            jnp.bfloat16
        )
        value_heads = lax.dynamic_slice_in_dim(values_all, key_start, width_block, 0).reshape(
            width_block, HEADS, -1
        )
        return running_out + jnp.einsum(
            "hqk,khd->qhd", weights, value_heads, preferred_element_type=jnp.float32
        )

    start_out = jnp.zeros((row_count, HEADS, query_heads.shape[-1]), jnp.float32)
    attention_output = lax.fori_loop(0, block_count, gather_output, start_out)
    return (attention_output.reshape(row_count, -1), log_total)


def attend_backward(
    query_rot,
    keys_all,
    values_all,
    segment_row,
    log_total,
    delta_sum,
    grad_low,
    offset,
    block_count,
    width_block,
):
    row_count = query_rot.shape[0]
    key_total = keys_all.shape[0]
    model_width = keys_all.shape[1]
    query_heads = query_rot.reshape(row_count, HEADS, -1)
    grad_heads = grad_low.reshape(row_count, HEADS, -1)
    query_pos = offset + jnp.arange(row_count, dtype=jnp.int32)
    query_seg = lax.dynamic_slice_in_dim(segment_row, offset, row_count, 0)
    score_scale = query_heads.shape[-1] ** (-0.5)

    def block_parts(number):
        key_start = number * width_block
        scaled, allowed, key_heads = block_scores(
            query_heads, keys_all, segment_row, query_pos, query_seg, key_start, width_block
        )
        prob_block = jnp.where(allowed, jnp.exp(scaled - log_total[..., None]), 0.0)
        value_heads = lax.dynamic_slice_in_dim(values_all, key_start, width_block, 0).reshape(
            width_block, HEADS, -1
        )
        grad_probs = jnp.einsum(
            "qhd,khd->hqk", grad_heads, value_heads, preferred_element_type=jnp.float32
        )
        grad_raw = (prob_block * (grad_probs - delta_sum[..., None]) * score_scale).astype(
            jnp.bfloat16
        )
        return (key_start, key_heads, prob_block, grad_raw)

    start_query = jnp.zeros((row_count, HEADS, query_heads.shape[-1]), jnp.float32)

    def accumulate(number, state_all):
        grad_query, grad_keys, grad_values = state_all
        key_start, key_heads, prob_block, grad_raw = block_parts(number)
        grad_query = grad_query + jnp.einsum(
            "hqk,khd->qhd", grad_raw, key_heads, preferred_element_type=jnp.float32
        )
        key_part = jnp.einsum(
            "hqk,qhd->khd", grad_raw, query_heads, preferred_element_type=jnp.float32
        )
        value_part = jnp.einsum(
            "hqk,qhd->khd",
            prob_block.astype(jnp.bfloat16),
            grad_heads,
            preferred_element_type=jnp.float32,
        )
        grad_keys = lax.dynamic_update_slice_in_dim(
            grad_keys, key_part.reshape(width_block, -1), key_start, 0
        )
        grad_values = lax.dynamic_update_slice_in_dim(
            grad_values, value_part.reshape(width_block, -1), key_start, 0
        )
        return (grad_query, grad_keys, grad_values)

    start_state = (
        start_query,
        jnp.zeros((key_total, model_width), jnp.float32),
        jnp.zeros((key_total, model_width), jnp.float32),
    )
    grad_query, grad_keys, grad_values = lax.fori_loop(0, block_count, accumulate, start_state)
    return (grad_query.reshape(row_count, -1), grad_keys, grad_values)


def body(
    tokens,
    segment_ids,
    routes,
    earlier_logits,
    out_cotangent,
    query_weight,
    key_weight,
    value_weight,
    output_weight,
    router_weight,
    const_vectors,
    attn_gain,
    moe_gain,
    gate_weight,
    up_weight,
    down_weight,
):
    (
        query_weight_wide,
        key_weight_wide,
        value_weight_wide,
        output_weight_wide,
        router_weight_wide,
        const_full,
        gain_attn,
        gain_moe,
    ) = (
        lax.all_gather(query_weight, "shard", axis=0, tiled=True),
        lax.all_gather(key_weight, "shard", axis=0, tiled=True),
        lax.all_gather(value_weight, "shard", axis=0, tiled=True),
        lax.all_gather(output_weight, "shard", axis=0, tiled=True),
        lax.all_gather(router_weight, "shard", axis=0, tiled=True),
        lax.all_gather(const_vectors, "shard", axis=0, tiled=True),
        lax.all_gather(attn_gain, "shard", axis=0, tiled=True),
        lax.all_gather(moe_gain, "shard", axis=0, tiled=True),
    )
    gate_full, up_full, down_full = (
        lax.all_gather(gate_weight, "shard", axis=1, tiled=True),
        lax.all_gather(up_weight, "shard", axis=1, tiled=True),
        lax.all_gather(down_weight, "shard", axis=1, tiled=True),
    )
    seq_count, pos_count, model_width = tokens.shape
    expert_pos = lax.axis_index("expert")
    offset = expert_pos * pos_count
    width_block = math.gcd(pos_count, 128)
    block_count = (expert_pos + 1) * (pos_count // width_block)
    positions = offset + jnp.arange(pos_count, dtype=jnp.int32)
    tokens_wide = tokens.astype(jnp.float32)
    scaled_one, inverse_one = rms_parts(tokens_wide)
    attn_gain_wide = gain_attn.astype(jnp.float32)
    normalized_first = (scaled_one * attn_gain_wide).astype(jnp.bfloat16)
    query_unrotated = jnp.einsum(
        "ibg,gv->ibv", normalized_first, query_weight_wide, preferred_element_type=jnp.float32
    )
    key_unrotated = jnp.einsum(
        "ibg,gv->ibv", normalized_first, key_weight_wide, preferred_element_type=jnp.float32
    )
    value_projected = jnp.einsum(
        "ibg,gv->ibv", normalized_first, value_weight_wide, preferred_element_type=jnp.float32
    )
    query_rot = rotary(query_unrotated, positions, 1.0).astype(jnp.bfloat16)
    key_rot = rotary(key_unrotated, positions, 1.0).astype(jnp.bfloat16)
    value_low = value_projected.astype(jnp.bfloat16)
    keys_all, values_all = (
        lax.all_gather(key_rot, "expert", axis=1, tiled=True),
        lax.all_gather(value_low, "expert", axis=1, tiled=True),
    )

    def forward_one(packed):
        return attend_forward(
            packed[0], packed[1], packed[2], packed[3], offset, block_count, width_block
        )

    attention_output, log_total = lax.map(
        forward_one, (query_rot, keys_all, values_all, segment_ids)
    )
    attention_output_narrow = attention_output.astype(jnp.bfloat16)
    projected_rows = jnp.einsum(
        "ibg,gv->ibv",
        attention_output_narrow,
        output_weight_wide,
        preferred_element_type=jnp.float32,
    )
    middle = tokens_wide + projected_rows
    scaled_two, inverse_two = rms_parts(middle)
    moe_gain_wide = gain_moe.astype(jnp.float32)
    normed_two = scaled_two * moe_gain_wide
    normalized_narrow = normed_two.astype(jnp.bfloat16)
    router_logits = (
        jnp.einsum(
            "ibg,gv->ibv", normalized_narrow, router_weight_wide, preferred_element_type=jnp.float32
        )
        + earlier_logits
    )
    chosen = jnp.take_along_axis(router_logits, routes, axis=-1)
    gate_probs = jax.nn.softmax(chosen, axis=-1)
    slot_count = seq_count * CAP
    route_entries = routes.reshape(seq_count, pos_count * 2)
    one_hot = (route_entries[..., None] == jnp.arange(EXPERTS, dtype=jnp.int32)).astype(jnp.int32)
    entry_ranks = jnp.cumsum(one_hot, axis=1) - one_hot
    slot_rank = jnp.sum(entry_ranks * one_hot, axis=-1)
    is_real = route_entries < EXPERTS
    destination = jnp.where(
        is_real,
        route_entries * slot_count
        + jnp.arange(seq_count, dtype=jnp.int32)[:, None] * CAP
        + slot_rank,
        EXPERTS * slot_count,
    ).reshape(-1)
    entry_rows = jnp.repeat(normalized_narrow.reshape(-1, model_width), 2, axis=0)
    send_rows = (
        jnp.zeros((EXPERTS * slot_count + 1, model_width), jnp.bfloat16)
        .at[destination]
        .set(entry_rows)[:-1]
        .reshape(EXPERTS, 1, slot_count, model_width)
    )
    received = lax.all_to_all(send_rows, "expert", split_axis=0, concat_axis=1, tiled=True)
    gate_pre = jnp.einsum("ensi,eif->ensf", received, gate_full, preferred_element_type=jnp.float32)
    up_pre = jnp.einsum("ensi,eif->ensf", received, up_full, preferred_element_type=jnp.float32)
    hidden = (jax.nn.silu(gate_pre) * up_pre).astype(jnp.bfloat16)
    result = jnp.einsum(
        "ensf,efi->ensi", hidden, down_full, preferred_element_type=jnp.float32
    ).astype(jnp.bfloat16)
    returned = lax.all_to_all(result, "expert", split_axis=1, concat_axis=0, tiled=True)
    zero_row = jnp.zeros((1, model_width), jnp.bfloat16)
    expert_vals = jnp.concatenate([returned.reshape(-1, model_width), zero_row], axis=0)[
        destination
    ].astype(jnp.float32)
    flat_routes = routes.reshape(-1)
    copy_rows = jnp.repeat(normed_two.reshape(-1, model_width), 2, axis=0)
    const_wide = const_full.astype(jnp.float32)
    is_copy = (flat_routes == EXPERTS + 1)[:, None]
    first_const = (flat_routes == EXPERTS + 2).astype(jnp.float32)[:, None]
    second_const = (flat_routes == EXPERTS + 3).astype(jnp.float32)[:, None]
    entry_vals = (
        expert_vals
        + jnp.where(is_copy, copy_rows, 0.0)
        + first_const * const_wide[:, 0][None, :]
        + second_const * const_wide[:, 1][None, :]
    )
    entry_vals = entry_vals.reshape(seq_count, pos_count, 2, model_width)
    layer_out = middle + jnp.sum(gate_probs[..., None] * entry_vals, axis=2)
    grad_mixed = out_cotangent.astype(jnp.float32)
    grad_gates = jnp.sum(grad_mixed[:, :, None, :] * entry_vals, axis=-1)
    grad_chosen = gate_probs * (
        grad_gates - jnp.sum(gate_probs * grad_gates, axis=-1, keepdims=True)
    )
    choice_ids = jnp.arange(EXPERTS + 4, dtype=jnp.int32)
    prior_logits_gradient = jnp.sum(
        (routes[..., None] == choice_ids).astype(jnp.float32) * grad_chosen[..., None], axis=2
    )
    grad_entries = (gate_probs[..., None] * grad_mixed[:, :, None, :]).reshape(-1, model_width)
    send_grads = (
        jnp.zeros((EXPERTS * slot_count + 1, model_width), jnp.bfloat16)
        .at[destination]
        .set(grad_entries.astype(jnp.bfloat16))[:-1]
        .reshape(EXPERTS, 1, slot_count, model_width)
    )
    owner_grads = lax.all_to_all(send_grads, "expert", split_axis=0, concat_axis=1, tiled=True)
    sigmoid_gate = jax.nn.sigmoid(gate_pre)
    silu_gate = gate_pre * sigmoid_gate
    hidden_back = (silu_gate * up_pre).astype(jnp.bfloat16)
    grad_hidden = jnp.einsum(
        "ensd,efd->ensf", owner_grads, down_full, preferred_element_type=jnp.float32
    )
    grad_gate_pre = (
        grad_hidden * up_pre * sigmoid_gate * (1.0 + gate_pre * (1.0 - sigmoid_gate))
    ).astype(jnp.bfloat16)
    grad_up_pre = (grad_hidden * silu_gate).astype(jnp.bfloat16)
    down_part = jnp.einsum(
        "ensf,ensd->efd", hidden_back, owner_grads, preferred_element_type=jnp.float32
    )
    gate_part = jnp.einsum(
        "ensi,ensf->eif", received, grad_gate_pre, preferred_element_type=jnp.float32
    )
    up_part = jnp.einsum(
        "ensi,ensf->eif", received, grad_up_pre, preferred_element_type=jnp.float32
    )
    grad_rows = (
        jnp.einsum("ensf,eif->ensi", grad_gate_pre, gate_full, preferred_element_type=jnp.float32)
        + jnp.einsum("ensf,eif->ensi", grad_up_pre, up_full, preferred_element_type=jnp.float32)
    ).astype(jnp.bfloat16)
    rows_back = lax.all_to_all(grad_rows, "expert", split_axis=1, concat_axis=0, tiled=True)
    gate_grad, up_grad, down_grad = (
        lax.psum_scatter(
            gate_part.astype(jnp.bfloat16), "shard", scatter_dimension=1, tiled=True
        ).astype(jnp.float32),
        lax.psum_scatter(
            up_part.astype(jnp.bfloat16), "shard", scatter_dimension=1, tiled=True
        ).astype(jnp.float32),
        lax.psum_scatter(
            down_part.astype(jnp.bfloat16), "shard", scatter_dimension=1, tiled=True
        ).astype(jnp.float32),
    )
    grad_row_entries = jnp.concatenate([rows_back.reshape(-1, model_width), zero_row], axis=0)[
        destination
    ].astype(jnp.float32)
    grad_copy = jnp.where(is_copy, grad_entries, 0.0)
    router_widened = router_weight_wide.astype(jnp.float32)
    grad_normed_two = jnp.sum(
        (grad_row_entries + grad_copy).reshape(seq_count, pos_count, 2, model_width), axis=2
    ) + jnp.einsum(
        "hwk,ok->hwo", prior_logits_gradient, router_widened, precision=lax.Precision.HIGHEST
    )
    router_part = jnp.einsum(
        "vrx,vrb->xb",
        normalized_narrow.astype(jnp.float32),
        prior_logits_gradient,
        precision=lax.Precision.HIGHEST,
    )
    const_part = jnp.stack(
        [jnp.sum(first_const * grad_entries, axis=0), jnp.sum(second_const * grad_entries, axis=0)],
        axis=-1,
    )
    moe_gain_part = jnp.sum(grad_normed_two * scaled_two, axis=(0, 1))
    grad_middle = grad_mixed + rms_back(grad_normed_two * moe_gain_wide, middle, inverse_two)
    gradient_projected = grad_middle.astype(jnp.bfloat16)
    output_part = jnp.einsum(
        "vrx,vrb->xb",
        attention_output_narrow,
        gradient_projected,
        preferred_element_type=jnp.float32,
    )
    grad_attended = jnp.einsum(
        "hwk,ok->hwo", gradient_projected, output_weight_wide, preferred_element_type=jnp.float32
    ).astype(jnp.bfloat16)
    delta_rows = jnp.sum(
        (grad_attended.astype(jnp.float32) * attention_output).reshape(
            seq_count, pos_count, HEADS, -1
        ),
        axis=-1,
    )
    delta_sum = jnp.transpose(delta_rows, (0, 2, 1))

    def backward_one(packed):
        return attend_backward(
            packed[0],
            packed[1],
            packed[2],
            packed[3],
            packed[4],
            packed[5],
            packed[6],
            offset,
            block_count,
            width_block,
        )

    grad_query_rot, grad_keys_all, grad_values_all = lax.map(
        backward_one,
        (query_rot, keys_all, values_all, segment_ids, log_total, delta_sum, grad_attended),
    )
    grad_keys, grad_values = (
        lax.psum_scatter(
            grad_keys_all.astype(jnp.bfloat16), "expert", scatter_dimension=1, tiled=True
        ).astype(jnp.float32),
        lax.psum_scatter(
            grad_values_all.astype(jnp.bfloat16), "expert", scatter_dimension=1, tiled=True
        ).astype(jnp.float32),
    )
    gradient_query_unrotated = rotary(grad_query_rot, positions, -1.0).astype(jnp.bfloat16)
    gradient_key_unrotated = rotary(grad_keys, positions, -1.0).astype(jnp.bfloat16)
    gradient_value_narrow = grad_values.astype(jnp.bfloat16)
    query_part = jnp.einsum(
        "vrx,vrb->xb",
        normalized_first,
        gradient_query_unrotated,
        preferred_element_type=jnp.float32,
    )
    key_part = jnp.einsum(
        "vrx,vrb->xb", normalized_first, gradient_key_unrotated, preferred_element_type=jnp.float32
    )
    value_part = jnp.einsum(
        "vrx,vrb->xb", normalized_first, gradient_value_narrow, preferred_element_type=jnp.float32
    )
    grad_normed_one = jnp.einsum(
        "hwk,ok->hwo",
        gradient_query_unrotated,
        query_weight_wide,
        preferred_element_type=jnp.float32,
    )
    grad_normed_one = grad_normed_one + jnp.einsum(
        "hwk,ok->hwo", gradient_key_unrotated, key_weight_wide, preferred_element_type=jnp.float32
    )
    grad_normed_one = grad_normed_one + jnp.einsum(
        "hwk,ok->hwo", gradient_value_narrow, value_weight_wide, preferred_element_type=jnp.float32
    )
    attn_gain_part = jnp.sum(grad_normed_one * scaled_one, axis=(0, 1))
    tokens_grad = grad_middle + rms_back(grad_normed_one * attn_gain_wide, tokens_wide, inverse_one)
    layer_parts = (
        lax.psum_scatter(
            query_part.astype(jnp.bfloat16), "shard", scatter_dimension=0, tiled=True
        ).astype(jnp.float32),
        lax.psum_scatter(
            key_part.astype(jnp.bfloat16), "shard", scatter_dimension=0, tiled=True
        ).astype(jnp.float32),
        lax.psum_scatter(
            value_part.astype(jnp.bfloat16), "shard", scatter_dimension=0, tiled=True
        ).astype(jnp.float32),
        lax.psum_scatter(
            output_part.astype(jnp.bfloat16), "shard", scatter_dimension=0, tiled=True
        ).astype(jnp.float32),
        lax.psum_scatter(
            router_part.astype(jnp.bfloat16), "shard", scatter_dimension=0, tiled=True
        ).astype(jnp.float32),
        lax.psum_scatter(
            const_part.astype(jnp.bfloat16), "shard", scatter_dimension=0, tiled=True
        ).astype(jnp.float32),
        lax.psum_scatter(
            attn_gain_part.astype(jnp.bfloat16), "shard", scatter_dimension=0, tiled=True
        ).astype(jnp.float32),
        lax.psum_scatter(
            moe_gain_part.astype(jnp.bfloat16), "shard", scatter_dimension=0, tiled=True
        ).astype(jnp.float32),
    )
    layer_grads = (
        lax.psum(layer_parts[0].astype(jnp.bfloat16), "expert").astype(jnp.float32),
        lax.psum(layer_parts[1].astype(jnp.bfloat16), "expert").astype(jnp.float32),
        lax.psum(layer_parts[2].astype(jnp.bfloat16), "expert").astype(jnp.float32),
        lax.psum(layer_parts[3].astype(jnp.bfloat16), "expert").astype(jnp.float32),
        lax.psum(layer_parts[4].astype(jnp.bfloat16), "expert").astype(jnp.float32),
        lax.psum(layer_parts[5].astype(jnp.bfloat16), "expert").astype(jnp.float32),
        lax.psum(layer_parts[6].astype(jnp.bfloat16), "expert").astype(jnp.float32),
        lax.psum(layer_parts[7].astype(jnp.bfloat16), "expert").astype(jnp.float32),
    )
    return (
        layer_out.astype(jnp.bfloat16),
        tokens_grad,
        prior_logits_gradient,
        layer_grads[0],
        layer_grads[1],
        layer_grads[2],
        layer_grads[3],
        layer_grads[4],
        layer_grads[5],
        layer_grads[6],
        layer_grads[7],
        gate_grad,
        up_grad,
        down_grad,
    )


RING = 4
PAIR = 2
LOCAL = 4
META = 16


def z_pairs(step):
    lines = PAIR * PAIR
    return [
        (z * lines + rest, (z + step) % RING * lines + rest)
        for z in range(RING)
        for rest in range(lines)
    ]


def along_z(values, step):
    return lax.ppermute(values, "shard", z_pairs(step))


def across_y(values):
    return lax.ppermute(values, "shard", [(s, s ^ PAIR) for s in range(RING * PAIR * PAIR)])


def across_core(values):
    return lax.ppermute(values, "shard", [(s, s ^ 1) for s in range(RING * PAIR * PAIR)])


def across_x(values):
    return lax.ppermute(values, "expert", [(0, 1), (1, 0)])


def together(*values):
    return lax.optimization_barrier(values)


def gather_rows(own, beside=()):
    ring, crossed = [own], []
    for step in range(RING - 1):
        following, other = along_z(ring[-1], 1), across_x(ring[-1])
        if step == 1 and beside:
            following, other, beside = together(following, other, beside)
        else:
            following, other = together(following, other)
        ring.append(following)
        crossed.append(other)
    return ring + crossed + [across_x(ring[-1])], beside


def add_all(*values):
    return sum(value.astype(jnp.float32) for value in values)


def reduce_rows(parts, beside, late):
    other, beside = together(across_x(parts[2 * RING - 1]), beside)
    total = add_all(parts[RING - 1], other)
    for step in reversed(range(RING - 1)):
        passed, other = along_z(total.astype(jnp.bfloat16), -1), across_x(parts[RING + step])
        if step == 1:
            passed, other, late = together(passed, other, late)
        else:
            passed, other = together(passed, other)
        total = add_all(parts[step], passed, other)
    return total, beside, late


def plane_groups():
    lines = PAIR * PAIR
    return [[z * lines + i for i in range(lines)] for z in range(RING)]


def scatter_plane(part):
    return lax.psum_scatter(
        part, "shard", scatter_dimension=0, axis_index_groups=plane_groups(), tiled=False
    )


def gather_plane(part):
    return lax.all_gather(part, "shard", axis=0, axis_index_groups=plane_groups(), tiled=False)


def split_core(part, core_place):
    rows, width = part.shape
    part = part.reshape(RING, PAIR, PAIR, rows // (RING * PAIR * PAIR), width)
    mine = jnp.where(core_place == 0, part[:, :, 0], part[:, :, 1])
    other = jnp.where(core_place == 0, part[:, :, 1], part[:, :, 0])
    return mine, other


def reduce_packed(parts, z_place, y_place, first_grad, late, finish):
    total = None
    for step in reversed(range(RING)):
        owner = lax.rem(z_place - step + RING, RING)
        blocks = [lax.dynamic_index_in_dim(part, owner, 0, keepdims=False) for part in parts]
        block = jnp.concatenate(blocks, axis=-1)
        other = across_y(jnp.where(y_place == 0, block[1], block[0]))
        mine = jnp.where(y_place == 0, block[0], block[1])
        if total is None:
            other, first_grad, passed = together(other, first_grad, late[1])
            late = (late[0], passed)
            here = add_all(mine, other)
            shared = lax.ppermute(first_grad, "expert", [(1, 0)])
        else:
            passed, other = together(along_z(total, -1), other)
            if step == 1:
                passed, shared, late = together(passed, shared, late)
            here = add_all(mine, passed, other)
        total = here.astype(jnp.bfloat16)
    total, late = together(total, late)
    return add_all(total, across_x(total)), shared, finish(late)


def meta_rows(rows, width):
    filled = jnp.concatenate(rows, axis=-1).reshape(len(rows) // 2, -1)
    return jnp.pad(filled, ((0, META - filled.shape[0]), (0, width - filled.shape[1]))).astype(
        jnp.bfloat16
    )


def dot_rows(left, right):
    return lax.dot_general(left, right, (((1,), (0,)), ((), ())), preferred_element_type=jnp.float32)


def dot_wide(left, right):
    return lax.dot_general(left, right, (((1,), (1,)), ((), ())), preferred_element_type=jnp.float32)


def dot_tall(left, right):
    return lax.dot_general(left, right, (((0,), (0,)), ((), ())), preferred_element_type=jnp.float32)


def pick_kernel(place, *refs):
    block_count = RING * PAIR
    grads = refs[:block_count]
    pick_ref, slot_ref, stage = refs[block_count:]
    rows = pick_ref.shape[2]
    later = lax.broadcasted_iota(jnp.int32, (rows, rows), 1)
    earlier = lax.broadcasted_iota(jnp.int32, (rows, rows), 0)
    before = jnp.where(earlier < later, 1.0, 0.0).astype(jnp.bfloat16)
    wanted = (lax.broadcasted_iota(jnp.int32, (8, rows), 0) + place[0] * LOCAL).astype(
        jnp.float32
    )
    inside = lax.broadcasted_iota(jnp.int32, (8, rows), 0) < LOCAL
    ranks = lax.broadcasted_iota(jnp.int32, (CAP, rows), 0).astype(jnp.float32)
    for block in range(block_count):
        stage[block] = grads[block][...]

    def fill(block, nothing):
        meta = stage[block, rows : rows + META, :].astype(jnp.float32)
        first = meta[1:2, :rows]
        second = meta[1:2, rows : 2 * rows]
        named = jnp.where(((first == wanted) | (second == wanted)) & inside, 1.0, 0.0)
        rank = dot_rows(named.astype(jnp.bfloat16), before)
        pieces = []
        for expert in range(LOCAL):
            hit = (rank[expert : expert + 1] == ranks) & (named[expert : expert + 1] > 0.5)
            pieces.append(jnp.where(hit, 1.0, 0.0))
        pick = jnp.concatenate(pieces, axis=0).astype(jnp.bfloat16)
        pick_ref[block] = pick
        slot_ref[block] = dot_rows(pick, stage[block, :rows, :]).astype(jnp.bfloat16)
        return nothing

    lax.fori_loop(0, block_count, fill, 0)


def prepare_kernel(place, slot_ref, own_ref, moved_ref, *refs):
    downs = refs[:4]
    back_ref, wide_ref, down_ref = refs[4:]
    number = pl.program_id(0)
    block_count = slot_ref.shape[0]
    half = wide_ref.shape[2] // 2
    depth = own_ref.shape[3]
    for line in range(PAIR * PAIR):
        for step in range(RING):
            owner = lax.rem(place[1] - step + RING, RING) * (PAIR * PAIR) + line
            start = pl.multiple_of(owner * depth, 16)
            for side in range(2):
                piece = own_ref[line, side, 0] if step == 0 else moved_ref[line, step - 1, side, 0]
                wide_ref[0, pl.ds(start, depth), side * half : (side + 1) * half] = piece
        part = downs[line]
        deep = part.shape[1]
        source = (place[2] ^ (line % PAIR)) * PAIR + (place[3] ^ (line // PAIR))
        down_ref[0, pl.ds(pl.multiple_of(source * deep, 16), deep), :] = part[0]
    width = slot_ref.shape[2]
    mine = slot_ref[:, pl.ds(pl.multiple_of(number * CAP, CAP), CAP), :]
    back_ref[0] = dot_wide(mine.reshape(block_count * CAP, width), down_ref[0])


def expert_kernel(place, *refs):
    block_count = RING * PAIR
    tokens = refs[:block_count]
    pick_ref, wide_ref, down_ref, back_ref = refs[block_count : block_count + 4]
    rest = refs[block_count + 4 :]
    slot_ref, hidden_ref, mixed_ref = rest[:3]
    grad_refs = rest[3 : 3 + block_count]
    out_refs = rest[3 + block_count : 3 + 2 * block_count]
    out_slots, grad_slots, gate_grads, stage, product_ref, chance_ref = rest[3 + 2 * block_count :]
    number = pl.program_id(0)
    rows = pick_ref.shape[2]
    width = slot_ref.shape[2]
    half = wide_ref.shape[2] // 2

    @pl.when(number == 0)
    def _():
        gate_grads[...] = jnp.zeros_like(gate_grads)
        for block in range(block_count):
            stage[block] = tokens[block][...]

        def gather(block, nothing):
            slot_ref[block] = dot_rows(pick_ref[block], stage[block, :rows, :]).astype(
                jnp.bfloat16
            )
            return nothing

        lax.fori_loop(0, block_count, gather, 0)

    span = pl.ds(pl.multiple_of(number * CAP, CAP), CAP)
    mine = slot_ref[:, span, :].reshape(block_count * CAP, width)
    both = dot_rows(mine, wide_ref[0])
    gate = both[:, :half]
    up = both[:, half:]
    sigmoid = 1.0 / (1.0 + jnp.exp(-gate))
    silu = gate * sigmoid
    hidden = silu * up
    back = back_ref[0]
    expert_id = (number + place[0] * LOCAL).astype(jnp.float32)
    product_ref[...] = jnp.sum(hidden * back, axis=1, keepdims=True)

    def spread_block(block, nothing):
        meta = stage[block, rows : rows + META, :].astype(jnp.float32)
        first = jnp.where(meta[1:2, :rows] == expert_id, 1.0, 0.0)
        second = jnp.where(meta[1:2, rows : 2 * rows] == expert_id, 1.0, 0.0)
        pick = pick_ref[block, span, :].astype(jnp.float32)
        chance = first * meta[0:1, :rows] + second * meta[0:1, rows : 2 * rows]
        slots = pl.ds(pl.multiple_of(block * CAP, CAP), CAP)
        chance_ref[slots, :] = jnp.sum(pick * chance, axis=1, keepdims=True)
        spread = jnp.sum(pick * product_ref[slots, :], axis=0, keepdims=True)
        gate_grads[block, 0:1, :rows] += first * spread
        gate_grads[block, 0:1, rows : 2 * rows] += second * spread
        return nothing

    lax.fori_loop(0, block_count, spread_block, 0, unroll=4)
    chance = chance_ref[...]
    back = back * chance
    weighted = (hidden * chance).astype(jnp.bfloat16)
    grad_gate = back * up * sigmoid * (1.0 + gate * (1.0 - sigmoid))
    grad_up = back * silu
    mixed = jnp.concatenate([grad_gate, grad_up], axis=1).astype(jnp.bfloat16)
    hidden_ref[0] = weighted
    mixed_ref[0] = mixed
    out_part = dot_rows(weighted, down_ref[0]).astype(jnp.bfloat16)
    out_slots[:, span, :] = out_part.reshape(block_count, CAP, width)
    grad_part = dot_wide(mixed, wide_ref[0]).astype(jnp.bfloat16)
    grad_slots[:, span, :] = grad_part.reshape(block_count, CAP, width)

    @pl.when(number == LOCAL - 1)
    def _():
        def scatter(block, nothing):
            pick = pick_ref[block]
            grad_slots[block] = dot_tall(pick, grad_slots[block]).astype(jnp.bfloat16)
            out_slots[block] = dot_tall(pick, out_slots[block]).astype(jnp.bfloat16)
            return nothing

        lax.fori_loop(0, block_count, scatter, 0)
        for block in range(block_count):
            grad_refs[block][:rows, :] = grad_slots[block]
            grad_refs[block][rows : rows + META, :] = gate_grads[block].astype(jnp.bfloat16)
            out_refs[block][...] = out_slots[block]


def weight_grad_kernel(place, *refs):
    slot_ref, back_ref, hidden_ref, mixed_ref, wide_ref, near_ref, core_ref, wide_sum = refs
    number = pl.program_id(0)
    block_count, _, width = slot_ref.shape
    span = pl.ds(pl.multiple_of(number * CAP, CAP), CAP)
    rows = slot_ref[:, span, :].reshape(block_count * CAP, width)
    wide_sum[...] = dot_tall(rows, mixed_ref[0])
    grads = back_ref[:, span, :].reshape(block_count * CAP, width)
    half = wide_sum.shape[1] // 2
    deep = near_ref.shape[2]
    depth = wide_ref.shape[4]
    for line in range(PAIR * PAIR):
        for step in range(RING):
            owner = lax.rem(place[1] - step + RING, RING) * (PAIR * PAIR) + line
            part = wide_sum[pl.ds(pl.multiple_of(owner * depth, 16), depth), :]
            wide_ref[line, step, 0, 0] = part[:, :half].astype(jnp.bfloat16)
            wide_ref[line, step, 1, 0] = part[:, half:].astype(jnp.bfloat16)
        side, core = line % PAIR, line // PAIR
        source = (place[2] ^ side) * PAIR + (place[3] ^ core)
        columns = hidden_ref[0, :, pl.ds(pl.multiple_of(source * deep, deep), deep)]
        target = core_ref if core else near_ref
        target[side, 0] = dot_tall(columns, grads).astype(jnp.bfloat16)


def busy(microseconds):
    return pl.CostEstimate(
        flops=microseconds * 400_000_000,
        transcendentals=0,
        bytes_accessed=microseconds * 3_000_000,
    )


def whole(shape):
    return pl.BlockSpec(shape, lambda number, place: (0,) * len(shape))


def by_expert(shape, axis=0):
    return pl.BlockSpec(
        shape,
        lambda number, place: tuple(number if d == axis else 0 for d in range(len(shape))),
    )


def pick_slots(place, grads):
    padded, width = grads[0].shape
    rows = padded - META
    blocks = len(grads)
    shapes = [(blocks, LOCAL * CAP, rows), (blocks, LOCAL * CAP, width)]
    return pl.pallas_call(
        pick_kernel,
        name="pick_slots",
        cost_estimate=busy(4),
        out_shape=[jax.ShapeDtypeStruct(shape, jnp.bfloat16) for shape in shapes],
        grid_spec=pltpu.PrefetchScalarGridSpec(
            num_scalar_prefetch=1,
            grid=(1,),
            in_specs=[whole(g.shape) for g in grads],
            out_specs=[whole(shape) for shape in shapes],
            scratch_shapes=[pltpu.VMEM((blocks, padded, width), jnp.bfloat16)],
        ),
    )(place, *grads)


def prepare_experts(place, slot_rows, own, moved, downs):
    blocks, _, width = slot_rows.shape
    lines, _, local, depth, span = own.shape
    deep = downs[0].shape[1]
    model = depth * RING * lines
    slots = blocks * CAP
    shapes = [
        ((local, slots, span), jnp.float32),
        ((local, model, 2 * span), jnp.bfloat16),
        ((local, deep * lines, width), jnp.bfloat16),
    ]
    return pl.pallas_call(
        prepare_kernel,
        name="prepare_experts",
        cost_estimate=busy(10),
        out_shape=[jax.ShapeDtypeStruct(s, d) for s, d in shapes],
        grid_spec=pltpu.PrefetchScalarGridSpec(
            num_scalar_prefetch=1,
            grid=(local,),
            in_specs=[
                whole(slot_rows.shape),
                by_expert((lines, 2, 1, depth, span), 2),
                by_expert((lines, RING - 1, 2, 1, depth, span), 3),
            ]
            + [by_expert((1, deep, width))] * 4,
            out_specs=[
                by_expert((1, slots, span)),
                by_expert((1, model, 2 * span)),
                by_expert((1, deep * lines, width)),
            ],
        ),
    )(place, slot_rows, own, moved, *downs)


def run_experts(place, tokens, pick, wide, down, back):
    padded, width = tokens[0].shape
    rows = padded - META
    blocks = len(tokens)
    local, model, span2 = wide.shape
    span = span2 // 2
    slots = blocks * CAP
    shapes = [
        ((blocks, local * CAP, width), jnp.bfloat16),
        ((local, slots, span), jnp.bfloat16),
        ((local, slots, span2), jnp.bfloat16),
    ]
    shapes = shapes + [((padded, width), jnp.bfloat16)] * blocks
    shapes = shapes + [((rows, width), jnp.bfloat16)] * blocks
    results = pl.pallas_call(
        expert_kernel,
        name="run_experts",
        cost_estimate=busy(22),
        out_shape=[jax.ShapeDtypeStruct(s, d) for s, d in shapes],
        grid_spec=pltpu.PrefetchScalarGridSpec(
            num_scalar_prefetch=1,
            grid=(local,),
            in_specs=[whole(t.shape) for t in tokens]
            + [
                whole(pick.shape),
                by_expert((1, model, span2)),
                by_expert((1, span, width)),
                by_expert((1, slots, span)),
            ],
            out_specs=[
                whole(shapes[0][0]),
                by_expert((1, slots, span)),
                by_expert((1, slots, span2)),
            ]
            + [whole(s) for s, _ in shapes[3:]],
            scratch_shapes=[
                pltpu.VMEM((blocks, local * CAP, width), jnp.bfloat16),
                pltpu.VMEM((blocks, local * CAP, width), jnp.bfloat16),
                pltpu.VMEM((blocks, META, width), jnp.float32),
                pltpu.VMEM((blocks, padded, width), jnp.bfloat16),
                pltpu.VMEM((slots, 1), jnp.float32),
                pltpu.VMEM((slots, 1), jnp.float32),
            ],
        ),
    )(place, *tokens, pick, wide, down, back)
    return results[:3], results[3 : 3 + blocks], results[3 + blocks :]


def weight_grads(place, slots, backs, hidden, mixed):
    blocks, total, width = slots.shape
    local, rows, span = hidden.shape
    lines = PAIR * PAIR
    depth = width // (RING * lines)
    deep = span // lines
    return pl.pallas_call(
        weight_grad_kernel,
        name="weight_grads",
        cost_estimate=busy(12),
        out_shape=[
            jax.ShapeDtypeStruct((lines, RING, 2, local, depth, span), jnp.bfloat16),
            jax.ShapeDtypeStruct((PAIR, local, deep, width), jnp.bfloat16),
            jax.ShapeDtypeStruct((PAIR, local, deep, width), jnp.bfloat16),
        ],
        grid_spec=pltpu.PrefetchScalarGridSpec(
            num_scalar_prefetch=1,
            grid=(local,),
            in_specs=[
                whole(slots.shape),
                whole(backs.shape),
                by_expert((1, rows, span)),
                by_expert((1, rows, 2 * span)),
            ],
            out_specs=[
                by_expert((lines, RING, 2, 1, depth, span), 3),
                by_expert((PAIR, 1, deep, width), 1),
                by_expert((PAIR, 1, deep, width), 1),
            ],
            scratch_shapes=[pltpu.VMEM((width, 2 * span), jnp.float32)],
        ),
    )(place, slots, backs, hidden, mixed)


def add_low(left, right):
    return (left.astype(jnp.float32) + right.astype(jnp.float32)).astype(jnp.bfloat16)


def turn_pairs(values, cosine, sine):
    half = values.shape[1] // 4
    lane = lax.rem(lax.broadcasted_iota(jnp.int32, values.shape, 1), 2 * half)
    swapped = jnp.where(
        lane < half,
        pltpu.roll(values, 3 * half, 1),
        pltpu.roll(values, half, 1),
    )
    return values * cosine + swapped * sine


def mask_bias(x_place, rows, columns, row_segments, column_segments):
    row = lax.broadcasted_iota(jnp.int32, (rows, columns), 0) + x_place * rows
    column = lax.broadcasted_iota(jnp.int32, (rows, columns), 1)
    return jnp.where((column <= row) & (row_segments == column_segments), 0.0, masked_fill)


def attention_forward_kernel(
    place,
    normed_ref,
    query_weight,
    key_weight,
    value_weight,
    output_weight,
    cosine_ref,
    sine_ref,
    column_ref,
    row_ref,
    query_ref,
    key_ref,
    value_ref,
    mixed_ref,
    total_ref,
    result_ref,
    bias_ref,
):
    rows, columns = bias_ref.shape
    own = pl.ds(pl.multiple_of(place[0] * rows, rows), rows)

    @pl.when(pl.program_id(0) == 0)
    def _():
        bias_ref[...] = mask_bias(place[0], rows, columns, column_ref[own, :], row_ref[...])
        result_ref[...] = jnp.zeros_like(result_ref)

    normed = normed_ref[...]
    query = dot_rows(normed_ref[own, :], query_weight[...])
    query = turn_pairs(query, cosine_ref[own, :], sine_ref[own, :]).astype(jnp.bfloat16)
    key = turn_pairs(dot_rows(normed, key_weight[...]), cosine_ref[...], sine_ref[...])
    key = key.astype(jnp.bfloat16)
    value = dot_rows(normed, value_weight[...]).astype(jnp.bfloat16)
    query_ref[...] = query
    key_ref[...] = key
    value_ref[...] = value
    width = query.shape[1]
    low = lax.broadcasted_iota(jnp.int32, (rows, width), 1) < width // 2
    scale = (width // 2) ** (-0.5)
    sides = []
    for side in range(2):
        keep = low if side == 0 else jnp.logical_not(low)
        scores = dot_wide(jnp.where(keep, query, 0), key) * scale + bias_ref[...]
        top = jnp.max(scores, axis=1, keepdims=True)
        terms = jnp.exp(scores - top)
        count = jnp.sum(terms, axis=1, keepdims=True)
        probs = (terms * (1.0 / count)).astype(jnp.bfloat16)
        sides.append((dot_rows(probs, value), top + jnp.log(count)))
    mixed = jnp.where(low, sides[0][0], sides[1][0])
    mixed_ref[...] = mixed
    total_ref[0] = jnp.where(low, sides[0][1], sides[1][1])
    result_ref[...] += dot_rows(mixed.astype(jnp.bfloat16), output_weight[...])


def attention_backward_kernel(
    place,
    normed_ref,
    query_weight,
    key_weight,
    value_weight,
    output_weight,
    cosine_ref,
    sine_ref,
    column_ref,
    row_ref,
    query_ref,
    key_ref,
    value_ref,
    mixed_ref,
    total_ref,
    grad_ref,
    carried_ref,
    weight_mine,
    weight_other,
    result_ref,
    bias_ref,
    weight_ref,
):
    rows, columns = bias_ref.shape
    own = pl.ds(pl.multiple_of(place[0] * rows, rows), rows)

    @pl.when(pl.program_id(0) == 0)
    def _():
        bias_ref[...] = mask_bias(place[0], rows, columns, column_ref[own, :], row_ref[...])
        result_ref[...] = carried_ref[...]

    normed = normed_ref[...]
    grad = grad_ref[...]
    query, key, value, mixed = query_ref[...], key_ref[...], value_ref[...], mixed_ref[...]
    attended = dot_wide(grad, output_weight[...]).astype(jnp.bfloat16)
    product = attended.astype(jnp.float32) * mixed
    width = query.shape[1]
    low = lax.broadcasted_iota(jnp.int32, (rows, width), 1) < width // 2
    low_keys = lax.broadcasted_iota(jnp.int32, (columns, width), 1) < width // 2
    scale = (width // 2) ** (-0.5)
    sides = []
    for side in range(2):
        keep = low if side == 0 else jnp.logical_not(low)
        start = side * (width // 2)
        delta = jnp.sum(jnp.where(keep, product, 0.0), axis=1, keepdims=True)
        scores = dot_wide(jnp.where(keep, query, 0), key) * scale + bias_ref[...]
        probs = jnp.exp(scores - total_ref[0, :, start : start + 1])
        grad_probs = dot_wide(jnp.where(keep, attended, 0), value)
        grad_scores = (probs * (grad_probs - delta) * scale).astype(jnp.bfloat16)
        sides.append(
            (
                dot_rows(grad_scores, key),
                dot_tall(grad_scores, query),
                dot_tall(probs.astype(jnp.bfloat16), attended),
            )
        )
    grad_query = jnp.where(low, sides[0][0], sides[1][0])
    grad_key = jnp.where(low_keys, sides[0][1], sides[1][1])
    grad_value = jnp.where(low_keys, sides[0][2], sides[1][2]).astype(jnp.bfloat16)
    grad_query = turn_pairs(grad_query, cosine_ref[own, :], -sine_ref[own, :])
    grad_query = grad_query.astype(jnp.bfloat16)
    grad_key = turn_pairs(grad_key, cosine_ref[...], -sine_ref[...]).astype(jnp.bfloat16)
    result_ref[...] += dot_wide(grad_key, key_weight[...]) + dot_wide(
        grad_value, value_weight[...]
    )
    result_ref[own, :] += dot_wide(grad_query, query_weight[...])
    weight_ref[:, :width] = dot_tall(normed_ref[own, :], grad_query)
    weight_ref[:, width : 2 * width] = dot_tall(normed, grad_key)
    weight_ref[:, 2 * width :] = dot_tall(normed, grad_value)
    depth = weight_mine.shape[3]
    for z in range(RING):
        for y in range(PAIR):
            pair = (z * PAIR + y) * PAIR
            near = pl.ds(pl.multiple_of((pair + place[3]) * depth, 16), depth)
            far = pl.ds(pl.multiple_of((pair + 1 - place[3]) * depth, 16), depth)
            for kind in range(3):
                span = slice(kind * width, (kind + 1) * width)
                weight_mine[kind, z, y] = weight_ref[near, span].astype(jnp.bfloat16)
                weight_other[kind, z, y] = weight_ref[far, span].astype(jnp.bfloat16)


def attention_specs(normed, weights, cosine, column, row, first):
    columns, model = normed.shape
    pairs = HEADS // 2
    width = model // pairs

    def block(shape, index):
        return pl.BlockSpec(shape, lambda number, place: index(number + first))

    return [
        whole(normed.shape),
        block((model, width), lambda n: (0, n)),
        block((model, width), lambda n: (0, pairs + n)),
        block((model, width), lambda n: (0, 2 * pairs + n)),
        block((width, model), lambda n: (n, 3)),
        whole(cosine.shape),
        whole(cosine.shape),
        whole(column.shape),
        whole(row.shape),
    ]


def attention_forward(place, normed, weights, cosine, sine, column, row):
    columns, model = normed.shape
    rows = columns // PAIR
    pairs = HEADS // 2
    width = model // pairs
    across = lambda size: pl.BlockSpec((size, width), lambda number, place: (0, number))
    return pl.pallas_call(
        attention_forward_kernel,
        name="attention_forward",
        cost_estimate=busy(15),
        out_shape=[
            jax.ShapeDtypeStruct((rows, model), jnp.bfloat16),
            jax.ShapeDtypeStruct((columns, model), jnp.bfloat16),
            jax.ShapeDtypeStruct((columns, model), jnp.bfloat16),
            jax.ShapeDtypeStruct((rows, model), jnp.float32),
            jax.ShapeDtypeStruct((pairs, rows, width), jnp.float32),
            jax.ShapeDtypeStruct((rows, model), jnp.float32),
        ],
        grid_spec=pltpu.PrefetchScalarGridSpec(
            num_scalar_prefetch=1,
            grid=(pairs,),
            in_specs=attention_specs(normed, weights, cosine, column, row, 0),
            out_specs=[
                across(rows),
                across(columns),
                across(columns),
                across(rows),
                by_expert((1, rows, width)),
                whole((rows, model)),
            ],
            scratch_shapes=[pltpu.VMEM((rows, columns), jnp.float32)],
        ),
    )(place, normed, weights, weights, weights, weights, cosine, sine, column, row)


def attention_backward(
    place, normed, weights, cosine, sine, column, row, kept, grad, carried, first, count
):
    columns, model = normed.shape
    rows = columns // PAIR
    width = model // (HEADS // 2)
    depth = model // (RING * PAIR * PAIR)
    across = lambda size: pl.BlockSpec((size, width), lambda number, place: (0, number + first))
    return pl.pallas_call(
        attention_backward_kernel,
        name="attention_backward",
        cost_estimate=busy(14),
        out_shape=[
            jax.ShapeDtypeStruct((3, RING, PAIR, depth, width * count), jnp.bfloat16),
            jax.ShapeDtypeStruct((3, RING, PAIR, depth, width * count), jnp.bfloat16),
            jax.ShapeDtypeStruct((columns, model), jnp.float32),
        ],
        grid_spec=pltpu.PrefetchScalarGridSpec(
            num_scalar_prefetch=1,
            grid=(count,),
            in_specs=attention_specs(normed, weights, cosine, column, row, first)
            + [
                across(rows),
                across(columns),
                across(columns),
                across(rows),
                pl.BlockSpec((1, rows, width), lambda number, place: (number + first, 0, 0)),
                whole(grad.shape),
                whole(carried.shape),
            ],
            out_specs=[
                pl.BlockSpec((3, RING, PAIR, depth, width), lambda n, place: (0, 0, 0, 0, n)),
                pl.BlockSpec((3, RING, PAIR, depth, width), lambda n, place: (0, 0, 0, 0, n)),
                whole((columns, model)),
            ],
            scratch_shapes=[
                pltpu.VMEM((rows, columns), jnp.float32),
                pltpu.VMEM((model, 3 * width), jnp.float32),
            ],
        ),
    )(place, normed, weights, weights, weights, weights, cosine, sine, column, row, *kept, grad, carried)


def weight_pieces(gate_weight, up_weight, z_place):
    span = gate_weight.shape[2] // RING
    pieces = []
    for step in range(RING):
        start = lax.rem(z_place + step, RING) * span
        pieces.append(
            jnp.stack(
                [
                    lax.dynamic_slice_in_dim(gate_weight, start, span, 2),
                    lax.dynamic_slice_in_dim(up_weight, start, span, 2),
                ]
            )
        )
    return pieces


def place_columns(parts, z_place):
    columns = []
    for column in range(RING):
        choice = lax.rem(column - z_place + RING, RING)
        chosen = parts[0]
        for step in range(1, RING):
            chosen = jnp.where(choice == step, parts[step], chosen)
        columns.append(chosen)
    both = jnp.concatenate(columns, axis=-1).astype(jnp.float32)
    return both[0], both[1]


def body_split(
    tokens,
    segment_ids,
    routes,
    earlier_logits,
    out_cotangent,
    query_weight,
    key_weight,
    value_weight,
    output_weight,
    router_weight,
    const_vectors,
    attn_gain,
    moe_gain,
    gate_weight,
    up_weight,
    down_weight,
):
    _, pos_count, model_width = tokens.shape
    tokens, segment_row, routes = tokens[0], segment_ids[0], routes[0]
    earlier_logits, cotangent_low = earlier_logits[0], out_cotangent[0]
    x_place = lax.axis_index("expert")
    shard_place = lax.axis_index("shard")
    z_place = shard_place // (PAIR * PAIR)
    y_place = lax.rem(shard_place // PAIR, PAIR)
    core_place = lax.rem(shard_place, PAIR)
    order = jnp.arange(4, dtype=jnp.int32)
    place = jnp.where(
        order == 0,
        x_place,
        jnp.where(order == 1, z_place, jnp.where(order == 2, y_place, core_place)),
    ).astype(jnp.int32)
    choices = router_weight.shape[1]
    consts = const_vectors.shape[1]
    small_count = choices + consts + 2
    small = jnp.concatenate(
        [router_weight, const_vectors, attn_gain[:, None], moe_gain[:, None]], axis=1
    )
    small = jnp.pad(small, ((0, 0), (0, 128 - small_count)))
    packed = jnp.concatenate(
        [query_weight, key_weight, value_weight, output_weight, small], axis=1
    )
    routes_low = routes.astype(jnp.bfloat16)
    route_rows = [routes_low[:, 0], routes_low[:, 1]]
    zero_rows = [jnp.zeros_like(route_rows[0])] * 2
    cotangent_blocks, _ = gather_rows(
        jnp.concatenate([cotangent_low, meta_rows(zero_rows + route_rows, model_width)], axis=0)
    )
    gathered = lax.all_gather(packed, "shard", axis=0, tiled=True)
    other_tokens = across_x(tokens)
    frequency = jnp.exp(
        (jnp.arange(128, dtype=jnp.int32) % 32).astype(jnp.float32) * (-2.0 * math.log(10000.0) / 64)
    )
    angles = jnp.arange(PAIR * pos_count, dtype=jnp.float32)[:, None] * frequency[None, :]
    cosine = jnp.cos(angles)
    sine = jnp.sin(angles) * jnp.where(jnp.arange(128) % 64 < 32, -1.0, 1.0)
    segment_low = segment_row.astype(jnp.float32)[None, :]
    segment_column = segment_row.astype(jnp.float32)[:, None]
    cosine, sine, gathered, other_tokens, cotangent_blocks = together(
        cosine, sine, gathered, other_tokens, cotangent_blocks
    )
    pieces = weight_pieces(gate_weight, up_weight, z_place)
    down_other = across_y(down_weight)
    moved = [along_z(pieces[1], 1)]
    gathered, other_tokens, cotangent_blocks, pieces, down_other, moved = together(
        gathered, other_tokens, cotangent_blocks, pieces, down_other, moved
    )
    own_wide = gather_plane(pieces[0])
    downs = [down_weight, down_other, across_core(down_weight), across_core(down_other)]
    moved = moved + [along_z(pieces[step], step) for step in range(2, RING)]

    joint = 3 * model_width
    tail = gathered[:, joint + model_width :].astype(jnp.float32)
    router_low = gathered[:, joint + model_width : joint + model_width + choices]
    const_wide = tail[:, choices : choices + consts].T
    gain_attn = tail[:, choices + consts]
    gain_moe = tail[:, choices + consts + 1]

    first_tokens = jnp.where(x_place == 0, tokens, other_tokens)
    second_tokens = jnp.where(x_place == 0, other_tokens, tokens)
    all_wide = jnp.concatenate([first_tokens, second_tokens], axis=0).astype(jnp.float32)
    scaled_all, _ = rms_parts(all_wide)
    normed_all = (scaled_all * gain_attn).astype(jnp.bfloat16)
    tokens_wide = tokens.astype(jnp.float32)
    _, inverse_one = rms_parts(tokens_wide)
    query_rot, keys_all, values_all, mixed_heads, totals, projected = attention_forward(
        place, normed_all, gathered, cosine, sine, segment_column, segment_low
    )
    projected, moved = together(projected, moved)
    moved_wide = gather_plane(jnp.stack(moved))
    middle = tokens_wide + projected
    scaled_two, inverse_two = rms_parts(middle)
    normed_two = scaled_two * gain_moe
    normed_low = normed_two.astype(jnp.bfloat16)
    router_logits = dot_rows(normed_low, router_low) + earlier_logits
    choice_ids = jnp.arange(choices, dtype=jnp.int32)
    one_hot = (routes[..., None] == choice_ids).astype(jnp.float32)
    chosen = jnp.sum(one_hot * router_logits[:, None, :], axis=-1)
    gate_probs = jax.nn.softmax(chosen, axis=-1)
    probs_low = gate_probs.astype(jnp.bfloat16)
    payload = jnp.concatenate(
        [
            normed_low,
            meta_rows([probs_low[:, 0], probs_low[:, 1]] + route_rows, model_width),
        ],
        axis=0,
    )
    payload, cotangent_blocks = together(payload, cotangent_blocks)
    token_blocks, (pick, back_slots) = gather_rows(
        payload, tuple(pick_slots(place, cotangent_blocks))
    )
    back_hidden, wide_full, down_full = prepare_experts(
        place, back_slots, own_wide, moved_wide, downs
    )
    (token_slots, hidden, mixed), grad_parts, out_parts = run_experts(
        place, token_blocks, pick, wide_full, down_full, back_hidden
    )

    grad_total, (wide_grads, down_near, down_core), out_parts = reduce_rows(
        grad_parts, weight_grads(place, token_slots, back_slots, hidden, mixed), out_parts
    )
    wide_sum = scatter_plane(wide_grads)
    down_core = across_core(down_core)
    down_far = add_low(down_near[1], down_core[1])
    out_other = across_x(out_parts[7])

    cotangent = cotangent_low.astype(jnp.float32)
    copies = jnp.sum(one_hot[..., EXPERTS + 1] * gate_probs, axis=-1)[:, None]
    const_probs = jnp.sum(one_hot[..., EXPERTS + 2 :] * gate_probs[..., None], axis=1)
    copy_dot = jnp.sum(cotangent * normed_two, axis=-1)
    const_dot = jnp.stack(
        [jnp.sum(cotangent * const_wide[i], axis=-1) for i in range(consts)], axis=-1
    )
    grad_rows = grad_total[:pos_count]
    expert_dot = jnp.stack(
        [grad_total[pos_count, i * pos_count : (i + 1) * pos_count] for i in range(2)], axis=-1
    )
    grad_gates = (
        expert_dot
        + one_hot[..., EXPERTS + 1] * copy_dot[:, None]
        + jnp.sum(one_hot[..., EXPERTS + 2 :] * const_dot[:, None, :], axis=-1)
    )
    grad_chosen = gate_probs * (
        grad_gates - jnp.sum(gate_probs * grad_gates, axis=-1, keepdims=True)
    )
    prior_logits_gradient = jnp.sum(one_hot * grad_chosen[..., None], axis=1)
    prior_low = prior_logits_gradient.astype(jnp.bfloat16)
    grad_normed_two = (
        grad_rows
        + copies * cotangent
        + dot_wide(prior_low, router_low)
    )
    router_part = dot_tall(normed_low, prior_low)
    const_part = dot_tall(cotangent_low, const_probs.astype(jnp.bfloat16))
    moe_gain_part = jnp.sum(grad_normed_two * scaled_two, axis=0)
    grad_middle = cotangent + rms_back(grad_normed_two * gain_moe, middle, inverse_two)
    grad_projected = grad_middle.astype(jnp.bfloat16)
    small_early = jnp.concatenate(
        [router_part, const_part, jnp.zeros_like(moe_gain_part)[:, None], moe_gain_part[:, None]],
        axis=1,
    )
    small_early = jnp.pad(small_early, ((0, 0), (0, 128 - small_count)))
    output_part = dot_tall(mixed_heads.astype(jnp.bfloat16), grad_projected)
    output_mine, output_other = split_core(output_part.astype(jnp.bfloat16), core_place)
    grad_projected, out_other, output_mine, output_other, small_early = together(
        grad_projected, out_other, output_mine, output_other, small_early
    )
    kept = [query_rot, keys_all, values_all, mixed_heads, totals]
    shared_args = [place, normed_all, gathered, cosine, sine, segment_column, segment_low, kept]
    out_total = add_low(out_parts[3], out_other)
    out_passed, out_other = along_z(out_total, -1), across_x(out_parts[6])
    output_other = across_core(output_other)
    nothing = jnp.zeros(normed_all.shape, jnp.float32)
    grads_a = attention_backward(*shared_args, grad_projected, nothing, 0, 3)
    grad_projected, grads_a, out_passed, out_other, output_other, wide_sum, down_far = together(
        grad_projected, grads_a, out_passed, out_other, output_other, wide_sum, down_far
    )
    down_far = across_y(down_far)
    moved_first = along_z(wide_sum[1], -1)
    out_total = add_all(out_parts[2], out_passed, out_other).astype(jnp.bfloat16)
    output_sum = add_low(output_mine, output_other)
    out_passed, out_other = along_z(out_total, -1), across_x(out_parts[5])
    other_a = across_core(grads_a[1])
    grads_b = attention_backward(*shared_args, grad_projected, grads_a[2], 3, 3)
    grads_b, out_passed, out_other, other_a, wide_sum, down_far, moved_first = together(
        grads_b, out_passed, out_other, other_a, wide_sum, down_far, moved_first
    )
    moved_third = along_z(wide_sum[3], -3)
    out_total = add_all(out_parts[1], out_passed, out_other).astype(jnp.bfloat16)
    out_passed, out_other = along_z(out_total, -1), across_x(out_parts[4])
    moved_back = [wide_sum[0], moved_first, along_z(wide_sum[2], -2), moved_third]
    other_b = across_core(grads_b[1])
    sum_a = add_low(grads_a[0], other_a)
    grad_normed_all = grads_b[2]
    gain_lane = choices + consts
    chosen_lane = jnp.where(jnp.arange(128) == gain_lane, 1.0, 0.0).astype(jnp.bfloat16)
    gain_part = dot_tall(
        (grad_normed_all * scaled_all).astype(jnp.bfloat16),
        jnp.broadcast_to(chosen_lane, (grad_normed_all.shape[0], 128)),
    )
    first_grad = grad_normed_all[:pos_count]
    grad_normed_one = jnp.where(x_place == 0, first_grad, grad_normed_all[pos_count:])
    first_grad = first_grad.astype(jnp.bfloat16)
    small_part = (small_early + gain_part).astype(jnp.bfloat16)
    small_mine, small_other = split_core(small_part, core_place)
    small_sum = add_low(small_mine, across_core(small_other))
    sum_b = add_low(grads_b[0], other_b)
    packed_parts = [part[kind] for kind in range(3) for part in (sum_a, sum_b)]
    packed_parts = packed_parts + [output_sum, small_sum]

    def finish(late):
        moved_back = late[0]
        return (
            *place_columns(moved_back, z_place),
            add_all(down_near[0], down_core[0], down_far),
            add_all(out_parts[0], *late[1]),
        )

    packed_grad, shared, (gate_grad, up_grad, down_grad, out_total) = reduce_packed(
        packed_parts,
        z_place,
        y_place,
        first_grad,
        (moved_back, (out_passed, out_other)),
        finish,
    )
    const_rows = sum(const_probs[:, i : i + 1] * const_wide[i : i + 1] for i in range(consts))
    layer_out = (
        middle
        + out_total
        + copies * normed_two
        + const_rows
    )
    grad_normed_one = grad_normed_one + shared.astype(jnp.float32)
    tokens_grad = grad_middle + rms_back(grad_normed_one * gain_attn, tokens_wide, inverse_one)
    output_grad = packed_grad[:, joint : joint + model_width]
    small_grad = packed_grad[:, joint + model_width :]
    query_grad, key_grad, value_grad = (
        packed_grad[:, i * model_width : (i + 1) * model_width] for i in range(3)
    )
    return (
        layer_out.astype(jnp.bfloat16)[None],
        tokens_grad[None],
        prior_logits_gradient[None],
        query_grad,
        key_grad,
        value_grad,
        output_grad,
        small_grad[:, :choices],
        small_grad[:, choices : choices + consts],
        small_grad[:, choices + consts],
        small_grad[:, choices + consts + 1],
        gate_grad,
        up_grad,
        down_grad,
    )


def solution(mesh):
    in_specs = (
        P("shard", "expert", None),
        P("shard", None),
        P("shard", "expert", None),
        P("shard", "expert", None),
        P("shard", "expert", None),
        P("shard", None),
        P("shard", None),
        P("shard", None),
        P("shard", None),
        P("shard", None),
        P("shard", None),
        P("shard"),
        P("shard"),
        P("expert", "shard", None),
        P("expert", "shard", None),
        P("expert", "shard", None),
    )
    out_specs = (
        P("shard", "expert", None),
        P("shard", "expert", None),
        P("shard", "expert", None),
        P("shard", None),
        P("shard", None),
        P("shard", None),
        P("shard", None),
        P("shard", None),
        P("shard", None),
        P("shard"),
        P("shard"),
        P("expert", "shard", None),
        P("expert", "shard", None),
        P("expert", "shard", None),
    )
    divided = mesh.shape["expert"] == PAIR and mesh.shape["shard"] == RING * PAIR * PAIR
    chosen = body_split if divided else body
    return jax.shard_map(chosen, mesh=mesh, in_specs=in_specs, out_specs=out_specs, check_vma=False)
```
